32 devices in a mesh: dp: 4 (over y, x), mp: 8 (over z, core).
Axes of the slice: x: 2, y: 2, z: 4, core: 2. Of those that a mesh axis runs over, the one named last changes fastest.
Arguments:
- layer_in: bfloat16 [2048, 4, 2048], P('mp', 'dp'), may hold values from -18 to 18
- segment_ids: int32 [4, 2048], P('dp'), may hold values from 0 to 7, never falling along the last dimension, each value on 1 to 1024 neighbouring positions
- valid_counts: int32 [4], P('dp'), may hold values from 1024 to 2048
- norm_gain: float32 [2048], replicated, may hold values from 0.1 to 1.9
- norm_shift: float32 [2048], replicated, may hold values from -1.5 to 1.5
- w_qkv: bfloat16 [2048, 3, 2048], P(None, None, 'mp'), may hold values from -0.125 to 0.125
- b_qkv: bfloat16 [3, 2048], P(None, 'mp'), may hold values from -1.5 to 1.5
- w_out: bfloat16 [2048, 2048], P('mp'), may hold values from -0.5 to 0.5
- w_gate_up: bfloat16 [2048, 2, 5632], P(None, None, 'mp'), may hold values from -0.125 to 0.125
- w_down: bfloat16 [5632, 2048], P('mp'), may hold values from -0.078125 to 0.078125
- out_grad: bfloat16 [2048, 4, 2048], P('mp', 'dp'), may hold values from -6 to 6
Outputs:
- layer_out: bfloat16 [2048, 4, 2048], P('mp', 'dp')
- input_grad: float32 [2048, 4, 2048], P('mp', 'dp')
- grad_gain: float32 [2048], replicated
- grad_shift: float32 [2048], replicated
- grad_w_qkv: float32 [2048, 3, 2048], P(None, None, 'mp')
- grad_b_qkv: float32 [3, 2048], P(None, 'mp')
- grad_w_out: float32 [2048, 2048], P('mp')
- grad_w_gate_up: float32 [2048, 2, 5632], P(None, None, 'mp')
- grad_w_down: float32 [5632, 2048], P('mp')
- branch_rms: float32 [3], replicated
The draws below stay inside these ranges and needn't reach their ends.
Inputs may be any that keep to these rules, and one draw needn't show every extreme that they name: `segment_ids`: segment ids never fall along a row; each document has 1 to 1024 tokens.
All inputs are finite; a program needn't handle non-finite values.
Results may differ from the reference program's by a relative error of at most 0.014.
Values may be sent and summed in bfloat16 or wider, within the bound.
No kernel may reach another device: no remote copies, remote signals or barrier semaphores. Data moves between devices by JAX's collectives and lax.ppermute only.
A program may use at most 256 MiB of HBM per device.

```python
import math
from functools import partial
import jax
import jax.numpy as jnp
import numpy as np
from jax import lax

D = 2048
HEADS = 32
HEAD_DIM = 64
ROT = 16
FF = 5632
SEQ = 2048
DOCS = 8
BATCH = 4


def draw_layer_in(key, part):
    seq_idx = jnp.arange(SEQ, dtype=jnp.float32)[:, None, None]
    row_idx = jnp.arange(BATCH, dtype=jnp.float32)[None, :, None]
    rising = 1.0 + 2.0 * (row_idx * SEQ + seq_idx) / (BATCH * SEQ)
    return (jnp.clip(jax.random.normal(key, (SEQ, BATCH, D), jnp.float32), -6.0, 6.0) * rising).astype(jnp.bfloat16)


def set_ends(array, key, least, top_value):
    shape = array.shape
    place = [jax.random.randint(jax.random.fold_in(key, axis), (), 0, shape[axis]) for axis in range(len(shape))]
    array = array.at[tuple(place)].set(least)
    longest = shape.index(max(shape))
    place[longest] = (place[longest] + 1) % shape[longest]
    return array.at[tuple(place)].set(top_value)


def block_levels(own_key, shape, shards, low, high):
    level = 1.0
    for position, parts in shards:
        draws = jax.random.uniform(jax.random.fold_in(jax.random.fold_in(own_key, 6), position), (parts,), jnp.float32, low / len(shards), high / len(shards))
        level = level * jnp.repeat(jnp.exp(draws), shape[position] // parts).reshape((-1,) + (1,) * (len(shape) - 1 - position))
    return level


def length_profile(number_of, total, reach, skew):
    loads = [(1 << 20) // math.isqrt(grade ** skew) + 1 for grade in range(2, number_of + 1)]
    spare, counts = total - reach - (number_of - 1), [1] * (number_of - 1)
    while spare > 0:
        free = [i for i in range(number_of - 1) if counts[i] < reach]
        mass, left = sum([loads[i] for i in free]), spare
        for i in free:
            extra = min(reach - counts[i], max(1, left * loads[i] // mass), spare)
            counts[i] = counts[i] + extra
            spare = spare - extra
    return np.array([reach] + counts)


def uneven(own_key, amount, total, limit, skew):
    if amount == 2:
        one = jax.random.randint(own_key, (), max(1, total - limit), min(limit, total - 1) + 1)
        return jnp.stack([one, total - one])
    tallies = jnp.asarray(length_profile(amount, total, limit, skew), jnp.int32)
    twos = (amount - 1) // 2
    donor, taker = tallies[1:1 + 2 * twos:2], tallies[2:2 + 2 * twos:2]
    room = jnp.minimum(donor - 1, limit - taker)
    moved = jax.random.randint(jax.random.fold_in(own_key, 1), (twos,), 0, 1 << 20) % (room + 1)
    tallies = tallies.at[1:1 + 2 * twos:2].set(donor - moved).at[2:2 + 2 * twos:2].set(taker + moved)
    return tallies[jax.random.permutation(jax.random.fold_in(own_key, 2), amount)]


def gaussian(key, dims, spread, reach, cuts=(), held_as=jnp.bfloat16):
    level = block_levels(key, dims, cuts, -0.22, 0.18) if cuts else 1.0
    entries = jax.random.normal(key, dims, jnp.float32) * spread * level
    return jnp.minimum(jnp.maximum(entries, -reach), reach).astype(held_as)


def setup_inputs(seed: int = 0) -> dict:
    key_list = jax.random.split(jax.random.key(seed), 12)
    return {
        "layer_in": draw_layer_in(jax.random.fold_in(key_list[11], 71), 0),
        "segment_ids": jax.vmap(lambda own: jnp.searchsorted(jnp.cumsum(uneven(own, DOCS, SEQ, SEQ // 2, 1)), jnp.arange(SEQ), side="right"))(jax.random.split(key_list[1], BATCH)).reshape((BATCH, SEQ)).astype(jnp.int32),
        "valid_counts": set_ends(jax.random.randint(key_list[2], (BATCH,), SEQ // 2, SEQ + 1), jax.random.fold_in(key_list[2], 1), SEQ // 2, SEQ).astype(jnp.int32),
        "norm_gain": jnp.clip(1.0 + 0.18 * jax.random.normal(key_list[3], (D,), jnp.float32), 0.1, 1.9),
        "norm_shift": gaussian(key_list[4], (D,), 0.3, 1.5, (), jnp.float32),
        "w_qkv": gaussian(key_list[5], (D, 3, D), D ** -0.5, 0.125, ((2, 8),)),
        "b_qkv": gaussian(key_list[6], (3, D), 0.3, 1.5, ((1, 8),)),
        "w_out": gaussian(key_list[7], (D, D), (D // 16) ** -0.5, 0.5, ((0, 8),)),
        "w_gate_up": gaussian(key_list[8], (D, 2, FF), D ** -0.5, 0.125, ((2, 8),)),
        "w_down": gaussian(key_list[9], (FF, D), FF ** -0.5, 0.078125, ((0, 8),)),
        "out_grad": gaussian(key_list[10], (SEQ, BATCH, D), 1.0, 6.0, ((0, 8), (1, 4))),
    }


@jax.custom_vjp
def low(v):
    return lax.optimization_barrier(v.astype(jnp.bfloat16)).astype(jnp.float32)

@jax.custom_vjp
def low_back(v):
    return v

def low_keep(v):
    return (low(v), None)

def low_pass(kept, grad):
    return (grad,)

def back_keep(v):
    return (v, None)

def back_low(kept, grad):
    return (low(grad),)
low.defvjp(low_keep, low_pass)
low_back.defvjp(back_keep, back_low)
EPSILON = 1e-05
HIGHEST_PREC = lax.Precision.HIGHEST

def positions_of(segment_ids):
    length = segment_ids.shape[1]
    steps_all = jnp.arange(length, dtype=jnp.int32)[None, :]
    change = jnp.concatenate([jnp.ones_like(segment_ids[:, :1]), (segment_ids[:, 1:] != segment_ids[:, :-1]).astype(jnp.int32)], axis=1)
    starts = lax.cummax(jnp.where(change > 0, steps_all, jnp.zeros_like(change)), axis=1)
    return steps_all - starts

def rotary_tables(positions):
    half_rot = ROT // 2
    frequency = 10000.0 ** (-(jnp.arange(half_rot, dtype=jnp.float32) * 2.0) / ROT)
    angles = positions.astype(jnp.float32)[..., None] * frequency
    return (jnp.cos(angles), jnp.sin(angles))

def rotate(values, cosine, sine_table):
    half_rot = ROT // 2
    first = values[..., :half_rot]
    second = values[..., half_rot:ROT]
    return jnp.concatenate([first * cosine - second * sine_table, second * cosine + first * sine_table, values[..., ROT:]], axis=-1)

def attention(queries, keys_all, values_all, seg_row):
    q_heads = jnp.transpose(queries, (1, 0, 2))
    k_heads = jnp.transpose(keys_all, (1, 0, 2))
    v_heads = jnp.transpose(values_all, (1, 0, 2))
    block_len = min(512, SEQ)
    block_count = SEQ // block_len
    key_pos = jnp.arange(SEQ, dtype=jnp.int32)

    def one_block(block_id):
        offset = (block_id * block_len).astype(jnp.int32)
        q_part = lax.dynamic_slice_in_dim(q_heads, offset, block_len, 1)
        scores = low_back(jnp.einsum('hqd,hkd->hqk', q_part, k_heads, precision=HIGHEST_PREC) * HEAD_DIM ** (-0.5))
        q_seg = lax.dynamic_slice_in_dim(seg_row, offset, block_len, 0)
        q_pos = offset + jnp.arange(block_len, dtype=jnp.int32)
        allowed = (key_pos[None, :] <= q_pos[:, None]) & (q_seg[:, None] == seg_row[None, :])
        scores = jnp.where(allowed[None], scores, -1e+30)
        weights = low(jax.nn.softmax(scores, axis=-1))
        return jnp.einsum('hqk,hkd->hqd', weights, v_heads, precision=HIGHEST_PREC)
    blocks = lax.map(jax.checkpoint(one_block), jnp.arange(block_count, dtype=jnp.int32))
    return jnp.transpose(blocks, (0, 2, 1, 3)).reshape(SEQ, HEADS * HEAD_DIM)

def layer_row(params, inputs):
    gain, norm_shift, w_qkv, b_qkv, w_out, w_gate_up, w_down = params
    x_row, cosine, sine_table, seg_row, valid_row = inputs
    centered = x_row - lax.optimization_barrier(jnp.mean(x_row, -1, keepdims=True))
    variance = lax.optimization_barrier(jnp.mean(centered * centered, -1, keepdims=True))
    normalized = centered * lax.rsqrt(variance + EPSILON)
    normed = low(normalized * gain + norm_shift)
    projected = low_back(jnp.dot(normed, w_qkv.reshape(D, 3 * D), precision=HIGHEST_PREC) + b_qkv.reshape(3 * D))
    projected = projected.reshape(SEQ, 3, HEADS, HEAD_DIM)
    cos_row = cosine[:, None, :]
    sin_row = sine_table[:, None, :]
    queries = low_back(low(rotate(projected[:, 0], cos_row, sin_row)))
    keys_all = low_back(low(rotate(projected[:, 1], cos_row, sin_row)))
    values_all = low_back(low(projected[:, 2]))
    attended = low_back(low(attention(queries, keys_all, values_all, seg_row)))
    attn_part = jnp.dot(attended, w_out, precision=HIGHEST_PREC)
    gate_up = low_back(jnp.dot(normed, w_gate_up.reshape(D, 2 * FF), precision=HIGHEST_PREC))
    hidden = low_back(low(jax.nn.silu(gate_up[:, :FF]) * gate_up[:, FF:]))
    mlp_part = jnp.dot(hidden, w_down, precision=HIGHEST_PREC)
    output = x_row + attn_part + mlp_part
    statistics = jnp.stack([jnp.sum(valid_row * lax.optimization_barrier(jnp.sum(attn_part * attn_part, -1))), jnp.sum(valid_row * lax.optimization_barrier(jnp.sum(mlp_part * mlp_part, -1)))])
    return (output, statistics)

def reference(layer_in, segment_ids, valid_counts, norm_gain, norm_shift, w_qkv, b_qkv, w_out, w_gate_up, w_down, out_grad):
    rows_x = jnp.transpose(layer_in.astype(jnp.float32), (1, 0, 2))
    rows_grad = jnp.transpose(out_grad.astype(jnp.float32), (1, 0, 2))
    positions = positions_of(segment_ids)
    cosine, sine_table = rotary_tables(positions)
    valid = (jnp.arange(SEQ, dtype=jnp.int32)[None, :] < valid_counts[:, None]).astype(jnp.float32)
    params = (norm_gain.astype(jnp.float32), norm_shift.astype(jnp.float32), w_qkv.astype(jnp.float32), b_qkv.astype(jnp.float32), w_out.astype(jnp.float32), w_gate_up.astype(jnp.float32), w_down.astype(jnp.float32))
    checkpointed = jax.checkpoint(layer_row)

    def forward(weights, inputs_x):
        return lax.map(partial(checkpointed, weights), (inputs_x, cosine, sine_table, segment_ids, valid))
    (outputs, statistics), pullback = jax.vjp(forward, params, rows_x)
    cotangent = rows_grad * valid[:, :, None]
    grad_params, grad_x = pullback((cotangent, jnp.zeros_like(statistics)))
    squares_x = jnp.sum(valid * lax.optimization_barrier(jnp.sum(rows_x * rows_x, -1)))
    count_valid = jnp.sum(valid)
    totals = jnp.stack([squares_x, jnp.sum(statistics[:, 0]), jnp.sum(statistics[:, 1])])
    branch_rms = jnp.sqrt(totals / (count_valid * D))
    layer_out = jnp.transpose(outputs, (1, 0, 2)).astype(jnp.bfloat16)
    input_grad = jnp.transpose(grad_x, (1, 0, 2))
    return (layer_out, input_grad, grad_params[0], grad_params[1], grad_params[2], grad_params[3], grad_params[4], grad_params[5], grad_params[6], branch_rms)
```

```python
import functools

import jax
import jax.numpy as jnp
from jax import lax
from jax.experimental import pallas as pl
from jax.experimental.pallas import tpu as pltpu
from jax.sharding import PartitionSpec as P

HEAD_DIM = 64
ROT = 16
EPSILON = 1e-05
BQ = 128
BK = 256
NEG = -1e30
F32 = jnp.float32
BF16 = jnp.bfloat16


def starts_of(segment_ids):
    length = segment_ids.shape[1]
    steps_all = jnp.arange(length, dtype=jnp.int32)[None, :]
    change = jnp.concatenate(
        [
            jnp.ones_like(segment_ids[:, :1]),
            (segment_ids[:, 1:] != segment_ids[:, :-1]).astype(jnp.int32),
        ],
        axis=1,
    )
    return lax.cummax(jnp.where(change > 0, steps_all, jnp.zeros_like(change)), axis=1)


def rotary_lanes(positions):
    half_rot = ROT // 2
    lane = jnp.arange(2 * HEAD_DIM, dtype=jnp.int32) % HEAD_DIM
    power = (lane % half_rot).astype(F32)
    frequency = jnp.where(lane < ROT, 10000.0 ** (-(power * 2.0) / ROT), 0.0)
    angles = positions.astype(F32)[:, None] * frequency
    sine = jnp.sin(angles)
    low = jnp.where(lane < half_rot, -sine, 0.0)
    high = jnp.where((lane >= half_rot) & (lane < ROT), sine, 0.0)
    return jnp.cos(angles), low, high


def lane_tile(table, columns):
    return jnp.concatenate([table] * (columns // table.shape[1]), axis=1)


def turn(values, cosine, low, high):
    columns = values.shape[1]
    half_rot = ROT // 2
    return (
        values * lane_tile(cosine, columns)
        + pltpu.roll(values, columns - half_rot, 1) * lane_tile(low, columns)
        + pltpu.roll(values, half_rot, 1) * lane_tile(high, columns)
    )


def project_kernel(x_ref, w_ref, b_ref, cos_ref, low_ref, high_ref, q_ref, k_ref, v_ref):
    columns = q_ref.shape[1]
    flat = jnp.dot(x_ref[...], w_ref[...], preferred_element_type=F32) + b_ref[...]
    tables = (cos_ref[...], low_ref[...], high_ref[...])
    queries = turn(flat[:, :columns], *tables).astype(BF16)
    q_ref[...] = (queries.astype(F32) * HEAD_DIM**-0.5).astype(BF16)
    k_ref[...] = turn(flat[:, columns : 2 * columns], *tables).astype(BF16)
    v_ref[...] = flat[:, 2 * columns :].astype(BF16)


def project(gathered, w_flat, bias, tables):
    length, width = gathered.shape
    columns = w_flat.shape[1] // 3
    rows = min(512, length)
    table_spec = pl.BlockSpec((rows, tables[0].shape[1]), lambda i: (i, 0))
    out_spec = pl.BlockSpec((rows, columns), lambda i: (i, 0))
    return pl.pallas_call(
        project_kernel,
        grid=(length // rows,),
        in_specs=[
            pl.BlockSpec((rows, width), lambda i: (i, 0)),
            pl.BlockSpec((width, 3 * columns), lambda i: (0, 0)),
            pl.BlockSpec((1, 3 * columns), lambda i: (0, 0)),
            table_spec,
            table_spec,
            table_spec,
        ],
        out_specs=[out_spec] * 3,
        out_shape=[jax.ShapeDtypeStruct((length, columns), BF16)] * 3,
        cost_estimate=pl.CostEstimate(
            flops=6 * length * width * columns,
            bytes_accessed=2 * (length * width + 3 * width * columns + 3 * length * columns),
            transcendentals=0,
        ),
        name="project",
    )(gathered, w_flat, bias, *tables)


def stack_heads(block):
    columns = block.shape[1]
    head_of = lax.broadcasted_iota(jnp.int32, block.shape, 1) // HEAD_DIM
    return jnp.concatenate(
        [
            jnp.where(head_of == head, block, jnp.zeros_like(block))
            for head in range(columns // HEAD_DIM)
        ],
        axis=0,
    )


def unstack_heads(stacked, block):
    heads = stacked.shape[1] // block
    return jnp.concatenate(
        [
            stacked[head * HEAD_DIM : (head + 1) * HEAD_DIM, head * block : (head + 1) * block]
            for head in range(heads)
        ],
        axis=0,
    ).T


def score_block(key_block, stacked_queries, key_at, start_row, query_row):
    scores = lax.dot_general(
        key_block, stacked_queries, (((1,), (1,)), ((), ())), preferred_element_type=F32
    )
    key_pos = key_at + lax.broadcasted_iota(jnp.int32, scores.shape, 0)
    allowed = (key_pos >= start_row) & (key_pos <= query_row)
    return scores, allowed


def query_rows(start_ref, block, heads):
    start_row = jnp.concatenate([start_ref[0]] * heads, axis=1)
    query_row = pl.program_id(0) * block + lax.broadcasted_iota(jnp.int32, (1, block), 1)
    return start_row, jnp.concatenate([query_row] * heads, axis=1)


def attend_kernel(first_ref, q_ref, k_ref, v_ref, start_ref, o_ref, lse_ref, acc_ref):
    block, columns = q_ref.shape
    heads = columns // HEAD_DIM
    index = pl.program_id(0)
    stacked = stack_heads(q_ref[...])
    start_row, query_row = query_rows(start_ref, block, heads)
    acc_ref[...] = jnp.zeros_like(acc_ref)

    def body(step, carry):
        highest, total = carry
        at = pl.multiple_of(step * BK, BK)
        scores, allowed = score_block(
            k_ref[pl.ds(at, BK), :], stacked, at, start_row, query_row
        )
        scores = jnp.where(allowed, scores, NEG)
        newest = jnp.maximum(highest, jnp.max(scores, axis=0, keepdims=True))
        weights = jnp.exp(scores - newest)
        scale = jnp.exp(highest - newest)
        total = total * scale + jnp.sum(weights, axis=0, keepdims=True)
        acc_ref[...] = acc_ref[...] * scale + lax.dot_general(
            v_ref[pl.ds(at, BK), :],
            weights.astype(BF16),
            (((0,), (0,)), ((), ())),
            preferred_element_type=F32,
        )
        return newest, total

    highest, total = lax.fori_loop(
        first_ref[index],
        (index * block + block - 1) // BK + 1,
        body,
        (jnp.full((1, heads * block), NEG, F32), jnp.zeros((1, heads * block), F32)),
    )
    o_ref[...] = unstack_heads(acc_ref[...] / total, block).astype(BF16)
    lse_ref[0] = highest + jnp.log(total)


def attend(first, queries, key_rows, value_rows, start_blocks):
    length, columns = queries.shape
    blocks = length // BQ
    heads = columns // HEAD_DIM
    row_spec = pl.BlockSpec((BQ, columns), lambda i, f: (i, 0))
    whole = pl.BlockSpec((length, columns), lambda i, f: (0, 0))
    return pl.pallas_call(
        attend_kernel,
        grid_spec=pltpu.PrefetchScalarGridSpec(
            num_scalar_prefetch=1,
            grid=(blocks,),
            in_specs=[
                row_spec,
                whole,
                whole,
                pl.BlockSpec((1, 1, BQ), lambda i, f: (i, 0, 0)),
            ],
            out_specs=[
                row_spec,
                pl.BlockSpec((1, 1, heads * BQ), lambda i, f: (i, 0, 0)),
            ],
            scratch_shapes=[pltpu.VMEM((columns, heads * BQ), F32)],
        ),
        out_shape=[
            jax.ShapeDtypeStruct((length, columns), BF16),
            jax.ShapeDtypeStruct((blocks, 1, heads * BQ), F32),
        ],
        cost_estimate=pl.CostEstimate(
            flops=4 * length * 1024 * columns * heads,
            bytes_accessed=8 * length * columns,
            transcendentals=length * 1024 * heads,
        ),
        name="attend",
    )(first, queries, key_rows, value_rows, start_blocks)


def attend_back_kernel(
    first_ref,
    q_ref,
    k_ref,
    v_ref,
    do_ref,
    o_ref,
    lse_ref,
    start_ref,
    cos_ref,
    low_ref,
    high_ref,
    grad_ref,
    key_acc,
    value_acc,
    query_acc,
):
    block, columns = q_ref.shape
    heads = columns // HEAD_DIM
    length = k_ref.shape[0]
    index = pl.program_id(0)

    @pl.when(index == 0)
    def _():
        key_acc[...] = jnp.zeros_like(key_acc)
        value_acc[...] = jnp.zeros_like(value_acc)

    stacked = stack_heads(q_ref[...])
    stacked_do = stack_heads(do_ref[...])
    start_row, query_row = query_rows(start_ref, block, heads)
    lse_row = lse_ref[0]
    products = do_ref[...].astype(F32) * o_ref[...].astype(F32)
    head_rows = lax.broadcasted_iota(jnp.int32, (8, columns), 0)
    head_lanes = lax.broadcasted_iota(jnp.int32, (8, columns), 1) // HEAD_DIM
    picked = lax.dot_general(
        (head_rows == head_lanes).astype(F32),
        products,
        (((1,), (1,)), ((), ())),
        precision=lax.Precision.HIGHEST,
        preferred_element_type=F32,
    )
    inner_row = jnp.concatenate([picked[head : head + 1, :] for head in range(heads)], axis=1)
    query_acc[...] = jnp.zeros_like(query_acc)

    def body(step, carry):
        at = pl.multiple_of(step * BK, BK)
        key_block = k_ref[pl.ds(at, BK), :]
        scores, allowed = score_block(key_block, stacked, at, start_row, query_row)
        weights = jnp.where(allowed, jnp.exp(scores - lse_row), 0.0)
        grad_weights = lax.dot_general(
            v_ref[pl.ds(at, BK), :],
            stacked_do,
            (((1,), (1,)), ((), ())),
            preferred_element_type=F32,
        )
        grad_scores = (weights * (grad_weights - inner_row)).astype(BF16)
        value_acc[pl.ds(at, BK), :] += jnp.dot(
            weights.astype(BF16), stacked_do, preferred_element_type=F32
        )
        key_acc[pl.ds(at, BK), :] += jnp.dot(grad_scores, stacked, preferred_element_type=F32)
        query_acc[...] += lax.dot_general(
            key_block, grad_scores, (((0,), (0,)), ((), ())), preferred_element_type=F32
        )
        return carry

    lax.fori_loop(first_ref[index], (index * block + block - 1) // BK + 1, body, 0)

    def turn_back(grads, at, rows):
        kept = grads.astype(BF16).astype(F32)
        return turn(
            kept,
            cos_ref[pl.ds(at, rows), :],
            -low_ref[pl.ds(at, rows), :],
            -high_ref[pl.ds(at, rows), :],
        ).astype(BF16)

    at_query = pl.multiple_of(index * block, block)
    grad_ref[pl.ds(at_query, block), :columns] = turn_back(
        unstack_heads(query_acc[...], block) * HEAD_DIM**-0.5, at_query, block
    )

    @pl.when(index == pl.num_programs(0) - 1)
    def _():
        def finish(step, carry):
            at = pl.multiple_of(step * BK, BK)
            grad_ref[pl.ds(at, BK), columns : 2 * columns] = turn_back(
                key_acc[pl.ds(at, BK), :], at, BK
            )
            grad_ref[pl.ds(at, BK), 2 * columns :] = value_acc[pl.ds(at, BK), :].astype(BF16)
            return carry

        lax.fori_loop(0, length // BK, finish, 0)


def attend_back(first, queries, key_rows, value_rows, grad_att, attended, lse, start_blocks, tables):
    length, columns = queries.shape
    blocks = length // BQ
    heads = columns // HEAD_DIM
    row_spec = pl.BlockSpec((BQ, columns), lambda i, f: (i, 0))
    whole = pl.BlockSpec((length, columns), lambda i, f: (0, 0))
    table_spec = pl.BlockSpec(tables[0].shape, lambda i, f: (0, 0))
    return pl.pallas_call(
        attend_back_kernel,
        grid_spec=pltpu.PrefetchScalarGridSpec(
            num_scalar_prefetch=1,
            grid=(blocks,),
            in_specs=[
                row_spec,
                whole,
                whole,
                row_spec,
                row_spec,
                pl.BlockSpec((1, 1, heads * BQ), lambda i, f: (i, 0, 0)),
                pl.BlockSpec((1, 1, BQ), lambda i, f: (i, 0, 0)),
                table_spec,
                table_spec,
                table_spec,
            ],
            out_specs=pl.BlockSpec((length, 3 * columns), lambda i, f: (0, 0)),
            scratch_shapes=[
                pltpu.VMEM((length, columns), F32),
                pltpu.VMEM((length, columns), F32),
                pltpu.VMEM((columns, heads * BQ), F32),
            ],
        ),
        out_shape=jax.ShapeDtypeStruct((length, 3 * columns), BF16),
        cost_estimate=pl.CostEstimate(
            flops=10 * length * 1024 * columns * heads,
            bytes_accessed=16 * length * columns,
            transcendentals=length * 1024 * heads,
        ),
        name="attend_back",
    )(first, queries, key_rows, value_rows, grad_att, attended, lse, start_blocks, *tables)


def bits_of(name):
    size = lax.axis_size(name)
    count = size.bit_length() - 1
    return count if size == 1 << count else None


def swap(values, name, bit):
    size = lax.axis_size(name)
    return lax.ppermute(values, name, [(i, i ^ (1 << bit)) for i in range(size)])


def sum_over_dp(grad, axis):
    count = bits_of("dp")
    if not count or grad.shape[axis] % (2 << count):
        return lax.psum(grad, "dp").astype(F32)
    mine = lax.axis_index("dp")
    done = []
    for color, half in enumerate(jnp.split(grad, 2, axis=axis)):
        order = list(range(count))
        if color:
            order.reverse()
        for bit in order:
            size = half.shape[axis] // 2
            side = (mine >> bit) & 1
            keep = lax.dynamic_slice_in_dim(half, side * size, size, axis)
            send = lax.dynamic_slice_in_dim(half, (1 - side) * size, size, axis)
            got = swap(send, "dp", bit)
            half = (keep.astype(F32) + got.astype(F32)).astype(BF16)
        for bit in reversed(order):
            side = (mine >> bit) & 1
            got = swap(half, "dp", bit)
            half = jnp.where(
                side == 0,
                jnp.concatenate([half, got], axis=axis),
                jnp.concatenate([got, half], axis=axis),
            )
        done.append(half)
    return jnp.concatenate(done, axis=axis).astype(F32)


def sum_small(values, name):
    count = bits_of(name)
    if count is None:
        return lax.psum(values, name)
    for bit in range(count):
        values = values + swap(values, name, bit)
    return values


def local(
    layer_in,
    segment_ids,
    valid_counts,
    norm_gain,
    norm_shift,
    w_qkv,
    b_qkv,
    w_out,
    w_gate_up,
    w_down,
    out_grad,
):
    local_len, row_count, model_width = layer_in.shape
    seq_len = local_len * lax.axis_size("mp")
    col_qkv = w_qkv.shape[2]
    ff_local = w_gate_up.shape[2]
    position_here = lax.axis_index("mp") * local_len + jnp.arange(local_len, dtype=jnp.int32)
    valid_here = (position_here[:, None] < valid_counts[None, :]).astype(F32)

    residual = layer_in.astype(F32)
    centered = residual - jnp.mean(residual, -1, keepdims=True)
    inv_std = lax.rsqrt(jnp.mean(centered * centered, -1, keepdims=True) + EPSILON)
    normalized = centered * inv_std
    normed = (normalized * norm_gain + norm_shift).astype(BF16)
    cot_here = jnp.where(valid_here[:, :, None] > 0, out_grad, jnp.zeros_like(out_grad))

    gathered = lax.all_gather(normed, "mp", axis=0, tiled=True)
    cot_here, gathered_first = lax.optimization_barrier((cot_here, normed))
    cotangent = lax.all_gather(cot_here, "mp", axis=0, tiled=True)

    qkv_flat = w_qkv.reshape(model_width, 3 * col_qkv)
    gate_flat = w_gate_up.reshape(model_width, 2 * ff_local)
    starts = starts_of(segment_ids)
    positions = jnp.arange(seq_len, dtype=jnp.int32)[None, :] - starts
    bias = b_qkv.reshape(1, 3 * col_qkv).astype(F32)

    def each_row(row):
        tables = rotary_lanes(positions[row])
        start_blocks = starts[row].reshape(seq_len // BQ, 1, BQ)
        first = start_blocks[:, 0, 0] // BK
        return tables, start_blocks, first

    attended_rows = []
    kept = []
    for row in range(row_count):
        tables, start_blocks, first = each_row(row)
        queries, key_rows, value_rows = project(gathered[:, row], qkv_flat, bias, tables)
        attended, lse = attend(first, queries, key_rows, value_rows, start_blocks)
        attended_rows.append(attended)
        kept.append((first, queries, key_rows, value_rows, attended, lse, start_blocks, tables))
    attended = jnp.stack(attended_rows, axis=1)

    gate_up = jnp.dot(gathered, gate_flat, preferred_element_type=F32)
    gate_half = gate_up[..., :ff_local]
    up_half = gate_up[..., ff_local:]
    sigmoid_gate = jax.nn.sigmoid(gate_half)
    hidden = (gate_half * sigmoid_gate * up_half).astype(BF16)

    def scattered(partial):
        return lax.psum_scatter(
            partial.astype(BF16), "mp", scatter_dimension=0, tiled=True
        )

    mlp_sum = scattered(jnp.dot(hidden, w_down, preferred_element_type=F32))
    attn_sum = scattered(jnp.dot(attended, w_out, preferred_element_type=F32))
    mlp_sum, attn_sum = lax.optimization_barrier((mlp_sum, attn_sum))
    mlp_part = mlp_sum.astype(F32)
    attn_part = attn_sum.astype(F32)
    layer_out = (residual + attn_part + mlp_part).astype(BF16)
    statistics = jnp.stack(
        [
            jnp.sum(valid_here * jnp.sum(residual * residual, -1)),
            jnp.sum(valid_here * jnp.sum(attn_part * attn_part, -1)),
            jnp.sum(valid_here * jnp.sum(mlp_part * mlp_part, -1)),
            jnp.sum(valid_here),
        ]
    )

    def token_sum(spec, left, right):
        return jnp.einsum(spec, left, right, preferred_element_type=F32).astype(BF16)

    grad_hid = jnp.einsum(
        "srd,fd->srf", cotangent, w_down, preferred_element_type=F32
    ).astype(BF16).astype(F32)
    grad_w_down = sum_over_dp(token_sum("srf,srd->fd", hidden, cotangent), 1)
    grad_gate = grad_hid * up_half * sigmoid_gate * (1.0 + gate_half * (1.0 - sigmoid_gate))
    grad_up = grad_hid * gate_half * sigmoid_gate
    grad_gate_up = jnp.concatenate([grad_gate, grad_up], axis=-1).astype(BF16)
    grad_w_gate_up = sum_over_dp(token_sum("srd,srf->df", gathered, grad_gate_up), 0)

    grad_att = jnp.einsum(
        "srd,nd->srn", cotangent, w_out, preferred_element_type=F32
    ).astype(BF16)
    grad_w_out = sum_over_dp(token_sum("srn,srd->nd", attended, cotangent), 1)
    grad_proj = jnp.stack(
        [
            attend_back(first, q, k, v, grad_att[:, row], att, lse, start_blocks, tables)
            for row, (first, q, k, v, att, lse, start_blocks, tables) in enumerate(kept)
        ],
        axis=1,
    )
    grad_w_qkv = sum_over_dp(token_sum("srd,srn->dn", gathered, grad_proj), 0)
    grad_normed = scattered(
        jnp.einsum("srn,dn->srd", grad_proj, qkv_flat, preferred_element_type=F32)
        + jnp.einsum("srf,df->srd", grad_gate_up, gate_flat, preferred_element_type=F32)
    ).astype(F32)

    small = jnp.concatenate(
        [
            jnp.sum(grad_normed * normalized, axis=(0, 1)),
            jnp.sum(grad_normed, axis=(0, 1)),
            statistics,
            jnp.zeros((124,), F32),
        ]
    )
    small = sum_small(sum_small(small.reshape(-1, 128), "mp"), "dp").reshape(-1)
    grad_gain = small[:model_width]
    grad_shift = small[model_width : 2 * model_width]
    totals = small[2 * model_width : 2 * model_width + 4]
    branch_rms = jnp.sqrt(totals[:3] / (totals[3] * model_width))
    grad_scaled = grad_normed * norm_gain
    input_grad = inv_std * (
        grad_scaled
        - jnp.mean(grad_scaled, -1, keepdims=True)
        - normalized * jnp.mean(grad_scaled * normalized, -1, keepdims=True)
    )
    input_grad = input_grad + cot_here.astype(F32)
    grad_b_qkv = jnp.sum(grad_proj, axis=(0, 1), dtype=F32)
    grad_b_qkv = sum_small(grad_b_qkv.reshape(-1, 128), "dp").reshape(3, col_qkv)
    return (
        layer_out,
        input_grad,
        grad_gain,
        grad_shift,
        grad_w_qkv.reshape(model_width, 3, col_qkv),
        grad_b_qkv,
        grad_w_out,
        grad_w_gate_up.reshape(model_width, 2, ff_local),
        grad_w_down,
        branch_rms,
    )


def solution(mesh):
    placed = (
        P("mp", "dp", None),
        P("dp", None),
        P("dp"),
        P(),
        P(),
        P(None, None, "mp"),
        P(None, "mp"),
        P("mp", None),
        P(None, None, "mp"),
        P("mp", None),
        P("mp", "dp", None),
    )
    return jax.shard_map(
        local,
        mesh=mesh,
        in_specs=placed,
        out_specs=(
            P("mp", "dp", None),
            P("mp", "dp", None),
            P(),
            P(),
            P(None, None, "mp"),
            P(None, "mp"),
            P("mp", None),
            P(None, None, "mp"),
            P("mp", None),
            P(),
        ),
        check_vma=False,
    )
```

```python
import functools

import jax
import jax.numpy as jnp
from jax import lax
from jax.experimental import pallas as pl
from jax.experimental.pallas import tpu as pltpu
from jax.sharding import PartitionSpec as P

HEAD_DIM = 64
ROT = 16
EPSILON = 1e-05
BQ = 128
BK = 256
NEG = -1e30
F32 = jnp.float32
BF16 = jnp.bfloat16


def starts_of(segment_ids):
    length = segment_ids.shape[1]
    steps_all = jnp.arange(length, dtype=jnp.int32)[None, :]
    change = jnp.concatenate(
        [
            jnp.ones_like(segment_ids[:, :1]),
            (segment_ids[:, 1:] != segment_ids[:, :-1]).astype(jnp.int32),
        ],
        axis=1,
    )
    return lax.cummax(jnp.where(change > 0, steps_all, jnp.zeros_like(change)), axis=1)


def rotary_lanes(positions):
    half_rot = ROT // 2
    lane = jnp.arange(2 * HEAD_DIM, dtype=jnp.int32) % HEAD_DIM
    power = (lane % half_rot).astype(F32)
    frequency = jnp.where(lane < ROT, 10000.0 ** (-(power * 2.0) / ROT), 0.0)
    angles = positions.astype(F32)[:, None] * frequency
    sine = jnp.sin(angles)
    low = jnp.where(lane < half_rot, -sine, 0.0)
    high = jnp.where((lane >= half_rot) & (lane < ROT), sine, 0.0)
    return jnp.cos(angles), low, high


def lane_tile(table, columns):
    return jnp.concatenate([table] * (columns // table.shape[1]), axis=1)


def turn(values, cosine, low, high):
    columns = values.shape[1]
    half_rot = ROT // 2
    return (
        values * lane_tile(cosine, columns)
        + pltpu.roll(values, columns - half_rot, 1) * lane_tile(low, columns)
        + pltpu.roll(values, half_rot, 1) * lane_tile(high, columns)
    )


def project_kernel(x_ref, w_ref, b_ref, cos_ref, low_ref, high_ref, q_ref, k_ref, v_ref):
    tables = (cos_ref[...], low_ref[...], high_ref[...])

    def part(number):
        flat = jnp.dot(x_ref[...], w_ref[number], preferred_element_type=F32)
        return flat + b_ref[number : number + 1, :].astype(F32)

    queries = turn(part(0), *tables).astype(BF16)
    q_ref[...] = (queries.astype(F32) * HEAD_DIM**-0.5).astype(BF16)
    k_ref[...] = turn(part(1), *tables).astype(BF16)
    v_ref[...] = part(2).astype(BF16)


def project(gathered, w_qkv, b_qkv, tables):
    length, width = gathered.shape
    columns = w_qkv.shape[2]
    rows = min(256, length)
    table_spec = pl.BlockSpec((rows, tables[0].shape[1]), lambda i: (i, 0))
    out_spec = pl.BlockSpec((rows, columns), lambda i: (i, 0))
    return pl.pallas_call(
        project_kernel,
        grid=(length // rows,),
        in_specs=[
            pl.BlockSpec((rows, width), lambda i: (i, 0)),
            pl.BlockSpec(w_qkv.shape, lambda i: (0, 0, 0)),
            pl.BlockSpec(b_qkv.shape, lambda i: (0, 0)),
            table_spec,
            table_spec,
            table_spec,
        ],
        out_specs=[out_spec] * 3,
        out_shape=[jax.ShapeDtypeStruct((length, columns), BF16)] * 3,
        cost_estimate=pl.CostEstimate(
            flops=6 * length * width * columns,
            bytes_accessed=2 * (length * width + 3 * width * columns + 3 * length * columns),
            transcendentals=0,
        ),
        name="project",
    )(gathered, w_qkv, b_qkv, *tables)


def stack_heads(block):
    columns = block.shape[1]
    head_of = lax.broadcasted_iota(jnp.int32, block.shape, 1) // HEAD_DIM
    return jnp.concatenate(
        [
            jnp.where(head_of == head, block, jnp.zeros_like(block))
            for head in range(columns // HEAD_DIM)
        ],
        axis=0,
    )


def unstack_heads(stacked, block):
    heads = stacked.shape[1] // block
    return jnp.concatenate(
        [
            stacked[head * HEAD_DIM : (head + 1) * HEAD_DIM, head * block : (head + 1) * block]
            for head in range(heads)
        ],
        axis=0,
    ).T


def score_block(key_block, stacked_queries, key_at, start_row, query_row):
    scores = lax.dot_general(
        key_block, stacked_queries, (((1,), (1,)), ((), ())), preferred_element_type=F32
    )
    key_pos = key_at + lax.broadcasted_iota(jnp.int32, scores.shape, 0)
    allowed = (key_pos >= start_row) & (key_pos <= query_row)
    return scores, allowed


def query_rows(start_ref, block, heads):
    start_row = jnp.concatenate([start_ref[0]] * heads, axis=1)
    query_row = pl.program_id(0) * block + lax.broadcasted_iota(jnp.int32, (1, block), 1)
    return start_row, jnp.concatenate([query_row] * heads, axis=1)


def attend_kernel(first_ref, q_ref, k_ref, v_ref, start_ref, o_ref, lse_ref, acc_ref):
    block, columns = q_ref.shape
    heads = columns // HEAD_DIM
    index = pl.program_id(0)
    stacked = stack_heads(q_ref[...])
    start_row, query_row = query_rows(start_ref, block, heads)
    acc_ref[...] = jnp.zeros_like(acc_ref)

    def body(step, carry):
        highest, total = carry
        at = pl.multiple_of(step * BK, BK)
        scores, allowed = score_block(
            k_ref[pl.ds(at, BK), :], stacked, at, start_row, query_row
        )
        scores = jnp.where(allowed, scores, NEG)
        newest = jnp.maximum(highest, jnp.max(scores, axis=0, keepdims=True))
        weights = jnp.exp(scores - newest)
        scale = jnp.exp(highest - newest)
        total = total * scale + jnp.sum(weights, axis=0, keepdims=True)
        acc_ref[...] = acc_ref[...] * scale + lax.dot_general(
            v_ref[pl.ds(at, BK), :],
            weights.astype(BF16),
            (((0,), (0,)), ((), ())),
            preferred_element_type=F32,
        )
        return newest, total

    highest, total = lax.fori_loop(
        first_ref[index],
        (index * block + block - 1) // BK + 1,
        body,
        (jnp.full((1, heads * block), NEG, F32), jnp.zeros((1, heads * block), F32)),
    )
    o_ref[...] = unstack_heads(acc_ref[...] / total, block).astype(BF16)
    lse_ref[0] = highest + jnp.log(total)


def attend(first, queries, key_rows, value_rows, start_blocks):
    length, columns = queries.shape
    blocks = length // BQ
    heads = columns // HEAD_DIM
    row_spec = pl.BlockSpec((BQ, columns), lambda i, f: (i, 0))
    whole = pl.BlockSpec((length, columns), lambda i, f: (0, 0))
    return pl.pallas_call(
        attend_kernel,
        grid_spec=pltpu.PrefetchScalarGridSpec(
            num_scalar_prefetch=1,
            grid=(blocks,),
            in_specs=[
                row_spec,
                whole,
                whole,
                pl.BlockSpec((1, 1, BQ), lambda i, f: (i, 0, 0)),
            ],
            out_specs=[
                row_spec,
                pl.BlockSpec((1, 1, heads * BQ), lambda i, f: (i, 0, 0)),
            ],
            scratch_shapes=[pltpu.VMEM((columns, heads * BQ), F32)],
        ),
        out_shape=[
            jax.ShapeDtypeStruct((length, columns), BF16),
            jax.ShapeDtypeStruct((blocks, 1, heads * BQ), F32),
        ],
        cost_estimate=pl.CostEstimate(
            flops=4 * length * 1024 * columns * heads,
            bytes_accessed=8 * length * columns,
            transcendentals=length * 1024 * heads,
        ),
        name="attend",
    )(first, queries, key_rows, value_rows, start_blocks)


def attend_back_kernel(
    first_ref,
    q_ref,
    k_ref,
    v_ref,
    do_ref,
    o_ref,
    lse_ref,
    start_ref,
    cos_ref,
    low_ref,
    high_ref,
    grad_ref,
    key_acc,
    value_acc,
    query_acc,
):
    block, columns = q_ref.shape
    heads = columns // HEAD_DIM
    length = k_ref.shape[0]
    index = pl.program_id(0)

    @pl.when(index == 0)
    def _():
        key_acc[...] = jnp.zeros_like(key_acc)
        value_acc[...] = jnp.zeros_like(value_acc)

    stacked = stack_heads(q_ref[...])
    stacked_do = stack_heads(do_ref[...])
    start_row, query_row = query_rows(start_ref, block, heads)
    lse_row = lse_ref[0]
    products = do_ref[...].astype(F32) * o_ref[...].astype(F32)
    head_rows = lax.broadcasted_iota(jnp.int32, (8, columns), 0)
    head_lanes = lax.broadcasted_iota(jnp.int32, (8, columns), 1) // HEAD_DIM
    picked = lax.dot_general(
        (head_rows == head_lanes).astype(F32),
        products,
        (((1,), (1,)), ((), ())),
        precision=lax.Precision.HIGHEST,
        preferred_element_type=F32,
    )
    inner_row = jnp.concatenate([picked[head : head + 1, :] for head in range(heads)], axis=1)
    query_acc[...] = jnp.zeros_like(query_acc)

    def body(step, carry):
        at = pl.multiple_of(step * BK, BK)
        key_block = k_ref[pl.ds(at, BK), :]
        scores, allowed = score_block(key_block, stacked, at, start_row, query_row)
        weights = jnp.where(allowed, jnp.exp(scores - lse_row), 0.0)
        grad_weights = lax.dot_general(
            v_ref[pl.ds(at, BK), :],
            stacked_do,
            (((1,), (1,)), ((), ())),
            preferred_element_type=F32,
        )
        grad_scores = (weights * (grad_weights - inner_row)).astype(BF16)
        value_acc[pl.ds(at, BK), :] += jnp.dot(
            weights.astype(BF16), stacked_do, preferred_element_type=F32
        )
        key_acc[pl.ds(at, BK), :] += jnp.dot(grad_scores, stacked, preferred_element_type=F32)
        query_acc[...] += lax.dot_general(
            key_block, grad_scores, (((0,), (0,)), ((), ())), preferred_element_type=F32
        )
        return carry

    lax.fori_loop(first_ref[index], (index * block + block - 1) // BK + 1, body, 0)

    def turn_back(grads, at, rows):
        kept = grads.astype(BF16).astype(F32)
        return turn(
            kept,
            cos_ref[pl.ds(at, rows), :],
            -low_ref[pl.ds(at, rows), :],
            -high_ref[pl.ds(at, rows), :],
        ).astype(BF16)

    at_query = pl.multiple_of(index * block, block)
    grad_ref[pl.ds(at_query, block), :columns] = turn_back(
        unstack_heads(query_acc[...], block) * HEAD_DIM**-0.5, at_query, block
    )

    @pl.when(index == pl.num_programs(0) - 1)
    def _():
        def finish(step, carry):
            at = pl.multiple_of(step * BK, BK)
            grad_ref[pl.ds(at, BK), columns : 2 * columns] = turn_back(
                key_acc[pl.ds(at, BK), :], at, BK
            )
            grad_ref[pl.ds(at, BK), 2 * columns :] = value_acc[pl.ds(at, BK), :].astype(BF16)
            return carry

        lax.fori_loop(0, length // BK, finish, 0)


def attend_back(first, queries, key_rows, value_rows, grad_att, attended, lse, start_blocks, tables):
    length, columns = queries.shape
    blocks = length // BQ
    heads = columns // HEAD_DIM
    row_spec = pl.BlockSpec((BQ, columns), lambda i, f: (i, 0))
    whole = pl.BlockSpec((length, columns), lambda i, f: (0, 0))
    table_spec = pl.BlockSpec(tables[0].shape, lambda i, f: (0, 0))
    return pl.pallas_call(
        attend_back_kernel,
        grid_spec=pltpu.PrefetchScalarGridSpec(
            num_scalar_prefetch=1,
            grid=(blocks,),
            in_specs=[
                row_spec,
                whole,
                whole,
                row_spec,
                row_spec,
                pl.BlockSpec((1, 1, heads * BQ), lambda i, f: (i, 0, 0)),
                pl.BlockSpec((1, 1, BQ), lambda i, f: (i, 0, 0)),
                table_spec,
                table_spec,
                table_spec,
            ],
            out_specs=pl.BlockSpec((length, 3 * columns), lambda i, f: (0, 0)),
            scratch_shapes=[
                pltpu.VMEM((length, columns), F32),
                pltpu.VMEM((length, columns), F32),
                pltpu.VMEM((columns, heads * BQ), F32),
            ],
        ),
        out_shape=jax.ShapeDtypeStruct((length, 3 * columns), BF16),
        cost_estimate=pl.CostEstimate(
            flops=10 * length * 1024 * columns * heads,
            bytes_accessed=16 * length * columns,
            transcendentals=length * 1024 * heads,
        ),
        name="attend_back",
    )(first, queries, key_rows, value_rows, grad_att, attended, lse, start_blocks, *tables)


def bits_of(name):
    size = lax.axis_size(name)
    count = size.bit_length() - 1
    return count if size == 1 << count else None


def swap(values, name, bit):
    size = lax.axis_size(name)
    return lax.ppermute(values, name, [(i, i ^ (1 << bit)) for i in range(size)])


def write_stacked(piece, outs):
    outs[0][0] = piece.astype(F32)


def write_rows(piece, outs):
    at = 0
    for out_ref in outs:
        size = out_ref.shape[0]
        out_ref[...] = piece[at : at + size, :].astype(F32)
        at += size


def write_lanes(piece, outs):
    parts, _, size = outs[0].shape
    for part in range(parts):
        outs[0][part] = piece[:, part * size : (part + 1) * size].astype(F32)


def place_kernel(write, count, color_ref, where_ref, *refs):
    step = pl.program_id(0)
    for number in range(count):

        @pl.when(step == number)
        def _(number=number):
            write(refs[number][...], refs[count:])


def place_blocks(write, color, where, pieces, out_shapes, out_specs):
    rows, columns = pieces[0].shape
    count = len(pieces)
    return pl.pallas_call(
        functools.partial(place_kernel, write, count),
        grid_spec=pltpu.PrefetchScalarGridSpec(
            num_scalar_prefetch=2,
            grid=(count,),
            in_specs=[pl.BlockSpec((rows, columns), lambda i, c, w: (0, 0))] * count,
            out_specs=out_specs,
        ),
        out_shape=[jax.ShapeDtypeStruct(shape, F32) for shape in out_shapes],
        cost_estimate=pl.CostEstimate(
            flops=0, bytes_accessed=6 * count * rows * columns, transcendentals=0
        ),
        name="place_blocks",
    )(color, where, *pieces)


class DpSum:
    def __init__(self, *grads, paired=False):
        self.grads = grads
        self.paired = paired
        self.count = bits_of("dp")
        pieces = (1 if paired else 2) << self.count
        self.axis = 0 if all(g.shape[0] % (8 * pieces) == 0 for g in grads) else 1
        self.sizes = [g.shape[self.axis] // pieces for g in grads]
        self.mine = lax.axis_index("dp")
        self.orders = [list(range(self.count)), list(range(self.count))[::-1]]
        self.level = 0
        if paired:
            self.state = [((grad,), self.sizes[:1], 0) for grad in grads]
        else:
            self.state = [(grads, self.sizes, color << self.count) for color in range(2)]
        self.held = None
        self.ready()

    def cut(self, color, side):
        grads, units, base = self.state[color]
        span = (1 << self.count) >> (self.level + 1)
        parts = []
        for grad, unit in zip(grads, units):
            at = (base + side * span) * unit
            parts.append(lax.dynamic_slice_in_dim(grad, at, span * unit, self.axis))
        if len(parts) == 1:
            return parts[0]
        if self.axis:
            return jnp.concatenate(parts, axis=0)
        parts = [p.reshape(span, unit, p.shape[1]) for p, unit in zip(parts, units)]
        joined = jnp.concatenate(parts, axis=1)
        return joined.reshape(-1, joined.shape[2])

    def side(self, color):
        return (self.mine >> self.orders[color][self.level]) & 1

    def ready(self):
        if self.level < self.count:
            self.out = [self.cut(color, 1 - self.side(color)) for color in range(2)]
        elif self.held is None:
            self.held = [[(self.state[color][0][0], 0)] for color in range(2)]

    def send(self):
        if self.level < self.count:
            self.got = [
                swap(self.out[color], "dp", self.orders[color][self.level])
                for color in range(2)
            ]
            return
        for color in range(2):
            bit = self.orders[color][2 * self.count - 1 - self.level]
            self.held[color] += [
                (swap(piece, "dp", bit), mask ^ (1 << bit)) for piece, mask in self.held[color]
            ]

    def arrive(self):
        if self.level < self.count:
            state = []
            for color in range(2):
                keep = self.cut(color, self.side(color))
                total = (keep.astype(F32) + self.got[color].astype(F32)).astype(BF16)
                whole = self.axis == 0 and not self.paired
                state.append(((total,), [sum(self.sizes) if whole else self.sizes[0]], 0))
            self.state = state
        self.level += 1
        self.ready()

    def moving(self):
        return self.out if self.held is None else self.held

    def result(self, write):
        pieces, colors, where = [], [], []
        for color in range(2):
            for piece, mask in self.held[color]:
                owner = self.mine ^ mask
                spot = 0 if self.paired else color
                for bit in self.orders[color]:
                    spot = spot * 2 + ((owner >> bit) & 1)
                pieces.append(piece)
                colors.append(color)
                where.append(spot)
        rows, columns = pieces[0].shape
        length, width = self.grads[0].shape
        if write is write_stacked:
            shapes = [(2, length, width)]
            blocks = [(1, rows, columns)]
        elif write is write_lanes:
            shapes = [(3, length, width // 3)]
            blocks = [(3, rows, columns // 3)]
        else:
            shapes = [g.shape for g in self.grads]
            blocks = [(rows * s[0] // sum(t[0] for t in shapes), columns) for s in shapes]
        lead = {write_stacked: lambda i, c: (c[i],), write_lanes: lambda i, c: (0,)}.get(
            write, lambda i, c: ()
        )

        def out_map(i, c, w):
            return lead(i, c) + ((w[i], 0) if self.axis == 0 else (0, w[i]))

        return place_blocks(
            write,
            jnp.array(colors, jnp.int32),
            jnp.stack(where).astype(jnp.int32),
            pieces,
            shapes,
            [pl.BlockSpec(block, out_map) for block in blocks],
        )


def fence(values, *sums):
    values, moving = lax.optimization_barrier((values, [item.moving() for item in sums]))
    for item, arrived in zip(sums, moving):
        if item.held is None:
            item.out = arrived
        else:
            item.held = arrived
    return values


def sum_small(values, name, bits=None):
    count = bits_of(name)
    if count is None:
        return lax.psum(values, name) if bits is None or 0 in bits else values
    for bit in range(count) if bits is None else bits:
        values = values + swap(values, name, bit)
    return values


def tail_kernel(x_ref, g_ref, c_ref, gain_ref, stat_ref, grad_ref, sums_ref):
    @pl.when(pl.program_id(0) == 0)
    def _():
        sums_ref[...] = jnp.zeros_like(sums_ref)
        sums_ref[2:3, :] = stat_ref[...]

    residual = x_ref[...].astype(F32)
    centered = residual - jnp.mean(residual, -1, keepdims=True)
    inv_std = lax.rsqrt(jnp.mean(centered * centered, -1, keepdims=True) + EPSILON)
    normalized = centered * inv_std
    grads = g_ref[...].astype(F32)
    sums_ref[0:1, :] += jnp.sum(grads * normalized, axis=0, keepdims=True)
    sums_ref[1:2, :] += jnp.sum(grads, axis=0, keepdims=True)
    scaled = grads * gain_ref[...]
    grad_ref[:, 0, :] = (
        inv_std
        * (
            scaled
            - jnp.mean(scaled, -1, keepdims=True)
            - normalized * jnp.mean(scaled * normalized, -1, keepdims=True)
        )
        + c_ref[...].astype(F32)
    )


def tail(layer_in, grad_normed, cot_here, norm_gain, stat_row):
    length, width = layer_in.shape
    rows = min(64, length)
    row_spec = pl.BlockSpec((rows, width), lambda i: (i, 0))
    one_spec = pl.BlockSpec((1, width), lambda i: (0, 0))
    return pl.pallas_call(
        tail_kernel,
        grid=(length // rows,),
        in_specs=[row_spec, row_spec, row_spec, one_spec, one_spec],
        out_specs=[
            pl.BlockSpec((rows, 1, width), lambda i: (i, 0, 0)),
            pl.BlockSpec((4, width), lambda i: (0, 0)),
        ],
        out_shape=[
            jax.ShapeDtypeStruct((length, 1, width), F32),
            jax.ShapeDtypeStruct((4, width), F32),
        ],
        name="tail",
    )(layer_in, grad_normed, cot_here, norm_gain.reshape(1, width), stat_row)


def back_products_kernel(p_ref, q_ref, g_ref, u_ref, w_ref, out_ref):
    turned = (((1,), (1,)), ((), ()))
    columns = q_ref.shape[2]
    total = jnp.dot(g_ref[...], w_ref[0], preferred_element_type=F32)
    total += jnp.dot(u_ref[...], w_ref[1], preferred_element_type=F32)
    for number in range(3):
        total += lax.dot_general(
            p_ref[:, number * columns : (number + 1) * columns],
            q_ref[number],
            turned,
            preferred_element_type=F32,
        )
    out_ref[...] = total.astype(BF16)


def back_products(grad_proj, w_qkv, grad_gate, grad_up, w_gate_up):
    length = grad_proj.shape[0]
    _, width, columns = w_qkv.shape
    hidden = grad_gate.shape[1]
    rows = min(256, length)
    return pl.pallas_call(
        back_products_kernel,
        grid=(length // rows,),
        in_specs=[
            pl.BlockSpec((rows, 3 * columns), lambda i: (i, 0)),
            pl.BlockSpec(w_qkv.shape, lambda i: (0, 0, 0)),
            pl.BlockSpec((rows, hidden), lambda i: (i, 0)),
            pl.BlockSpec((rows, hidden), lambda i: (i, 0)),
            pl.BlockSpec(w_gate_up.shape, lambda i: (0, 0, 0)),
        ],
        out_specs=pl.BlockSpec((rows, width), lambda i: (i, 0)),
        out_shape=jax.ShapeDtypeStruct((length, width), BF16),
        name="back_products",
    )(grad_proj, w_qkv, grad_gate, grad_up, w_gate_up)


def local(
    layer_in,
    segment_ids,
    valid_counts,
    norm_gain,
    norm_shift,
    w_qkv,
    b_qkv,
    w_out,
    w_gate_up,
    w_down,
    out_grad,
):
    local_len, row_count, model_width = layer_in.shape
    assert row_count == 1
    seq_len = local_len * lax.axis_size("mp")
    col_qkv = w_qkv.shape[2]
    ff_local = w_gate_up.shape[2]
    layer_in = layer_in[:, 0]
    position_here = lax.axis_index("mp") * local_len + jnp.arange(local_len, dtype=jnp.int32)
    valid_here = (position_here < valid_counts[0]).astype(F32)

    residual = layer_in.astype(F32)
    centered = residual - jnp.mean(residual, -1, keepdims=True)
    inv_std = lax.rsqrt(jnp.mean(centered * centered, -1, keepdims=True) + EPSILON)
    normalized = centered * inv_std
    normed = (normalized * norm_gain + norm_shift).astype(BF16)
    cot_here = jnp.where(valid_here[:, None] > 0, out_grad[:, 0], jnp.zeros((), BF16))
    gathered = lax.all_gather(normed, "mp", axis=0, tiled=True)
    cotangent = lax.all_gather(cot_here, "mp", axis=0, tiled=True)

    w_qkv = jnp.transpose(w_qkv, (1, 0, 2))
    w_gate_up = jnp.transpose(w_gate_up, (1, 2, 0))
    starts = starts_of(segment_ids)[0]
    tables = rotary_lanes(jnp.arange(seq_len, dtype=jnp.int32) - starts)
    start_blocks = starts.reshape(seq_len // BQ, 1, BQ)
    first = start_blocks[:, 0, 0] // BK
    gathered, tables, first, start_blocks = lax.optimization_barrier(
        (gathered, tables, first, start_blocks)
    )

    def product(left, right):
        return jnp.dot(left, right, preferred_element_type=F32).astype(BF16)

    def turned_product(left, right):
        return lax.dot_general(
            left, right, (((1,), (1,)), ((), ())), preferred_element_type=F32
        )

    def token_sum(left, right):
        return lax.dot_general(
            left, right, (((0,), (0,)), ((), ())), preferred_element_type=F32
        ).astype(BF16)

    def scattered(partial):
        return lax.psum_scatter(partial, "mp", scatter_dimension=0, tiled=True)

    gate = turned_product(gathered, w_gate_up[0])
    up = turned_product(gathered, w_gate_up[1])
    sigmoid_gate = jax.nn.sigmoid(gate)
    hidden = (gate * sigmoid_gate * up).astype(BF16)
    mlp_partial = product(hidden, w_down)
    mlp_sum = scattered(mlp_partial)
    gathered_next, mlp_partial = lax.optimization_barrier((gathered, mlp_partial))
    queries, key_rows, value_rows = project(gathered_next, w_qkv, b_qkv, tables)
    attended, lse = attend(first, queries, key_rows, value_rows, start_blocks)
    attn_partial = product(attended, w_out)
    attn_sum = scattered(attn_partial)

    cotangent, attn_partial = lax.optimization_barrier((cotangent, attn_partial))
    grad_hid = turned_product(cotangent, w_down).astype(BF16).astype(F32)
    grad_gate = (
        grad_hid * up * sigmoid_gate * (1.0 + gate * (1.0 - sigmoid_gate))
    ).astype(BF16)
    grad_up = (grad_hid * gate * sigmoid_gate).astype(BF16)
    sum_down = DpSum(token_sum(hidden, cotangent), token_sum(attended, cotangent))
    gathered_next = fence(gathered, sum_down)
    sum_down.send()
    sum_gate_up = DpSum(
        token_sum(grad_gate, gathered_next), token_sum(grad_up, gathered_next), paired=True
    )
    sum_down.arrive()
    cotangent = fence(cotangent, sum_gate_up, sum_down)
    grad_att = turned_product(cotangent, w_out).astype(BF16)
    sum_gate_up.send()
    sum_down.send()
    grad_proj = attend_back(
        first, queries, key_rows, value_rows, grad_att, attended, lse, start_blocks, tables
    )
    sum_gate_up.arrive()
    sum_down.arrive()
    grad_proj, mlp_sum = fence((grad_proj, mlp_sum), sum_gate_up, sum_down)
    sum_gate_up.send()
    sum_down.send()
    sum_qkv = DpSum(token_sum(gathered, grad_proj))
    sum_gate_up.arrive()
    sum_down.arrive()
    bias_sums = jnp.sum(grad_proj, axis=0, dtype=F32).reshape(-1, 128)
    grad_proj, bias_sums = fence((grad_proj, bias_sums), sum_gate_up, sum_down, sum_qkv)
    sum_qkv.send()
    sum_down.send()
    bias_sums = sum_small(bias_sums, "dp", [0])
    normed_partial = back_products(grad_proj, w_qkv, grad_gate, grad_up, w_gate_up)
    sum_qkv.arrive()
    sum_down.arrive()
    fresh = [held[len(held) // 2][0] for held in sum_down.held]
    normed_partial, attn_sum, bias_sums, _ = fence(
        (normed_partial, attn_sum, bias_sums, fresh), sum_gate_up, sum_qkv
    )
    grad_normed = scattered(normed_partial)
    sum_gate_up.send()
    sum_qkv.send()
    bias_sums = sum_small(bias_sums, "dp", range(1, sum_qkv.count))
    while sum_down.level < 2 * sum_down.count:
        sum_down.send()
        sum_down.arrive()
    down_sums = sum_down.result(write_rows)
    mlp_part = mlp_sum.astype(F32)
    attn_part = attn_sum.astype(F32)
    layer_out = (residual + attn_part + mlp_part).astype(BF16)
    statistics = jnp.stack(
        [
            jnp.sum(valid_here * jnp.sum(residual * residual, -1)),
            jnp.sum(valid_here * jnp.sum(attn_part * attn_part, -1)),
            jnp.sum(valid_here * jnp.sum(mlp_part * mlp_part, -1)),
            jnp.sum(valid_here),
        ]
    )
    stat_row = jnp.pad(statistics, (0, model_width - 4)).reshape(1, model_width)
    sum_gate_up.arrive()
    sum_qkv.arrive()
    bias_sums, layer_out, stat_row = fence(
        (bias_sums, layer_out, stat_row), sum_gate_up, sum_qkv
    )
    sum_gate_up.send()
    sum_qkv.send()
    sum_gate_up.arrive()
    sum_qkv.arrive()
    down_sums = fence(down_sums, sum_gate_up, sum_qkv)
    for item in (sum_gate_up, sum_qkv):
        while item.level < 2 * item.count:
            item.send()
            item.arrive()
    (grad_w_gate_up,) = sum_gate_up.result(write_stacked)
    grad_normed, grad_w_gate_up = fence((grad_normed, grad_w_gate_up), sum_qkv)
    (grad_w_qkv,) = sum_qkv.result(write_lanes)
    grad_w_down, grad_w_out = down_sums
    input_grad, small = tail(layer_in, grad_normed, cot_here, norm_gain, stat_row)
    small = sum_small(sum_small(small, "mp"), "dp")
    totals = small[2]
    return (
        layer_out[:, None],
        input_grad,
        small[0],
        small[1],
        jnp.transpose(grad_w_qkv, (1, 0, 2)),
        bias_sums.reshape(3, col_qkv),
        grad_w_out,
        jnp.transpose(grad_w_gate_up, (2, 0, 1)),
        grad_w_down,
        jnp.sqrt(totals[:3] / (totals[3] * model_width)),
    )


def solution(mesh):
    placed = (
        P("mp", "dp", None),
        P("dp", None),
        P("dp"),
        P(),
        P(),
        P(None, None, "mp"),
        P(None, "mp"),
        P("mp", None),
        P(None, None, "mp"),
        P("mp", None),
        P("mp", "dp", None),
    )
    return jax.shard_map(
        local,
        mesh=mesh,
        in_specs=placed,
        out_specs=(
            P("mp", "dp", None),
            P("mp", "dp", None),
            P(),
            P(),
            P(None, None, "mp"),
            P(None, "mp"),
            P("mp", None),
            P(None, None, "mp"),
            P("mp", None),
            P(),
        ),
        check_vma=False,
    )
```

```python
import functools

import jax
import jax.numpy as jnp
from jax import lax
from jax.experimental import pallas as pl
from jax.experimental.pallas import tpu as pltpu
from jax.sharding import PartitionSpec as P

HEAD_DIM = 64
ROT = 16
EPSILON = 1e-05
BQ = 128
BK = 256
NEG = -1e30
F32 = jnp.float32
BF16 = jnp.bfloat16


def starts_of(segment_ids):
    length = segment_ids.shape[1]
    steps_all = jnp.arange(length, dtype=jnp.int32)[None, :]
    change = jnp.concatenate(
        [
            jnp.ones_like(segment_ids[:, :1]),
            (segment_ids[:, 1:] != segment_ids[:, :-1]).astype(jnp.int32),
        ],
        axis=1,
    )
    return lax.cummax(jnp.where(change > 0, steps_all, jnp.zeros_like(change)), axis=1)


def rotary_lanes(positions):
    half_rot = ROT // 2
    lane = jnp.arange(2 * HEAD_DIM, dtype=jnp.int32) % HEAD_DIM
    power = (lane % half_rot).astype(F32)
    frequency = jnp.where(lane < ROT, 10000.0 ** (-(power * 2.0) / ROT), 0.0)
    angles = positions.astype(F32)[:, None] * frequency
    sine = jnp.sin(angles)
    low = jnp.where(lane < half_rot, -sine, 0.0)
    high = jnp.where((lane >= half_rot) & (lane < ROT), sine, 0.0)
    return jnp.cos(angles), low, high


def lane_tile(table, columns):
    return jnp.concatenate([table] * (columns // table.shape[1]), axis=1)


def turn(values, cosine, low, high):
    columns = values.shape[1]
    half_rot = ROT // 2
    return (
        values * lane_tile(cosine, columns)
        + pltpu.roll(values, columns - half_rot, 1) * lane_tile(low, columns)
        + pltpu.roll(values, half_rot, 1) * lane_tile(high, columns)
    )


def project_kernel(x_ref, w_ref, b_ref, cos_ref, low_ref, high_ref, q_ref, k_ref, v_ref):
    tables = (cos_ref[...], low_ref[...], high_ref[...])

    def part(number):
        flat = jnp.dot(x_ref[...], w_ref[number], preferred_element_type=F32)
        return flat + b_ref[number : number + 1, :].astype(F32)

    queries = turn(part(0), *tables).astype(BF16)
    q_ref[...] = (queries.astype(F32) * HEAD_DIM**-0.5).astype(BF16)
    k_ref[...] = turn(part(1), *tables).astype(BF16)
    v_ref[...] = part(2).astype(BF16)


def project(gathered, w_qkv, b_qkv, tables):
    length, width = gathered.shape
    columns = w_qkv.shape[2]
    rows = min(256, length)
    table_spec = pl.BlockSpec((rows, tables[0].shape[1]), lambda i: (i, 0))
    out_spec = pl.BlockSpec((rows, columns), lambda i: (i, 0))
    return pl.pallas_call(
        project_kernel,
        grid=(length // rows,),
        in_specs=[
            pl.BlockSpec((rows, width), lambda i: (i, 0)),
            pl.BlockSpec(w_qkv.shape, lambda i: (0, 0, 0)),
            pl.BlockSpec(b_qkv.shape, lambda i: (0, 0)),
            table_spec,
            table_spec,
            table_spec,
        ],
        out_specs=[out_spec] * 3,
        out_shape=[jax.ShapeDtypeStruct((length, columns), BF16)] * 3,
        cost_estimate=pl.CostEstimate(
            flops=6 * length * width * columns,
            bytes_accessed=2 * (length * width + 3 * width * columns + 3 * length * columns),
            transcendentals=0,
        ),
        name="project",
    )(gathered, w_qkv, b_qkv, *tables)


def stack_heads(block):
    columns = block.shape[1]
    head_of = lax.broadcasted_iota(jnp.int32, block.shape, 1) // HEAD_DIM
    return jnp.concatenate(
        [
            jnp.where(head_of == head, block, jnp.zeros_like(block))
            for head in range(columns // HEAD_DIM)
        ],
        axis=0,
    )


def unstack_heads(stacked, block):
    heads = stacked.shape[1] // block
    return jnp.concatenate(
        [
            stacked[head * HEAD_DIM : (head + 1) * HEAD_DIM, head * block : (head + 1) * block]
            for head in range(heads)
        ],
        axis=0,
    ).T


def score_block(key_block, stacked_queries, key_at, start_row, query_row):
    scores = lax.dot_general(
        key_block, stacked_queries, (((1,), (1,)), ((), ())), preferred_element_type=F32
    )
    key_pos = key_at + lax.broadcasted_iota(jnp.int32, scores.shape, 0)
    allowed = (key_pos >= start_row) & (key_pos <= query_row)
    return scores, allowed


def query_rows(start_ref, block, heads):
    start_row = jnp.concatenate([start_ref[0]] * heads, axis=1)
    query_row = pl.program_id(0) * block + lax.broadcasted_iota(jnp.int32, (1, block), 1)
    return start_row, jnp.concatenate([query_row] * heads, axis=1)


def attend_kernel(first_ref, q_ref, k_ref, v_ref, start_ref, o_ref, lse_ref, acc_ref):
    block, columns = q_ref.shape
    heads = columns // HEAD_DIM
    index = pl.program_id(0)
    stacked = stack_heads(q_ref[...])
    start_row, query_row = query_rows(start_ref, block, heads)
    acc_ref[...] = jnp.zeros_like(acc_ref)

    def body(step, carry):
        highest, total = carry
        at = pl.multiple_of(step * BK, BK)
        scores, allowed = score_block(
            k_ref[pl.ds(at, BK), :], stacked, at, start_row, query_row
        )
        scores = jnp.where(allowed, scores, NEG)
        newest = jnp.maximum(highest, jnp.max(scores, axis=0, keepdims=True))
        weights = jnp.exp(scores - newest)
        scale = jnp.exp(highest - newest)
        total = total * scale + jnp.sum(weights, axis=0, keepdims=True)
        acc_ref[...] = acc_ref[...] * scale + lax.dot_general(
            v_ref[pl.ds(at, BK), :],
            weights.astype(BF16),
            (((0,), (0,)), ((), ())),
            preferred_element_type=F32,
        )
        return newest, total

    highest, total = lax.fori_loop(
        first_ref[index],
        (index * block + block - 1) // BK + 1,
        body,
        (jnp.full((1, heads * block), NEG, F32), jnp.zeros((1, heads * block), F32)),
    )
    o_ref[...] = unstack_heads(acc_ref[...] / total, block).astype(BF16)
    lse_ref[0] = highest + jnp.log(total)


def attend(first, queries, key_rows, value_rows, start_blocks):
    length, columns = queries.shape
    blocks = length // BQ
    heads = columns // HEAD_DIM
    row_spec = pl.BlockSpec((BQ, columns), lambda i, f: (i, 0))
    whole = pl.BlockSpec((length, columns), lambda i, f: (0, 0))
    return pl.pallas_call(
        attend_kernel,
        grid_spec=pltpu.PrefetchScalarGridSpec(
            num_scalar_prefetch=1,
            grid=(blocks,),
            in_specs=[
                row_spec,
                whole,
                whole,
                pl.BlockSpec((1, 1, BQ), lambda i, f: (i, 0, 0)),
            ],
            out_specs=[
                row_spec,
                pl.BlockSpec((1, 1, heads * BQ), lambda i, f: (i, 0, 0)),
            ],
            scratch_shapes=[pltpu.VMEM((columns, heads * BQ), F32)],
        ),
        out_shape=[
            jax.ShapeDtypeStruct((length, columns), BF16),
            jax.ShapeDtypeStruct((blocks, 1, heads * BQ), F32),
        ],
        cost_estimate=pl.CostEstimate(
            flops=4 * length * 1024 * columns * heads,
            bytes_accessed=8 * length * columns,
            transcendentals=length * 1024 * heads,
        ),
        name="attend",
    )(first, queries, key_rows, value_rows, start_blocks)


def attend_back_kernel(
    first_ref,
    q_ref,
    k_ref,
    v_ref,
    do_ref,
    o_ref,
    lse_ref,
    start_ref,
    cos_ref,
    low_ref,
    high_ref,
    grad_ref,
    key_acc,
    value_acc,
    query_acc,
):
    block, columns = q_ref.shape
    heads = columns // HEAD_DIM
    length = k_ref.shape[0]
    index = pl.program_id(0)

    @pl.when(index == 0)
    def _():
        key_acc[...] = jnp.zeros_like(key_acc)
        value_acc[...] = jnp.zeros_like(value_acc)

    stacked = stack_heads(q_ref[...])
    stacked_do = stack_heads(do_ref[...])
    start_row, query_row = query_rows(start_ref, block, heads)
    lse_row = lse_ref[0]
    products = do_ref[...].astype(F32) * o_ref[...].astype(F32)
    head_rows = lax.broadcasted_iota(jnp.int32, (8, columns), 0)
    head_lanes = lax.broadcasted_iota(jnp.int32, (8, columns), 1) // HEAD_DIM
    picked = lax.dot_general(
        (head_rows == head_lanes).astype(F32),
        products,
        (((1,), (1,)), ((), ())),
        precision=lax.Precision.HIGHEST,
        preferred_element_type=F32,
    )
    inner_row = jnp.concatenate([picked[head : head + 1, :] for head in range(heads)], axis=1)
    query_acc[...] = jnp.zeros_like(query_acc)

    def body(step, carry):
        at = pl.multiple_of(step * BK, BK)
        key_block = k_ref[pl.ds(at, BK), :]
        scores, allowed = score_block(key_block, stacked, at, start_row, query_row)
        weights = jnp.where(allowed, jnp.exp(scores - lse_row), 0.0)
        grad_weights = lax.dot_general(
            v_ref[pl.ds(at, BK), :],
            stacked_do,
            (((1,), (1,)), ((), ())),
            preferred_element_type=F32,
        )
        grad_scores = (weights * (grad_weights - inner_row)).astype(BF16)
        value_acc[pl.ds(at, BK), :] += jnp.dot(
            weights.astype(BF16), stacked_do, preferred_element_type=F32
        )
        key_acc[pl.ds(at, BK), :] += jnp.dot(grad_scores, stacked, preferred_element_type=F32)
        query_acc[...] += lax.dot_general(
            key_block, grad_scores, (((0,), (0,)), ((), ())), preferred_element_type=F32
        )
        return carry

    lax.fori_loop(first_ref[index], (index * block + block - 1) // BK + 1, body, 0)

    def turn_back(grads, at, rows):
        kept = grads.astype(BF16).astype(F32)
        return turn(
            kept,
            cos_ref[pl.ds(at, rows), :],
            -low_ref[pl.ds(at, rows), :],
            -high_ref[pl.ds(at, rows), :],
        ).astype(BF16)

    at_query = pl.multiple_of(index * block, block)
    grad_ref[pl.ds(at_query, block), :columns] = turn_back(
        unstack_heads(query_acc[...], block) * HEAD_DIM**-0.5, at_query, block
    )

    @pl.when(index == pl.num_programs(0) - 1)
    def _():
        def finish(step, carry):
            at = pl.multiple_of(step * BK, BK)
            grad_ref[pl.ds(at, BK), columns : 2 * columns] = turn_back(
                key_acc[pl.ds(at, BK), :], at, BK
            )
            grad_ref[pl.ds(at, BK), 2 * columns :] = value_acc[pl.ds(at, BK), :].astype(BF16)
            return carry

        lax.fori_loop(0, length // BK, finish, 0)


def attend_back(first, queries, key_rows, value_rows, grad_att, attended, lse, start_blocks, tables):
    length, columns = queries.shape
    blocks = length // BQ
    heads = columns // HEAD_DIM
    row_spec = pl.BlockSpec((BQ, columns), lambda i, f: (i, 0))
    whole = pl.BlockSpec((length, columns), lambda i, f: (0, 0))
    table_spec = pl.BlockSpec(tables[0].shape, lambda i, f: (0, 0))
    return pl.pallas_call(
        attend_back_kernel,
        grid_spec=pltpu.PrefetchScalarGridSpec(
            num_scalar_prefetch=1,
            grid=(blocks,),
            in_specs=[
                row_spec,
                whole,
                whole,
                row_spec,
                row_spec,
                pl.BlockSpec((1, 1, heads * BQ), lambda i, f: (i, 0, 0)),
                pl.BlockSpec((1, 1, BQ), lambda i, f: (i, 0, 0)),
                table_spec,
                table_spec,
                table_spec,
            ],
            out_specs=pl.BlockSpec((length, 3 * columns), lambda i, f: (0, 0)),
            scratch_shapes=[
                pltpu.VMEM((length, columns), F32),
                pltpu.VMEM((length, columns), F32),
                pltpu.VMEM((columns, heads * BQ), F32),
            ],
        ),
        out_shape=jax.ShapeDtypeStruct((length, 3 * columns), BF16),
        cost_estimate=pl.CostEstimate(
            flops=10 * length * 1024 * columns * heads,
            bytes_accessed=16 * length * columns,
            transcendentals=length * 1024 * heads,
        ),
        name="attend_back",
    )(first, queries, key_rows, value_rows, grad_att, attended, lse, start_blocks, *tables)


def bits_of(name):
    size = lax.axis_size(name)
    count = size.bit_length() - 1
    return count if size == 1 << count else None


def swap(values, name, bit):
    size = lax.axis_size(name)
    return lax.ppermute(values, name, [(i, i ^ (1 << bit)) for i in range(size)])


def write_stacked(piece, outs):
    outs[0][0] = piece.astype(F32)


def write_rows(piece, outs):
    at = 0
    for out_ref in outs:
        size = out_ref.shape[0]
        out_ref[...] = piece[at : at + size, :].astype(F32)
        at += size


def write_lanes(piece, outs):
    parts, _, size = outs[0].shape
    for part in range(parts):
        outs[0][part] = piece[:, part * size : (part + 1) * size].astype(F32)


def place_kernel(write, count, color_ref, where_ref, *refs):
    step = pl.program_id(0)
    for number in range(count):

        @pl.when(step == number)
        def _(number=number):
            write(refs[number][...], refs[count:])


def place_blocks(write, color, where, pieces, out_shapes, out_specs):
    rows, columns = pieces[0].shape
    count = len(pieces)
    return pl.pallas_call(
        functools.partial(place_kernel, write, count),
        grid_spec=pltpu.PrefetchScalarGridSpec(
            num_scalar_prefetch=2,
            grid=(count,),
            in_specs=[pl.BlockSpec((rows, columns), lambda i, c, w: (0, 0))] * count,
            out_specs=out_specs,
        ),
        out_shape=[jax.ShapeDtypeStruct(shape, F32) for shape in out_shapes],
        cost_estimate=pl.CostEstimate(
            flops=0, bytes_accessed=6 * count * rows * columns, transcendentals=0
        ),
        name="place_blocks",
    )(color, where, *pieces)


class DpSum:
    def __init__(self, *grads, paired=False):
        self.grads = grads
        self.paired = paired
        self.count = bits_of("dp")
        pieces = (1 if paired else 2) << self.count
        self.axis = 0 if all(g.shape[0] % (8 * pieces) == 0 for g in grads) else 1
        self.sizes = [g.shape[self.axis] // pieces for g in grads]
        self.mine = lax.axis_index("dp")
        self.orders = [list(range(self.count)), list(range(self.count))[::-1]]
        self.level = 0
        if paired:
            self.state = [((grad,), self.sizes[:1], 0) for grad in grads]
        else:
            self.state = [(grads, self.sizes, color << self.count) for color in range(2)]
        self.held = None
        self.ready()

    def cut(self, color, side):
        grads, units, base = self.state[color]
        span = (1 << self.count) >> (self.level + 1)
        parts = []
        for grad, unit in zip(grads, units):
            at = (base + side * span) * unit
            parts.append(lax.dynamic_slice_in_dim(grad, at, span * unit, self.axis))
        if len(parts) == 1:
            return parts[0]
        if self.axis:
            return jnp.concatenate(parts, axis=0)
        parts = [p.reshape(span, unit, p.shape[1]) for p, unit in zip(parts, units)]
        joined = jnp.concatenate(parts, axis=1)
        return joined.reshape(-1, joined.shape[2])

    def side(self, color):
        return (self.mine >> self.orders[color][self.level]) & 1

    def ready(self):
        if self.level < self.count:
            self.out = [self.cut(color, 1 - self.side(color)) for color in range(2)]
        elif self.held is None:
            self.held = [[(self.state[color][0][0], 0)] for color in range(2)]

    def send(self):
        if self.level < self.count:
            self.got = [
                swap(self.out[color], "dp", self.orders[color][self.level])
                for color in range(2)
            ]
            return
        for color in range(2):
            bit = self.orders[color][2 * self.count - 1 - self.level]
            self.held[color] += [
                (swap(piece, "dp", bit), mask ^ (1 << bit)) for piece, mask in self.held[color]
            ]

    def arrive(self):
        if self.level < self.count:
            state = []
            for color in range(2):
                keep = self.cut(color, self.side(color))
                total = (keep.astype(F32) + self.got[color].astype(F32)).astype(BF16)
                whole = self.axis == 0 and not self.paired
                state.append(((total,), [sum(self.sizes) if whole else self.sizes[0]], 0))
            self.state = state
        self.level += 1
        self.ready()

    def moving(self):
        return self.out if self.held is None else self.held

    def result(self, write):
        pieces, colors, where = [], [], []
        for color in range(2):
            for piece, mask in self.held[color]:
                owner = self.mine ^ mask
                spot = 0 if self.paired else color
                for bit in self.orders[color]:
                    spot = spot * 2 + ((owner >> bit) & 1)
                pieces.append(piece)
                colors.append(color)
                where.append(spot)
        rows, columns = pieces[0].shape
        length, width = self.grads[0].shape
        if write is write_stacked:
            shapes = [(2, length, width)]
            blocks = [(1, rows, columns)]
        elif write is write_lanes:
            shapes = [(3, length, width // 3)]
            blocks = [(3, rows, columns // 3)]
        else:
            shapes = [g.shape for g in self.grads]
            blocks = [(rows * s[0] // sum(t[0] for t in shapes), columns) for s in shapes]
        lead = {write_stacked: lambda i, c: (c[i],), write_lanes: lambda i, c: (0,)}.get(
            write, lambda i, c: ()
        )

        def out_map(i, c, w):
            return lead(i, c) + ((w[i], 0) if self.axis == 0 else (0, w[i]))

        return place_blocks(
            write,
            jnp.array(colors, jnp.int32),
            jnp.stack(where).astype(jnp.int32),
            pieces,
            shapes,
            [pl.BlockSpec(block, out_map) for block in blocks],
        )


def fence(values, *sums):
    values, moving = lax.optimization_barrier((values, [item.moving() for item in sums]))
    for item, arrived in zip(sums, moving):
        if item.held is None:
            item.out = arrived
        else:
            item.held = arrived
    return values


def sum_small(values, name, bits=None):
    count = bits_of(name)
    if count is None:
        return lax.psum(values, name) if bits is None or 0 in bits else values
    for bit in range(count) if bits is None else bits:
        values = values + swap(values, name, bit)
    return values


def tail_kernel(x_ref, g_ref, c_ref, gain_ref, stat_ref, grad_ref, sums_ref):
    @pl.when(pl.program_id(0) == 0)
    def _():
        sums_ref[...] = jnp.zeros_like(sums_ref)
        sums_ref[2:3, :] = stat_ref[...]

    residual = x_ref[...].astype(F32)
    centered = residual - jnp.mean(residual, -1, keepdims=True)
    inv_std = lax.rsqrt(jnp.mean(centered * centered, -1, keepdims=True) + EPSILON)
    normalized = centered * inv_std
    grads = g_ref[...].astype(F32)
    sums_ref[0:1, :] += jnp.sum(grads * normalized, axis=0, keepdims=True)
    sums_ref[1:2, :] += jnp.sum(grads, axis=0, keepdims=True)
    scaled = grads * gain_ref[...]
    grad_ref[:, 0, :] = (
        inv_std
        * (
            scaled
            - jnp.mean(scaled, -1, keepdims=True)
            - normalized * jnp.mean(scaled * normalized, -1, keepdims=True)
        )
        + c_ref[...].astype(F32)
    )


def tail(layer_in, grad_normed, cot_here, norm_gain, stat_row):
    length, width = layer_in.shape
    rows = min(64, length)
    row_spec = pl.BlockSpec((rows, width), lambda i: (i, 0))
    one_spec = pl.BlockSpec((1, width), lambda i: (0, 0))
    return pl.pallas_call(
        tail_kernel,
        grid=(length // rows,),
        in_specs=[row_spec, row_spec, row_spec, one_spec, one_spec],
        out_specs=[
            pl.BlockSpec((rows, 1, width), lambda i: (i, 0, 0)),
            pl.BlockSpec((4, width), lambda i: (0, 0)),
        ],
        out_shape=[
            jax.ShapeDtypeStruct((length, 1, width), F32),
            jax.ShapeDtypeStruct((4, width), F32),
        ],
        name="tail",
    )(layer_in, grad_normed, cot_here, norm_gain.reshape(1, width), stat_row)


def back_products_kernel(p_ref, q_ref, g_ref, u_ref, w_ref, out_ref):
    turned = (((1,), (1,)), ((), ()))
    columns = q_ref.shape[2]
    total = jnp.dot(g_ref[...], w_ref[0], preferred_element_type=F32)
    total += jnp.dot(u_ref[...], w_ref[1], preferred_element_type=F32)
    for number in range(3):
        total += lax.dot_general(
            p_ref[:, number * columns : (number + 1) * columns],
            q_ref[number],
            turned,
            preferred_element_type=F32,
        )
    out_ref[...] = total.astype(BF16)


def back_products(grad_proj, w_qkv, grad_gate, grad_up, w_gate_up):
    length = grad_proj.shape[0]
    _, width, columns = w_qkv.shape
    hidden = grad_gate.shape[1]
    rows = min(256, length)
    return pl.pallas_call(
        back_products_kernel,
        grid=(length // rows,),
        in_specs=[
            pl.BlockSpec((rows, 3 * columns), lambda i: (i, 0)),
            pl.BlockSpec(w_qkv.shape, lambda i: (0, 0, 0)),
            pl.BlockSpec((rows, hidden), lambda i: (i, 0)),
            pl.BlockSpec((rows, hidden), lambda i: (i, 0)),
            pl.BlockSpec(w_gate_up.shape, lambda i: (0, 0, 0)),
        ],
        out_specs=pl.BlockSpec((rows, width), lambda i: (i, 0)),
        out_shape=jax.ShapeDtypeStruct((length, width), BF16),
        name="back_products",
    )(grad_proj, w_qkv, grad_gate, grad_up, w_gate_up)


def local(
    layer_in,
    segment_ids,
    valid_counts,
    norm_gain,
    norm_shift,
    w_qkv,
    b_qkv,
    w_out,
    w_gate_up,
    w_down,
    out_grad,
):
    local_len, row_count, model_width = layer_in.shape
    assert row_count == 1
    seq_len = local_len * lax.axis_size("mp")
    col_qkv = w_qkv.shape[2]
    ff_local = w_gate_up.shape[2]
    layer_in = layer_in[:, 0]
    position_here = lax.axis_index("mp") * local_len + jnp.arange(local_len, dtype=jnp.int32)
    valid_here = (position_here < valid_counts[0]).astype(F32)

    residual = layer_in.astype(F32)
    centered = residual - jnp.mean(residual, -1, keepdims=True)
    inv_std = lax.rsqrt(jnp.mean(centered * centered, -1, keepdims=True) + EPSILON)
    normalized = centered * inv_std
    normed = (normalized * norm_gain + norm_shift).astype(BF16)
    cot_here = jnp.where(valid_here[:, None] > 0, out_grad[:, 0], jnp.zeros((), BF16))
    gathered = lax.all_gather(normed, "mp", axis=0, tiled=True)
    cotangent = lax.all_gather(cot_here, "mp", axis=0, tiled=True)

    w_qkv = jnp.transpose(w_qkv, (1, 0, 2))
    w_gate_up = jnp.transpose(w_gate_up, (1, 2, 0))
    starts = starts_of(segment_ids)[0]
    tables = rotary_lanes(jnp.arange(seq_len, dtype=jnp.int32) - starts)
    start_blocks = starts.reshape(seq_len // BQ, 1, BQ)
    first = start_blocks[:, 0, 0] // BK
    gathered, tables, first, start_blocks = lax.optimization_barrier(
        (gathered, tables, first, start_blocks)
    )

    def product(left, right):
        return jnp.dot(left, right, preferred_element_type=F32).astype(BF16)

    def turned_product(left, right):
        return lax.dot_general(
            left, right, (((1,), (1,)), ((), ())), preferred_element_type=F32
        )

    def token_sum(left, right):
        return lax.dot_general(
            left, right, (((0,), (0,)), ((), ())), preferred_element_type=F32
        ).astype(BF16)

    def scattered(partial):
        return lax.psum_scatter(partial, "mp", scatter_dimension=0, tiled=True)

    gate = turned_product(gathered, w_gate_up[0])
    up = turned_product(gathered, w_gate_up[1])
    sigmoid_gate = jax.nn.sigmoid(gate)
    hidden = (gate * sigmoid_gate * up).astype(BF16)
    mlp_partial = product(hidden, w_down)
    mlp_sum = scattered(mlp_partial)
    gathered_next, mlp_partial = lax.optimization_barrier((gathered, mlp_partial))
    queries, key_rows, value_rows = project(gathered_next, w_qkv, b_qkv, tables)
    attended, lse = attend(first, queries, key_rows, value_rows, start_blocks)
    attn_partial = product(attended, w_out)
    attn_sum = scattered(attn_partial)

    cotangent, attn_partial = lax.optimization_barrier((cotangent, attn_partial))
    grad_hid = turned_product(cotangent, w_down).astype(BF16).astype(F32)
    grad_gate = (
        grad_hid * up * sigmoid_gate * (1.0 + gate * (1.0 - sigmoid_gate))
    ).astype(BF16)
    grad_up = (grad_hid * gate * sigmoid_gate).astype(BF16)
    sum_down = DpSum(token_sum(hidden, cotangent), token_sum(attended, cotangent))
    gathered_next = fence(gathered, sum_down)
    sum_down.send()
    sum_gate_up = DpSum(
        token_sum(grad_gate, gathered_next), token_sum(grad_up, gathered_next), paired=True
    )
    sum_down.arrive()
    cotangent = fence(cotangent, sum_gate_up, sum_down)
    grad_att = turned_product(cotangent, w_out).astype(BF16)
    sum_gate_up.send()
    sum_down.send()
    grad_proj = attend_back(
        first, queries, key_rows, value_rows, grad_att, attended, lse, start_blocks, tables
    )
    sum_gate_up.arrive()
    sum_down.arrive()
    grad_proj, mlp_sum = fence((grad_proj, mlp_sum), sum_gate_up, sum_down)
    sum_gate_up.send()
    sum_down.send()
    normed_partial = back_products(grad_proj, w_qkv, grad_gate, grad_up, w_gate_up)
    sum_gate_up.arrive()
    sum_down.arrive()
    grad_proj, normed_partial = fence((grad_proj, normed_partial), sum_gate_up, sum_down)
    while sum_down.level < 2 * sum_down.count:
        sum_down.send()
        sum_down.arrive()
    sum_qkv = DpSum(fence(token_sum(gathered, grad_proj), sum_down))
    bias_sums = jnp.sum(grad_proj, axis=0, dtype=F32).reshape(-1, 128)
    sum_qkv.send()
    sum_qkv.arrive()
    normed_partial, attn_sum, bias_sums = fence(
        (normed_partial, attn_sum, bias_sums), sum_gate_up, sum_qkv
    )
    grad_normed = scattered(normed_partial)
    sum_gate_up.send()
    sum_qkv.send()
    bias_sums = sum_small(bias_sums, "dp", [0])
    mlp_part = mlp_sum.astype(F32)
    attn_part = attn_sum.astype(F32)
    layer_out = (residual + attn_part + mlp_part).astype(BF16)
    statistics = jnp.stack(
        [
            jnp.sum(valid_here * jnp.sum(residual * residual, -1)),
            jnp.sum(valid_here * jnp.sum(attn_part * attn_part, -1)),
            jnp.sum(valid_here * jnp.sum(mlp_part * mlp_part, -1)),
            jnp.sum(valid_here),
        ]
    )
    stat_row = jnp.pad(statistics, (0, model_width - 4)).reshape(1, model_width)
    sum_gate_up.arrive()
    sum_qkv.arrive()
    bias_sums, layer_out, stat_row = fence(
        (bias_sums, layer_out, stat_row), sum_gate_up, sum_qkv
    )
    sum_gate_up.send()
    sum_qkv.send()
    bias_sums = sum_small(bias_sums, "dp", range(1, sum_qkv.count))
    down_sums = sum_down.result(write_rows)
    sum_gate_up.arrive()
    sum_qkv.arrive()
    down_sums, bias_sums = fence((down_sums, bias_sums), sum_gate_up, sum_qkv)
    for item in (sum_gate_up, sum_qkv):
        while item.level < 2 * item.count:
            item.send()
            item.arrive()
    (grad_w_gate_up,) = sum_gate_up.result(write_stacked)
    grad_normed, grad_w_gate_up = fence((grad_normed, grad_w_gate_up), sum_qkv)
    (grad_w_qkv,) = sum_qkv.result(write_lanes)
    grad_w_down, grad_w_out = down_sums
    input_grad, small = tail(layer_in, grad_normed, cot_here, norm_gain, stat_row)
    small = sum_small(sum_small(small, "mp"), "dp")
    totals = small[2]
    return (
        layer_out[:, None],
        input_grad,
        small[0],
        small[1],
        jnp.transpose(grad_w_qkv, (1, 0, 2)),
        bias_sums.reshape(3, col_qkv),
        grad_w_out,
        jnp.transpose(grad_w_gate_up, (2, 0, 1)),
        grad_w_down,
        jnp.sqrt(totals[:3] / (totals[3] * model_width)),
    )


def solution(mesh):
    placed = (
        P("mp", "dp", None),
        P("dp", None),
        P("dp"),
        P(),
        P(),
        P(None, None, "mp"),
        P(None, "mp"),
        P("mp", None),
        P(None, None, "mp"),
        P("mp", None),
        P("mp", "dp", None),
    )
    return jax.shard_map(
        local,
        mesh=mesh,
        in_specs=placed,
        out_specs=(
            P("mp", "dp", None),
            P("mp", "dp", None),
            P(),
            P(),
            P(None, None, "mp"),
            P(None, "mp"),
            P("mp", None),
            P(None, None, "mp"),
            P("mp", None),
            P(),
        ),
        check_vma=False,
    )
```

```python
import functools

import jax
import jax.numpy as jnp
from jax import lax
from jax.experimental import pallas as pl
from jax.experimental.pallas import tpu as pltpu
from jax.sharding import PartitionSpec as P

HEAD_DIM = 64
ROT = 16
EPSILON = 1e-05
BQ = 128
BK = 256
NEG = -1e30
F32 = jnp.float32
BF16 = jnp.bfloat16


def starts_of(segment_ids):
    length = segment_ids.shape[1]
    steps_all = jnp.arange(length, dtype=jnp.int32)[None, :]
    change = jnp.concatenate(
        [
            jnp.ones_like(segment_ids[:, :1]),
            (segment_ids[:, 1:] != segment_ids[:, :-1]).astype(jnp.int32),
        ],
        axis=1,
    )
    return lax.cummax(jnp.where(change > 0, steps_all, jnp.zeros_like(change)), axis=1)


def rotary_lanes(positions):
    half_rot = ROT // 2
    lane = jnp.arange(2 * HEAD_DIM, dtype=jnp.int32) % HEAD_DIM
    power = (lane % half_rot).astype(F32)
    frequency = jnp.where(lane < ROT, 10000.0 ** (-(power * 2.0) / ROT), 0.0)
    angles = positions.astype(F32)[:, None] * frequency
    sine = jnp.sin(angles)
    low = jnp.where(lane < half_rot, -sine, 0.0)
    high = jnp.where((lane >= half_rot) & (lane < ROT), sine, 0.0)
    return jnp.cos(angles), low, high


def lane_tile(table, columns):
    return jnp.concatenate([table] * (columns // table.shape[1]), axis=1)


def turn(values, cosine, low, high):
    columns = values.shape[1]
    half_rot = ROT // 2
    return (
        values * lane_tile(cosine, columns)
        + pltpu.roll(values, columns - half_rot, 1) * lane_tile(low, columns)
        + pltpu.roll(values, half_rot, 1) * lane_tile(high, columns)
    )


def project_kernel(x_ref, w_ref, b_ref, cos_ref, low_ref, high_ref, q_ref, k_ref, v_ref):
    tables = (cos_ref[...], low_ref[...], high_ref[...])

    def part(number):
        flat = jnp.dot(x_ref[...], w_ref[number], preferred_element_type=F32)
        return flat + b_ref[number : number + 1, :].astype(F32)

    queries = turn(part(0), *tables).astype(BF16)
    q_ref[...] = (queries.astype(F32) * HEAD_DIM**-0.5).astype(BF16)
    k_ref[...] = turn(part(1), *tables).astype(BF16)
    v_ref[...] = part(2).astype(BF16)


def project(gathered, w_qkv, b_qkv, tables):
    length, width = gathered.shape
    columns = w_qkv.shape[2]
    rows = min(256, length)
    table_spec = pl.BlockSpec((rows, tables[0].shape[1]), lambda i: (i, 0))
    out_spec = pl.BlockSpec((rows, columns), lambda i: (i, 0))
    return pl.pallas_call(
        project_kernel,
        grid=(length // rows,),
        in_specs=[
            pl.BlockSpec((rows, width), lambda i: (i, 0)),
            pl.BlockSpec(w_qkv.shape, lambda i: (0, 0, 0)),
            pl.BlockSpec(b_qkv.shape, lambda i: (0, 0)),
            table_spec,
            table_spec,
            table_spec,
        ],
        out_specs=[out_spec] * 3,
        out_shape=[jax.ShapeDtypeStruct((length, columns), BF16)] * 3,
        cost_estimate=pl.CostEstimate(
            flops=6 * length * width * columns,
            bytes_accessed=2 * (length * width + 3 * width * columns + 3 * length * columns),
            transcendentals=0,
        ),
        name="project",
    )(gathered, w_qkv, b_qkv, *tables)


def stack_heads(block):
    columns = block.shape[1]
    head_of = lax.broadcasted_iota(jnp.int32, block.shape, 1) // HEAD_DIM
    return jnp.concatenate(
        [
            jnp.where(head_of == head, block, jnp.zeros_like(block))
            for head in range(columns // HEAD_DIM)
        ],
        axis=0,
    )


def unstack_heads(stacked, block):
    heads = stacked.shape[1] // block
    return jnp.concatenate(
        [
            stacked[head * HEAD_DIM : (head + 1) * HEAD_DIM, head * block : (head + 1) * block]
            for head in range(heads)
        ],
        axis=0,
    ).T


def score_block(key_block, stacked_queries, key_at, start_row, query_row):
    scores = lax.dot_general(
        key_block, stacked_queries, (((1,), (1,)), ((), ())), preferred_element_type=F32
    )
    key_pos = key_at + lax.broadcasted_iota(jnp.int32, scores.shape, 0)
    allowed = (key_pos >= start_row) & (key_pos <= query_row)
    return scores, allowed


def query_rows(start_ref, block, heads):
    start_row = jnp.concatenate([start_ref[0]] * heads, axis=1)
    query_row = pl.program_id(0) * block + lax.broadcasted_iota(jnp.int32, (1, block), 1)
    return start_row, jnp.concatenate([query_row] * heads, axis=1)


def attend_kernel(first_ref, q_ref, k_ref, v_ref, start_ref, o_ref, lse_ref, acc_ref):
    block, columns = q_ref.shape
    heads = columns // HEAD_DIM
    index = pl.program_id(0)
    stacked = stack_heads(q_ref[...])
    start_row, query_row = query_rows(start_ref, block, heads)
    acc_ref[...] = jnp.zeros_like(acc_ref)

    def body(step, carry):
        highest, total = carry
        at = pl.multiple_of(step * BK, BK)
        scores, allowed = score_block(
            k_ref[pl.ds(at, BK), :], stacked, at, start_row, query_row
        )
        scores = jnp.where(allowed, scores, NEG)
        newest = jnp.maximum(highest, jnp.max(scores, axis=0, keepdims=True))
        weights = jnp.exp(scores - newest)
        scale = jnp.exp(highest - newest)
        total = total * scale + jnp.sum(weights, axis=0, keepdims=True)
        acc_ref[...] = acc_ref[...] * scale + lax.dot_general(
            v_ref[pl.ds(at, BK), :],
            weights.astype(BF16),
            (((0,), (0,)), ((), ())),
            preferred_element_type=F32,
        )
        return newest, total

    highest, total = lax.fori_loop(
        first_ref[index],
        (index * block + block - 1) // BK + 1,
        body,
        (jnp.full((1, heads * block), NEG, F32), jnp.zeros((1, heads * block), F32)),
    )
    o_ref[...] = unstack_heads(acc_ref[...] / total, block).astype(BF16)
    lse_ref[0] = highest + jnp.log(total)


def attend(first, queries, key_rows, value_rows, start_blocks):
    length, columns = queries.shape
    blocks = length // BQ
    heads = columns // HEAD_DIM
    row_spec = pl.BlockSpec((BQ, columns), lambda i, f: (i, 0))
    whole = pl.BlockSpec((length, columns), lambda i, f: (0, 0))
    return pl.pallas_call(
        attend_kernel,
        grid_spec=pltpu.PrefetchScalarGridSpec(
            num_scalar_prefetch=1,
            grid=(blocks,),
            in_specs=[
                row_spec,
                whole,
                whole,
                pl.BlockSpec((1, 1, BQ), lambda i, f: (i, 0, 0)),
            ],
            out_specs=[
                row_spec,
                pl.BlockSpec((1, 1, heads * BQ), lambda i, f: (i, 0, 0)),
            ],
            scratch_shapes=[pltpu.VMEM((columns, heads * BQ), F32)],
        ),
        out_shape=[
            jax.ShapeDtypeStruct((length, columns), BF16),
            jax.ShapeDtypeStruct((blocks, 1, heads * BQ), F32),
        ],
        cost_estimate=pl.CostEstimate(
            flops=4 * length * 1024 * columns * heads,
            bytes_accessed=8 * length * columns,
            transcendentals=length * 1024 * heads,
        ),
        name="attend",
    )(first, queries, key_rows, value_rows, start_blocks)


def attend_back_kernel(
    first_ref,
    q_ref,
    k_ref,
    v_ref,
    do_ref,
    o_ref,
    lse_ref,
    start_ref,
    cos_ref,
    low_ref,
    high_ref,
    grad_ref,
    key_acc,
    value_acc,
    query_acc,
):
    block, columns = q_ref.shape
    heads = columns // HEAD_DIM
    length = k_ref.shape[0]
    index = pl.program_id(0)

    @pl.when(index == 0)
    def _():
        key_acc[...] = jnp.zeros_like(key_acc)
        value_acc[...] = jnp.zeros_like(value_acc)

    stacked = stack_heads(q_ref[...])
    stacked_do = stack_heads(do_ref[...])
    start_row, query_row = query_rows(start_ref, block, heads)
    lse_row = lse_ref[0]
    products = do_ref[...].astype(F32) * o_ref[...].astype(F32)
    head_rows = lax.broadcasted_iota(jnp.int32, (8, columns), 0)
    head_lanes = lax.broadcasted_iota(jnp.int32, (8, columns), 1) // HEAD_DIM
    picked = lax.dot_general(
        (head_rows == head_lanes).astype(F32),
        products,
        (((1,), (1,)), ((), ())),
        precision=lax.Precision.HIGHEST,
        preferred_element_type=F32,
    )
    inner_row = jnp.concatenate([picked[head : head + 1, :] for head in range(heads)], axis=1)
    query_acc[...] = jnp.zeros_like(query_acc)

    def body(step, carry):
        at = pl.multiple_of(step * BK, BK)
        key_block = k_ref[pl.ds(at, BK), :]
        scores, allowed = score_block(key_block, stacked, at, start_row, query_row)
        weights = jnp.where(allowed, jnp.exp(scores - lse_row), 0.0)
        grad_weights = lax.dot_general(
            v_ref[pl.ds(at, BK), :],
            stacked_do,
            (((1,), (1,)), ((), ())),
            preferred_element_type=F32,
        )
        grad_scores = (weights * (grad_weights - inner_row)).astype(BF16)
        value_acc[pl.ds(at, BK), :] += jnp.dot(
            weights.astype(BF16), stacked_do, preferred_element_type=F32
        )
        key_acc[pl.ds(at, BK), :] += jnp.dot(grad_scores, stacked, preferred_element_type=F32)
        query_acc[...] += lax.dot_general(
            key_block, grad_scores, (((0,), (0,)), ((), ())), preferred_element_type=F32
        )
        return carry

    lax.fori_loop(first_ref[index], (index * block + block - 1) // BK + 1, body, 0)

    def turn_back(grads, at, rows):
        kept = grads.astype(BF16).astype(F32)
        return turn(
            kept,
            cos_ref[pl.ds(at, rows), :],
            -low_ref[pl.ds(at, rows), :],
            -high_ref[pl.ds(at, rows), :],
        ).astype(BF16)

    at_query = pl.multiple_of(index * block, block)
    grad_ref[pl.ds(at_query, block), :columns] = turn_back(
        unstack_heads(query_acc[...], block) * HEAD_DIM**-0.5, at_query, block
    )

    @pl.when(index == pl.num_programs(0) - 1)
    def _():
        def finish(step, carry):
            at = pl.multiple_of(step * BK, BK)
            grad_ref[pl.ds(at, BK), columns : 2 * columns] = turn_back(
                key_acc[pl.ds(at, BK), :], at, BK
            )
            grad_ref[pl.ds(at, BK), 2 * columns :] = value_acc[pl.ds(at, BK), :].astype(BF16)
            return carry

        lax.fori_loop(0, length // BK, finish, 0)


def attend_back(first, queries, key_rows, value_rows, grad_att, attended, lse, start_blocks, tables):
    length, columns = queries.shape
    blocks = length // BQ
    heads = columns // HEAD_DIM
    row_spec = pl.BlockSpec((BQ, columns), lambda i, f: (i, 0))
    whole = pl.BlockSpec((length, columns), lambda i, f: (0, 0))
    table_spec = pl.BlockSpec(tables[0].shape, lambda i, f: (0, 0))
    return pl.pallas_call(
        attend_back_kernel,
        grid_spec=pltpu.PrefetchScalarGridSpec(
            num_scalar_prefetch=1,
            grid=(blocks,),
            in_specs=[
                row_spec,
                whole,
                whole,
                row_spec,
                row_spec,
                pl.BlockSpec((1, 1, heads * BQ), lambda i, f: (i, 0, 0)),
                pl.BlockSpec((1, 1, BQ), lambda i, f: (i, 0, 0)),
                table_spec,
                table_spec,
                table_spec,
            ],
            out_specs=pl.BlockSpec((length, 3 * columns), lambda i, f: (0, 0)),
            scratch_shapes=[
                pltpu.VMEM((length, columns), F32),
                pltpu.VMEM((length, columns), F32),
                pltpu.VMEM((columns, heads * BQ), F32),
            ],
        ),
        out_shape=jax.ShapeDtypeStruct((length, 3 * columns), BF16),
        cost_estimate=pl.CostEstimate(
            flops=10 * length * 1024 * columns * heads,
            bytes_accessed=16 * length * columns,
            transcendentals=length * 1024 * heads,
        ),
        name="attend_back",
    )(first, queries, key_rows, value_rows, grad_att, attended, lse, start_blocks, *tables)


def bits_of(name):
    size = lax.axis_size(name)
    count = size.bit_length() - 1
    return count if size == 1 << count else None


def swap(values, name, bit):
    size = lax.axis_size(name)
    return lax.ppermute(values, name, [(i, i ^ (1 << bit)) for i in range(size)])


def write_stacked(piece, outs):
    outs[0][0] = piece.astype(F32)


def write_rows(piece, outs):
    at = 0
    for out_ref in outs:
        size = out_ref.shape[0]
        out_ref[...] = piece[at : at + size, :].astype(F32)
        at += size


def write_lanes(piece, outs):
    parts, _, size = outs[0].shape
    for part in range(parts):
        outs[0][part] = piece[:, part * size : (part + 1) * size].astype(F32)


def place_kernel(write, count, color_ref, where_ref, *refs):
    step = pl.program_id(0)
    for number in range(count):

        @pl.when(step == number)
        def _(number=number):
            write(refs[number][...], refs[count:])


def place_blocks(write, color, where, pieces, out_shapes, out_specs):
    rows, columns = pieces[0].shape
    count = len(pieces)
    return pl.pallas_call(
        functools.partial(place_kernel, write, count),
        grid_spec=pltpu.PrefetchScalarGridSpec(
            num_scalar_prefetch=2,
            grid=(count,),
            in_specs=[pl.BlockSpec((rows, columns), lambda i, c, w: (0, 0))] * count,
            out_specs=out_specs,
        ),
        out_shape=[jax.ShapeDtypeStruct(shape, F32) for shape in out_shapes],
        cost_estimate=pl.CostEstimate(
            flops=0, bytes_accessed=6 * count * rows * columns, transcendentals=0
        ),
        name="place_blocks",
    )(color, where, *pieces)


class DpSum:
    def __init__(self, *grads, paired=False):
        self.grads = grads
        self.paired = paired
        self.count = bits_of("dp")
        pieces = (1 if paired else 2) << self.count
        self.axis = 0 if all(g.shape[0] % (8 * pieces) == 0 for g in grads) else 1
        self.sizes = [g.shape[self.axis] // pieces for g in grads]
        self.mine = lax.axis_index("dp")
        self.orders = [list(range(self.count)), list(range(self.count))[::-1]]
        self.level = 0
        if paired:
            self.state = [((grad,), self.sizes[:1], 0) for grad in grads]
        else:
            self.state = [(grads, self.sizes, color << self.count) for color in range(2)]
        self.held = None
        self.ready()

    def cut(self, color, side):
        grads, units, base = self.state[color]
        span = (1 << self.count) >> (self.level + 1)
        parts = []
        for grad, unit in zip(grads, units):
            at = (base + side * span) * unit
            parts.append(lax.dynamic_slice_in_dim(grad, at, span * unit, self.axis))
        if len(parts) == 1:
            return parts[0]
        if self.axis:
            return jnp.concatenate(parts, axis=0)
        parts = [p.reshape(span, unit, p.shape[1]) for p, unit in zip(parts, units)]
        joined = jnp.concatenate(parts, axis=1)
        return joined.reshape(-1, joined.shape[2])

    def side(self, color):
        return (self.mine >> self.orders[color][self.level]) & 1

    def ready(self):
        if self.level < self.count:
            self.out = [self.cut(color, 1 - self.side(color)) for color in range(2)]
        elif self.held is None:
            self.held = [[(self.state[color][0][0], 0)] for color in range(2)]

    def send(self):
        if self.level < self.count:
            self.got = [
                swap(self.out[color], "dp", self.orders[color][self.level])
                for color in range(2)
            ]
            return
        for color in range(2):
            bit = self.orders[color][2 * self.count - 1 - self.level]
            self.held[color] += [
                (swap(piece, "dp", bit), mask ^ (1 << bit)) for piece, mask in self.held[color]
            ]

    def arrive(self):
        if self.level < self.count:
            state = []
            for color in range(2):
                keep = self.cut(color, self.side(color))
                total = (keep.astype(F32) + self.got[color].astype(F32)).astype(BF16)
                whole = self.axis == 0 and not self.paired
                state.append(((total,), [sum(self.sizes) if whole else self.sizes[0]], 0))
            self.state = state
        self.level += 1
        self.ready()

    def moving(self):
        return self.out if self.held is None else self.held

    def result(self, write):
        pieces, colors, where = [], [], []
        for color in range(2):
            for piece, mask in self.held[color]:
                owner = self.mine ^ mask
                spot = 0 if self.paired else color
                for bit in self.orders[color]:
                    spot = spot * 2 + ((owner >> bit) & 1)
                pieces.append(piece)
                colors.append(color)
                where.append(spot)
        rows, columns = pieces[0].shape
        length, width = self.grads[0].shape
        if write is write_stacked:
            shapes = [(2, length, width)]
            blocks = [(1, rows, columns)]
        elif write is write_lanes:
            shapes = [(3, length, width // 3)]
            blocks = [(3, rows, columns // 3)]
        else:
            shapes = [g.shape for g in self.grads]
            blocks = [(rows * s[0] // sum(t[0] for t in shapes), columns) for s in shapes]
        lead = {write_stacked: lambda i, c: (c[i],), write_lanes: lambda i, c: (0,)}.get(
            write, lambda i, c: ()
        )

        def out_map(i, c, w):
            return lead(i, c) + ((w[i], 0) if self.axis == 0 else (0, w[i]))

        return place_blocks(
            write,
            jnp.array(colors, jnp.int32),
            jnp.stack(where).astype(jnp.int32),
            pieces,
            shapes,
            [pl.BlockSpec(block, out_map) for block in blocks],
        )


def fence(values, *sums):
    values, moving = lax.optimization_barrier((values, [item.moving() for item in sums]))
    for item, arrived in zip(sums, moving):
        if item.held is None:
            item.out = arrived
        else:
            item.held = arrived
    return values


def sum_small(values, name, bits=None):
    count = bits_of(name)
    if count is None:
        return lax.psum(values, name) if bits is None or 0 in bits else values
    for bit in range(count) if bits is None else bits:
        values = values + swap(values, name, bit)
    return values


def tail_kernel(x_ref, g_ref, c_ref, gain_ref, stat_ref, grad_ref, sums_ref):
    @pl.when(pl.program_id(0) == 0)
    def _():
        sums_ref[...] = jnp.zeros_like(sums_ref)
        sums_ref[2:3, :] = stat_ref[...]

    residual = x_ref[...].astype(F32)
    centered = residual - jnp.mean(residual, -1, keepdims=True)
    inv_std = lax.rsqrt(jnp.mean(centered * centered, -1, keepdims=True) + EPSILON)
    normalized = centered * inv_std
    grads = g_ref[...].astype(F32)
    sums_ref[0:1, :] += jnp.sum(grads * normalized, axis=0, keepdims=True)
    sums_ref[1:2, :] += jnp.sum(grads, axis=0, keepdims=True)
    scaled = grads * gain_ref[...]
    grad_ref[:, 0, :] = (
        inv_std
        * (
            scaled
            - jnp.mean(scaled, -1, keepdims=True)
            - normalized * jnp.mean(scaled * normalized, -1, keepdims=True)
        )
        + c_ref[...].astype(F32)
    )


def tail(layer_in, grad_normed, cot_here, norm_gain, stat_row):
    length, width = layer_in.shape
    rows = min(64, length)
    row_spec = pl.BlockSpec((rows, width), lambda i: (i, 0))
    one_spec = pl.BlockSpec((1, width), lambda i: (0, 0))
    return pl.pallas_call(
        tail_kernel,
        grid=(length // rows,),
        in_specs=[row_spec, row_spec, row_spec, one_spec, one_spec],
        out_specs=[
            pl.BlockSpec((rows, 1, width), lambda i: (i, 0, 0)),
            pl.BlockSpec((4, width), lambda i: (0, 0)),
        ],
        out_shape=[
            jax.ShapeDtypeStruct((length, 1, width), F32),
            jax.ShapeDtypeStruct((4, width), F32),
        ],
        name="tail",
    )(layer_in, grad_normed, cot_here, norm_gain.reshape(1, width), stat_row)


def back_products_kernel(p_ref, q_ref, g_ref, u_ref, w_ref, out_ref):
    turned = (((1,), (1,)), ((), ()))
    columns = q_ref.shape[2]
    total = jnp.dot(g_ref[...], w_ref[0], preferred_element_type=F32)
    total += jnp.dot(u_ref[...], w_ref[1], preferred_element_type=F32)
    for number in range(3):
        total += lax.dot_general(
            p_ref[:, number * columns : (number + 1) * columns],
            q_ref[number],
            turned,
            preferred_element_type=F32,
        )
    out_ref[...] = total.astype(BF16)


def back_products(grad_proj, w_qkv, grad_gate, grad_up, w_gate_up):
    length = grad_proj.shape[0]
    _, width, columns = w_qkv.shape
    hidden = grad_gate.shape[1]
    rows = min(256, length)
    return pl.pallas_call(
        back_products_kernel,
        grid=(length // rows,),
        in_specs=[
            pl.BlockSpec((rows, 3 * columns), lambda i: (i, 0)),
            pl.BlockSpec(w_qkv.shape, lambda i: (0, 0, 0)),
            pl.BlockSpec((rows, hidden), lambda i: (i, 0)),
            pl.BlockSpec((rows, hidden), lambda i: (i, 0)),
            pl.BlockSpec(w_gate_up.shape, lambda i: (0, 0, 0)),
        ],
        out_specs=pl.BlockSpec((rows, width), lambda i: (i, 0)),
        out_shape=jax.ShapeDtypeStruct((length, width), BF16),
        name="back_products",
    )(grad_proj, w_qkv, grad_gate, grad_up, w_gate_up)


def local(
    layer_in,
    segment_ids,
    valid_counts,
    norm_gain,
    norm_shift,
    w_qkv,
    b_qkv,
    w_out,
    w_gate_up,
    w_down,
    out_grad,
):
    local_len, row_count, model_width = layer_in.shape
    assert row_count == 1
    seq_len = local_len * lax.axis_size("mp")
    col_qkv = w_qkv.shape[2]
    ff_local = w_gate_up.shape[2]
    layer_in = layer_in[:, 0]
    position_here = lax.axis_index("mp") * local_len + jnp.arange(local_len, dtype=jnp.int32)
    valid_here = (position_here < valid_counts[0]).astype(F32)

    residual = layer_in.astype(F32)
    centered = residual - jnp.mean(residual, -1, keepdims=True)
    inv_std = lax.rsqrt(jnp.mean(centered * centered, -1, keepdims=True) + EPSILON)
    normalized = centered * inv_std
    normed = (normalized * norm_gain + norm_shift).astype(BF16)
    cot_here = jnp.where(valid_here[:, None] > 0, out_grad[:, 0], jnp.zeros((), BF16))
    gathered = lax.all_gather(normed, "mp", axis=0, tiled=True)
    cotangent = lax.all_gather(cot_here, "mp", axis=0, tiled=True)

    w_qkv = jnp.transpose(w_qkv, (1, 0, 2))
    w_gate_up = jnp.transpose(w_gate_up, (1, 2, 0))
    starts = starts_of(segment_ids)[0]
    tables = rotary_lanes(jnp.arange(seq_len, dtype=jnp.int32) - starts)
    start_blocks = starts.reshape(seq_len // BQ, 1, BQ)
    first = start_blocks[:, 0, 0] // BK
    gathered, tables, first, start_blocks = lax.optimization_barrier(
        (gathered, tables, first, start_blocks)
    )

    def product(left, right):
        return jnp.dot(left, right, preferred_element_type=F32).astype(BF16)

    def turned_product(left, right):
        return lax.dot_general(
            left, right, (((1,), (1,)), ((), ())), preferred_element_type=F32
        )

    def token_sum(left, right):
        return lax.dot_general(
            left, right, (((0,), (0,)), ((), ())), preferred_element_type=F32
        ).astype(BF16)

    def scattered(partial):
        return lax.psum_scatter(partial, "mp", scatter_dimension=0, tiled=True)

    gate = turned_product(gathered, w_gate_up[0])
    up = turned_product(gathered, w_gate_up[1])
    sigmoid_gate = jax.nn.sigmoid(gate)
    hidden = (gate * sigmoid_gate * up).astype(BF16)
    mlp_partial = product(hidden, w_down)
    mlp_sum = scattered(mlp_partial)
    gathered_next, mlp_partial = lax.optimization_barrier((gathered, mlp_partial))
    queries, key_rows, value_rows = project(gathered_next, w_qkv, b_qkv, tables)
    attended, lse = attend(first, queries, key_rows, value_rows, start_blocks)
    attn_partial = product(attended, w_out)
    attn_sum = scattered(attn_partial)

    cotangent, attn_partial = lax.optimization_barrier((cotangent, attn_partial))
    sum_down = DpSum(token_sum(hidden, cotangent), token_sum(attended, cotangent))
    cotangent = fence(cotangent, sum_down)
    sum_down.send()
    grad_hid = turned_product(cotangent, w_down).astype(BF16).astype(F32)
    grad_gate = (
        grad_hid * up * sigmoid_gate * (1.0 + gate * (1.0 - sigmoid_gate))
    ).astype(BF16)
    grad_up = (grad_hid * gate * sigmoid_gate).astype(BF16)
    sum_gate = token_sum(grad_gate, gathered)
    sum_down.arrive()
    sum_gate, grad_up = fence((sum_gate, grad_up), sum_down)
    sum_down.send()
    sum_gate_up = DpSum(sum_gate, token_sum(grad_up, gathered), paired=True)
    sum_down.arrive()
    cotangent = fence(cotangent, sum_gate_up, sum_down)
    grad_att = turned_product(cotangent, w_out).astype(BF16)
    sum_gate_up.send()
    sum_down.send()
    grad_proj = attend_back(
        first, queries, key_rows, value_rows, grad_att, attended, lse, start_blocks, tables
    )
    sum_gate_up.arrive()
    sum_down.arrive()
    grad_proj, mlp_sum = fence((grad_proj, mlp_sum), sum_gate_up, sum_down)
    sum_gate_up.send()
    sum_down.send()
    fresh = [held[len(held) // 2][0] for held in sum_down.held]
    normed_partial = back_products(grad_proj, w_qkv, grad_gate, grad_up, w_gate_up)
    sum_gate_up.arrive()
    sum_down.arrive()
    grad_proj, normed_partial, _ = fence((grad_proj, normed_partial, fresh), sum_gate_up)
    while sum_down.level < 2 * sum_down.count:
        sum_down.send()
        sum_down.arrive()
    sum_qkv = DpSum(fence(token_sum(gathered, grad_proj), sum_down))
    bias_sums = jnp.sum(grad_proj, axis=0, dtype=F32).reshape(-1, 128)
    sum_qkv.send()
    sum_gate_up.send()
    sum_qkv.arrive()
    sum_gate_up.arrive()
    normed_partial, attn_sum, bias_sums = fence(
        (normed_partial, attn_sum, bias_sums), sum_gate_up, sum_qkv
    )
    grad_normed = scattered(normed_partial)
    sum_gate_up.send()
    sum_qkv.send()
    bias_sums = sum_small(bias_sums, "dp", [0])
    mlp_part = mlp_sum.astype(F32)
    attn_part = attn_sum.astype(F32)
    layer_out = (residual + attn_part + mlp_part).astype(BF16)
    statistics = jnp.stack(
        [
            jnp.sum(valid_here * jnp.sum(residual * residual, -1)),
            jnp.sum(valid_here * jnp.sum(attn_part * attn_part, -1)),
            jnp.sum(valid_here * jnp.sum(mlp_part * mlp_part, -1)),
            jnp.sum(valid_here),
        ]
    )
    stat_row = jnp.pad(statistics, (0, model_width - 4)).reshape(1, model_width)
    sum_gate_up.arrive()
    sum_qkv.arrive()
    bias_sums, layer_out, stat_row = fence(
        (bias_sums, layer_out, stat_row), sum_gate_up, sum_qkv
    )
    sum_qkv.send()
    bias_sums = sum_small(bias_sums, "dp", range(1, sum_qkv.count))
    down_sums = sum_down.result(write_rows)
    sum_qkv.arrive()
    down_sums, bias_sums = fence((down_sums, bias_sums), sum_qkv)
    for item in (sum_gate_up, sum_qkv):
        while item.level < 2 * item.count:
            item.send()
            item.arrive()
    (grad_w_gate_up,) = sum_gate_up.result(write_stacked)
    grad_w_gate_up = fence(grad_w_gate_up, sum_qkv)
    (grad_w_qkv,) = sum_qkv.result(write_lanes)
    grad_w_down, grad_w_out = down_sums
    grad_normed, grad_w_gate_up, grad_w_qkv = fence(
        (grad_normed, grad_w_gate_up, grad_w_qkv)
    )
    input_grad, small = tail(layer_in, grad_normed, cot_here, norm_gain, stat_row)
    small = sum_small(sum_small(small, "mp"), "dp")
    totals = small[2]
    return (
        layer_out[:, None],
        input_grad,
        small[0],
        small[1],
        jnp.transpose(grad_w_qkv, (1, 0, 2)),
        bias_sums.reshape(3, col_qkv),
        grad_w_out,
        jnp.transpose(grad_w_gate_up, (2, 0, 1)),
        grad_w_down,
        jnp.sqrt(totals[:3] / (totals[3] * model_width)),
    )


def solution(mesh):
    placed = (
        P("mp", "dp", None),
        P("dp", None),
        P("dp"),
        P(),
        P(),
        P(None, None, "mp"),
        P(None, "mp"),
        P("mp", None),
        P(None, None, "mp"),
        P("mp", None),
        P("mp", "dp", None),
    )
    return jax.shard_map(
        local,
        mesh=mesh,
        in_specs=placed,
        out_specs=(
            P("mp", "dp", None),
            P("mp", "dp", None),
            P(),
            P(),
            P(None, None, "mp"),
            P(None, "mp"),
            P("mp", None),
            P(None, None, "mp"),
            P("mp", None),
            P(),
        ),
        check_vma=False,
    )
```

```python
import functools

import jax
import jax.numpy as jnp
from jax import lax
from jax.experimental import pallas as pl
from jax.experimental.pallas import tpu as pltpu
from jax.sharding import PartitionSpec as P

HEAD_DIM = 64
ROT = 16
EPSILON = 1e-05
BQ = 128
BK = 256
NEG = -1e30
F32 = jnp.float32
BF16 = jnp.bfloat16


def starts_of(segment_ids):
    length = segment_ids.shape[1]
    steps_all = jnp.arange(length, dtype=jnp.int32)[None, :]
    change = jnp.concatenate(
        [
            jnp.ones_like(segment_ids[:, :1]),
            (segment_ids[:, 1:] != segment_ids[:, :-1]).astype(jnp.int32),
        ],
        axis=1,
    )
    return lax.cummax(jnp.where(change > 0, steps_all, jnp.zeros_like(change)), axis=1)


def rotary_lanes(positions):
    half_rot = ROT // 2
    lane = jnp.arange(2 * HEAD_DIM, dtype=jnp.int32) % HEAD_DIM
    power = (lane % half_rot).astype(F32)
    frequency = jnp.where(lane < ROT, 10000.0 ** (-(power * 2.0) / ROT), 0.0)
    angles = positions.astype(F32)[:, None] * frequency
    sine = jnp.sin(angles)
    low = jnp.where(lane < half_rot, -sine, 0.0)
    high = jnp.where((lane >= half_rot) & (lane < ROT), sine, 0.0)
    return jnp.cos(angles), low, high


def lane_tile(table, columns):
    return jnp.concatenate([table] * (columns // table.shape[1]), axis=1)


def turn(values, cosine, low, high):
    columns = values.shape[1]
    half_rot = ROT // 2
    return (
        values * lane_tile(cosine, columns)
        + pltpu.roll(values, columns - half_rot, 1) * lane_tile(low, columns)
        + pltpu.roll(values, half_rot, 1) * lane_tile(high, columns)
    )


def project_kernel(x_ref, w_ref, b_ref, cos_ref, low_ref, high_ref, q_ref, k_ref, v_ref):
    tables = (cos_ref[...], low_ref[...], high_ref[...])

    def part(number):
        flat = jnp.dot(x_ref[...], w_ref[number], preferred_element_type=F32)
        return flat + b_ref[number : number + 1, :].astype(F32)

    queries = turn(part(0), *tables).astype(BF16)
    q_ref[...] = (queries.astype(F32) * HEAD_DIM**-0.5).astype(BF16)
    k_ref[...] = turn(part(1), *tables).astype(BF16)
    v_ref[...] = part(2).astype(BF16)


def project(gathered, w_qkv, b_qkv, tables):
    length, width = gathered.shape
    columns = w_qkv.shape[2]
    rows = min(256, length)
    table_spec = pl.BlockSpec((rows, tables[0].shape[1]), lambda i: (i, 0))
    out_spec = pl.BlockSpec((rows, columns), lambda i: (i, 0))
    return pl.pallas_call(
        project_kernel,
        grid=(length // rows,),
        in_specs=[
            pl.BlockSpec((rows, width), lambda i: (i, 0)),
            pl.BlockSpec(w_qkv.shape, lambda i: (0, 0, 0)),
            pl.BlockSpec(b_qkv.shape, lambda i: (0, 0)),
            table_spec,
            table_spec,
            table_spec,
        ],
        out_specs=[out_spec] * 3,
        out_shape=[jax.ShapeDtypeStruct((length, columns), BF16)] * 3,
        cost_estimate=pl.CostEstimate(
            flops=6 * length * width * columns,
            bytes_accessed=2 * (length * width + 3 * width * columns + 3 * length * columns),
            transcendentals=0,
        ),
        name="project",
    )(gathered, w_qkv, b_qkv, *tables)


def stack_heads(block):
    columns = block.shape[1]
    head_of = lax.broadcasted_iota(jnp.int32, block.shape, 1) // HEAD_DIM
    return jnp.concatenate(
        [
            jnp.where(head_of == head, block, jnp.zeros_like(block))
            for head in range(columns // HEAD_DIM)
        ],
        axis=0,
    )


def unstack_heads(stacked, block):
    heads = stacked.shape[1] // block
    return jnp.concatenate(
        [
            stacked[head * HEAD_DIM : (head + 1) * HEAD_DIM, head * block : (head + 1) * block]
            for head in range(heads)
        ],
        axis=0,
    ).T


def score_block(key_block, stacked_queries, key_at, start_row, query_row):
    scores = lax.dot_general(
        key_block, stacked_queries, (((1,), (1,)), ((), ())), preferred_element_type=F32
    )
    key_pos = key_at + lax.broadcasted_iota(jnp.int32, scores.shape, 0)
    allowed = (key_pos >= start_row) & (key_pos <= query_row)
    return scores, allowed


def query_rows(start_ref, block, heads):
    start_row = jnp.concatenate([start_ref[0]] * heads, axis=1)
    query_row = pl.program_id(0) * block + lax.broadcasted_iota(jnp.int32, (1, block), 1)
    return start_row, jnp.concatenate([query_row] * heads, axis=1)


def attend_kernel(first_ref, q_ref, k_ref, v_ref, start_ref, o_ref, lse_ref, acc_ref):
    block, columns = q_ref.shape
    heads = columns // HEAD_DIM
    index = pl.program_id(0)
    stacked = stack_heads(q_ref[...])
    start_row, query_row = query_rows(start_ref, block, heads)
    acc_ref[...] = jnp.zeros_like(acc_ref)

    def body(step, carry):
        highest, total = carry
        at = pl.multiple_of(step * BK, BK)
        scores, allowed = score_block(
            k_ref[pl.ds(at, BK), :], stacked, at, start_row, query_row
        )
        scores = jnp.where(allowed, scores, NEG)
        newest = jnp.maximum(highest, jnp.max(scores, axis=0, keepdims=True))
        weights = jnp.exp(scores - newest)
        scale = jnp.exp(highest - newest)
        total = total * scale + jnp.sum(weights, axis=0, keepdims=True)
        acc_ref[...] = acc_ref[...] * scale + lax.dot_general(
            v_ref[pl.ds(at, BK), :],
            weights.astype(BF16),
            (((0,), (0,)), ((), ())),
            preferred_element_type=F32,
        )
        return newest, total

    highest, total = lax.fori_loop(
        first_ref[index],
        (index * block + block - 1) // BK + 1,
        body,
        (jnp.full((1, heads * block), NEG, F32), jnp.zeros((1, heads * block), F32)),
    )
    o_ref[...] = unstack_heads(acc_ref[...] / total, block).astype(BF16)
    lse_ref[0] = highest + jnp.log(total)


def attend(first, queries, key_rows, value_rows, start_blocks):
    length, columns = queries.shape
    blocks = length // BQ
    heads = columns // HEAD_DIM
    row_spec = pl.BlockSpec((BQ, columns), lambda i, f: (i, 0))
    whole = pl.BlockSpec((length, columns), lambda i, f: (0, 0))
    return pl.pallas_call(
        attend_kernel,
        grid_spec=pltpu.PrefetchScalarGridSpec(
            num_scalar_prefetch=1,
            grid=(blocks,),
            in_specs=[
                row_spec,
                whole,
                whole,
                pl.BlockSpec((1, 1, BQ), lambda i, f: (i, 0, 0)),
            ],
            out_specs=[
                row_spec,
                pl.BlockSpec((1, 1, heads * BQ), lambda i, f: (i, 0, 0)),
            ],
            scratch_shapes=[pltpu.VMEM((columns, heads * BQ), F32)],
        ),
        out_shape=[
            jax.ShapeDtypeStruct((length, columns), BF16),
            jax.ShapeDtypeStruct((blocks, 1, heads * BQ), F32),
        ],
        cost_estimate=pl.CostEstimate(
            flops=4 * length * 1024 * columns * heads,
            bytes_accessed=8 * length * columns,
            transcendentals=length * 1024 * heads,
        ),
        name="attend",
    )(first, queries, key_rows, value_rows, start_blocks)


def attend_back_kernel(
    first_ref,
    q_ref,
    k_ref,
    v_ref,
    do_ref,
    o_ref,
    lse_ref,
    start_ref,
    cos_ref,
    low_ref,
    high_ref,
    grad_ref,
    key_acc,
    value_acc,
    query_acc,
):
    block, columns = q_ref.shape
    heads = columns // HEAD_DIM
    length = k_ref.shape[0]
    index = pl.program_id(0)

    @pl.when(index == 0)
    def _():
        key_acc[...] = jnp.zeros_like(key_acc)
        value_acc[...] = jnp.zeros_like(value_acc)

    stacked = stack_heads(q_ref[...])
    stacked_do = stack_heads(do_ref[...])
    start_row, query_row = query_rows(start_ref, block, heads)
    lse_row = lse_ref[0]
    products = do_ref[...].astype(F32) * o_ref[...].astype(F32)
    head_rows = lax.broadcasted_iota(jnp.int32, (8, columns), 0)
    head_lanes = lax.broadcasted_iota(jnp.int32, (8, columns), 1) // HEAD_DIM
    picked = lax.dot_general(
        (head_rows == head_lanes).astype(F32),
        products,
        (((1,), (1,)), ((), ())),
        precision=lax.Precision.HIGHEST,
        preferred_element_type=F32,
    )
    inner_row = jnp.concatenate([picked[head : head + 1, :] for head in range(heads)], axis=1)
    query_acc[...] = jnp.zeros_like(query_acc)

    def body(step, carry):
        at = pl.multiple_of(step * BK, BK)
        key_block = k_ref[pl.ds(at, BK), :]
        scores, allowed = score_block(key_block, stacked, at, start_row, query_row)
        weights = jnp.where(allowed, jnp.exp(scores - lse_row), 0.0)
        grad_weights = lax.dot_general(
            v_ref[pl.ds(at, BK), :],
            stacked_do,
            (((1,), (1,)), ((), ())),
            preferred_element_type=F32,
        )
        grad_scores = (weights * (grad_weights - inner_row)).astype(BF16)
        value_acc[pl.ds(at, BK), :] += jnp.dot(
            weights.astype(BF16), stacked_do, preferred_element_type=F32
        )
        key_acc[pl.ds(at, BK), :] += jnp.dot(grad_scores, stacked, preferred_element_type=F32)
        query_acc[...] += lax.dot_general(
            key_block, grad_scores, (((0,), (0,)), ((), ())), preferred_element_type=F32
        )
        return carry

    lax.fori_loop(first_ref[index], (index * block + block - 1) // BK + 1, body, 0)

    def turn_back(grads, at, rows):
        kept = grads.astype(BF16).astype(F32)
        return turn(
            kept,
            cos_ref[pl.ds(at, rows), :],
            -low_ref[pl.ds(at, rows), :],
            -high_ref[pl.ds(at, rows), :],
        ).astype(BF16)

    at_query = pl.multiple_of(index * block, block)
    grad_ref[pl.ds(at_query, block), :columns] = turn_back(
        unstack_heads(query_acc[...], block) * HEAD_DIM**-0.5, at_query, block
    )

    @pl.when(index == pl.num_programs(0) - 1)
    def _():
        def finish(step, carry):
            at = pl.multiple_of(step * BK, BK)
            grad_ref[pl.ds(at, BK), columns : 2 * columns] = turn_back(
                key_acc[pl.ds(at, BK), :], at, BK
            )
            grad_ref[pl.ds(at, BK), 2 * columns :] = value_acc[pl.ds(at, BK), :].astype(BF16)
            return carry

        lax.fori_loop(0, length // BK, finish, 0)


def attend_back(first, queries, key_rows, value_rows, grad_att, attended, lse, start_blocks, tables):
    length, columns = queries.shape
    blocks = length // BQ
    heads = columns // HEAD_DIM
    row_spec = pl.BlockSpec((BQ, columns), lambda i, f: (i, 0))
    whole = pl.BlockSpec((length, columns), lambda i, f: (0, 0))
    table_spec = pl.BlockSpec(tables[0].shape, lambda i, f: (0, 0))
    return pl.pallas_call(
        attend_back_kernel,
        grid_spec=pltpu.PrefetchScalarGridSpec(
            num_scalar_prefetch=1,
            grid=(blocks,),
            in_specs=[
                row_spec,
                whole,
                whole,
                row_spec,
                row_spec,
                pl.BlockSpec((1, 1, heads * BQ), lambda i, f: (i, 0, 0)),
                pl.BlockSpec((1, 1, BQ), lambda i, f: (i, 0, 0)),
                table_spec,
                table_spec,
                table_spec,
            ],
            out_specs=pl.BlockSpec((length, 3 * columns), lambda i, f: (0, 0)),
            scratch_shapes=[
                pltpu.VMEM((length, columns), F32),
                pltpu.VMEM((length, columns), F32),
                pltpu.VMEM((columns, heads * BQ), F32),
            ],
        ),
        out_shape=jax.ShapeDtypeStruct((length, 3 * columns), BF16),
        cost_estimate=pl.CostEstimate(
            flops=10 * length * 1024 * columns * heads,
            bytes_accessed=16 * length * columns,
            transcendentals=length * 1024 * heads,
        ),
        name="attend_back",
    )(first, queries, key_rows, value_rows, grad_att, attended, lse, start_blocks, *tables)


def bits_of(name):
    size = lax.axis_size(name)
    count = size.bit_length() - 1
    return count if size == 1 << count else None


def swap(values, name, bit):
    size = lax.axis_size(name)
    return lax.ppermute(values, name, [(i, i ^ (1 << bit)) for i in range(size)])


def write_stacked(piece, outs):
    outs[0][0] = piece.astype(F32)


def write_rows(piece, outs):
    at = 0
    for out_ref in outs:
        size = out_ref.shape[0]
        out_ref[...] = piece[at : at + size, :].astype(F32)
        at += size


def write_lanes(piece, outs):
    parts, _, size = outs[0].shape
    for part in range(parts):
        outs[0][part] = piece[:, part * size : (part + 1) * size].astype(F32)


def place_kernel(write, count, color_ref, where_ref, *refs):
    step = pl.program_id(0)
    for number in range(count):

        @pl.when(step == number)
        def _(number=number):
            write(refs[number][...], refs[count:])


def place_blocks(write, color, where, pieces, out_shapes, out_specs):
    rows, columns = pieces[0].shape
    count = len(pieces)
    return pl.pallas_call(
        functools.partial(place_kernel, write, count),
        grid_spec=pltpu.PrefetchScalarGridSpec(
            num_scalar_prefetch=2,
            grid=(count,),
            in_specs=[pl.BlockSpec((rows, columns), lambda i, c, w: (0, 0))] * count,
            out_specs=out_specs,
        ),
        out_shape=[jax.ShapeDtypeStruct(shape, F32) for shape in out_shapes],
        cost_estimate=pl.CostEstimate(
            flops=0, bytes_accessed=6 * count * rows * columns, transcendentals=0
        ),
        name="place_blocks",
    )(color, where, *pieces)


class DpSum:
    def __init__(self, *grads, paired=False):
        self.grads = grads
        self.paired = paired
        self.count = bits_of("dp")
        pieces = (1 if paired else 2) << self.count
        self.axis = 0 if all(g.shape[0] % (8 * pieces) == 0 for g in grads) else 1
        self.sizes = [g.shape[self.axis] // pieces for g in grads]
        self.mine = lax.axis_index("dp")
        self.orders = [list(range(self.count)), list(range(self.count))[::-1]]
        self.level = 0
        if paired:
            self.state = [((grad,), self.sizes[:1], 0) for grad in grads]
        else:
            self.state = [(grads, self.sizes, color << self.count) for color in range(2)]
        self.held = None
        self.ready()

    def cut(self, color, side):
        grads, units, base = self.state[color]
        span = (1 << self.count) >> (self.level + 1)
        parts = []
        for grad, unit in zip(grads, units):
            at = (base + side * span) * unit
            parts.append(lax.dynamic_slice_in_dim(grad, at, span * unit, self.axis))
        if len(parts) == 1:
            return parts[0]
        if self.axis:
            return jnp.concatenate(parts, axis=0)
        parts = [p.reshape(span, unit, p.shape[1]) for p, unit in zip(parts, units)]
        joined = jnp.concatenate(parts, axis=1)
        return joined.reshape(-1, joined.shape[2])

    def side(self, color):
        return (self.mine >> self.orders[color][self.level]) & 1

    def ready(self):
        if self.level < self.count:
            self.out = [self.cut(color, 1 - self.side(color)) for color in range(2)]
        elif self.held is None:
            self.held = [[(self.state[color][0][0], 0)] for color in range(2)]

    def send(self):
        if self.level < self.count:
            self.got = [
                swap(self.out[color], "dp", self.orders[color][self.level])
                for color in range(2)
            ]
            return
        for color in range(2):
            bit = self.orders[color][2 * self.count - 1 - self.level]
            self.held[color] += [
                (swap(piece, "dp", bit), mask ^ (1 << bit)) for piece, mask in self.held[color]
            ]

    def arrive(self):
        if self.level < self.count:
            state = []
            for color in range(2):
                keep = self.cut(color, self.side(color))
                total = (keep.astype(F32) + self.got[color].astype(F32)).astype(BF16)
                whole = self.axis == 0 and not self.paired
                state.append(((total,), [sum(self.sizes) if whole else self.sizes[0]], 0))
            self.state = state
        self.level += 1
        self.ready()

    def moving(self):
        return self.out if self.held is None else self.held

    def fresh(self):
        return [held[len(held) // 2][0] for held in self.held]

    def result(self, write):
        pieces, colors, where = [], [], []
        for color in range(2):
            for piece, mask in self.held[color]:
                owner = self.mine ^ mask
                spot = 0 if self.paired else color
                for bit in self.orders[color]:
                    spot = spot * 2 + ((owner >> bit) & 1)
                pieces.append(piece)
                colors.append(color)
                where.append(spot)
        rows, columns = pieces[0].shape
        length, width = self.grads[0].shape
        if write is write_stacked:
            shapes = [(2, length, width)]
            blocks = [(1, rows, columns)]
        elif write is write_lanes:
            shapes = [(3, length, width // 3)]
            blocks = [(3, rows, columns // 3)]
        else:
            shapes = [g.shape for g in self.grads]
            blocks = [(rows * s[0] // sum(t[0] for t in shapes), columns) for s in shapes]
        lead = {write_stacked: lambda i, c: (c[i],), write_lanes: lambda i, c: (0,)}.get(
            write, lambda i, c: ()
        )

        def out_map(i, c, w):
            return lead(i, c) + ((w[i], 0) if self.axis == 0 else (0, w[i]))

        return place_blocks(
            write,
            jnp.array(colors, jnp.int32),
            jnp.stack(where).astype(jnp.int32),
            pieces,
            shapes,
            [pl.BlockSpec(block, out_map) for block in blocks],
        )


def fence(values, *sums):
    values, moving = lax.optimization_barrier((values, [item.moving() for item in sums]))
    for item, arrived in zip(sums, moving):
        if item.held is None:
            item.out = arrived
        else:
            item.held = arrived
    return values


def sum_small(values, name, bits=None):
    count = bits_of(name)
    if count is None:
        return lax.psum(values, name) if bits is None or 0 in bits else values
    for bit in range(count) if bits is None else bits:
        values = values + swap(values, name, bit)
    return values


def tail_kernel(x_ref, g_ref, c_ref, gain_ref, stat_ref, grad_ref, sums_ref):
    @pl.when(pl.program_id(0) == 0)
    def _():
        sums_ref[...] = jnp.zeros_like(sums_ref)
        sums_ref[2:3, :] = stat_ref[...]

    residual = x_ref[...].astype(F32)
    centered = residual - jnp.mean(residual, -1, keepdims=True)
    inv_std = lax.rsqrt(jnp.mean(centered * centered, -1, keepdims=True) + EPSILON)
    normalized = centered * inv_std
    grads = g_ref[...].astype(F32)
    sums_ref[0:1, :] += jnp.sum(grads * normalized, axis=0, keepdims=True)
    sums_ref[1:2, :] += jnp.sum(grads, axis=0, keepdims=True)
    scaled = grads * gain_ref[...]
    grad_ref[:, 0, :] = (
        inv_std
        * (
            scaled
            - jnp.mean(scaled, -1, keepdims=True)
            - normalized * jnp.mean(scaled * normalized, -1, keepdims=True)
        )
        + c_ref[...].astype(F32)
    )


def tail(layer_in, grad_normed, cot_here, norm_gain, stat_row):
    length, width = layer_in.shape
    rows = min(64, length)
    row_spec = pl.BlockSpec((rows, width), lambda i: (i, 0))
    one_spec = pl.BlockSpec((1, width), lambda i: (0, 0))
    return pl.pallas_call(
        tail_kernel,
        grid=(length // rows,),
        in_specs=[row_spec, row_spec, row_spec, one_spec, one_spec],
        out_specs=[
            pl.BlockSpec((rows, 1, width), lambda i: (i, 0, 0)),
            pl.BlockSpec((4, width), lambda i: (0, 0)),
        ],
        out_shape=[
            jax.ShapeDtypeStruct((length, 1, width), F32),
            jax.ShapeDtypeStruct((4, width), F32),
        ],
        name="tail",
    )(layer_in, grad_normed, cot_here, norm_gain.reshape(1, width), stat_row)


def back_products_kernel(p_ref, q_ref, g_ref, u_ref, w_ref, out_ref):
    turned = (((1,), (1,)), ((), ()))
    columns = q_ref.shape[2]
    total = jnp.dot(g_ref[...], w_ref[0], preferred_element_type=F32)
    total += jnp.dot(u_ref[...], w_ref[1], preferred_element_type=F32)
    for number in range(3):
        total += lax.dot_general(
            p_ref[:, number * columns : (number + 1) * columns],
            q_ref[number],
            turned,
            preferred_element_type=F32,
        )
    out_ref[...] = total.astype(BF16)


def back_products(grad_proj, w_qkv, grad_gate, grad_up, w_gate_up):
    length = grad_proj.shape[0]
    _, width, columns = w_qkv.shape
    hidden = grad_gate.shape[1]
    rows = min(256, length)
    return pl.pallas_call(
        back_products_kernel,
        grid=(length // rows,),
        in_specs=[
            pl.BlockSpec((rows, 3 * columns), lambda i: (i, 0)),
            pl.BlockSpec(w_qkv.shape, lambda i: (0, 0, 0)),
            pl.BlockSpec((rows, hidden), lambda i: (i, 0)),
            pl.BlockSpec((rows, hidden), lambda i: (i, 0)),
            pl.BlockSpec(w_gate_up.shape, lambda i: (0, 0, 0)),
        ],
        out_specs=pl.BlockSpec((rows, width), lambda i: (i, 0)),
        out_shape=jax.ShapeDtypeStruct((length, width), BF16),
        name="back_products",
    )(grad_proj, w_qkv, grad_gate, grad_up, w_gate_up)


def local(
    layer_in,
    segment_ids,
    valid_counts,
    norm_gain,
    norm_shift,
    w_qkv,
    b_qkv,
    w_out,
    w_gate_up,
    w_down,
    out_grad,
):
    local_len, row_count, model_width = layer_in.shape
    assert row_count == 1
    seq_len = local_len * lax.axis_size("mp")
    col_qkv = w_qkv.shape[2]
    ff_local = w_gate_up.shape[2]
    layer_in = layer_in[:, 0]
    position_here = lax.axis_index("mp") * local_len + jnp.arange(local_len, dtype=jnp.int32)
    valid_here = (position_here < valid_counts[0]).astype(F32)

    residual = layer_in.astype(F32)
    centered = residual - jnp.mean(residual, -1, keepdims=True)
    inv_std = lax.rsqrt(jnp.mean(centered * centered, -1, keepdims=True) + EPSILON)
    normalized = centered * inv_std
    normed = (normalized * norm_gain + norm_shift).astype(BF16)
    cot_here = jnp.where(valid_here[:, None] > 0, out_grad[:, 0], jnp.zeros((), BF16))
    gathered = lax.all_gather(normed, "mp", axis=0, tiled=True)
    cotangent = lax.all_gather(cot_here, "mp", axis=0, tiled=True)

    w_qkv = jnp.transpose(w_qkv, (1, 0, 2))
    w_gate_up = jnp.transpose(w_gate_up, (1, 2, 0))
    starts = starts_of(segment_ids)[0]
    tables = rotary_lanes(jnp.arange(seq_len, dtype=jnp.int32) - starts)
    start_blocks = starts.reshape(seq_len // BQ, 1, BQ)
    first = start_blocks[:, 0, 0] // BK
    gathered, tables, first, start_blocks = lax.optimization_barrier(
        (gathered, tables, first, start_blocks)
    )

    def product(left, right):
        return jnp.dot(left, right, preferred_element_type=F32).astype(BF16)

    def turned_product(left, right):
        return lax.dot_general(
            left, right, (((1,), (1,)), ((), ())), preferred_element_type=F32
        )

    def token_sum(left, right):
        return lax.dot_general(
            left, right, (((0,), (0,)), ((), ())), preferred_element_type=F32
        ).astype(BF16)

    def scattered(partial):
        return lax.psum_scatter(partial, "mp", scatter_dimension=0, tiled=True)

    gate = turned_product(gathered, w_gate_up[0])
    up = turned_product(gathered, w_gate_up[1])
    sigmoid_gate = jax.nn.sigmoid(gate)
    hidden = (gate * sigmoid_gate * up).astype(BF16)
    mlp_partial = product(hidden, w_down)
    mlp_sum = scattered(mlp_partial)
    gathered_next, mlp_partial = lax.optimization_barrier((gathered, mlp_partial))
    queries, key_rows, value_rows = project(gathered_next, w_qkv, b_qkv, tables)
    attended, lse = attend(first, queries, key_rows, value_rows, start_blocks)
    attn_partial = product(attended, w_out)
    attn_sum = scattered(attn_partial)

    cotangent, attn_partial = lax.optimization_barrier((cotangent, attn_partial))
    sum_down = DpSum(token_sum(hidden, cotangent), token_sum(attended, cotangent))
    cotangent = fence(cotangent, sum_down)
    sum_down.send()
    grad_hid = turned_product(cotangent, w_down).astype(BF16).astype(F32)
    grad_gate = (
        grad_hid * up * sigmoid_gate * (1.0 + gate * (1.0 - sigmoid_gate))
    ).astype(BF16)
    grad_up = (grad_hid * gate * sigmoid_gate).astype(BF16)
    grad_att = turned_product(cotangent, w_out).astype(BF16)
    sum_down.arrive()
    grad_gate, grad_up, grad_att = fence((grad_gate, grad_up, grad_att), sum_down)
    sum_down.send()
    sum_gate = token_sum(grad_gate, gathered)
    sum_down.arrive()
    sum_gate, grad_up = fence((sum_gate, grad_up), sum_down)
    sum_down.send()
    sum_gate_up = DpSum(sum_gate, token_sum(grad_up, gathered), paired=True)
    sum_down.arrive()
    grad_att = fence(grad_att, sum_gate_up, sum_down)
    sum_gate_up.send()
    sum_down.send()
    fresh = sum_down.fresh()
    grad_proj = attend_back(
        first, queries, key_rows, value_rows, grad_att, attended, lse, start_blocks, tables
    )
    sum_gate_up.arrive()
    sum_down.arrive()
    grad_proj, mlp_sum, _ = fence((grad_proj, mlp_sum, fresh), sum_gate_up)
    sum_gate_up.send()
    normed_partial = back_products(grad_proj, w_qkv, grad_gate, grad_up, w_gate_up)
    while sum_down.level < 2 * sum_down.count:
        sum_down.send()
        sum_down.arrive()
    sum_gate_up.arrive()
    grad_proj, normed_partial = fence((grad_proj, normed_partial), sum_gate_up, sum_down)
    sum_gate_up.send()
    sum_qkv = token_sum(gathered, grad_proj)
    sum_gate_up.arrive()
    sum_qkv = DpSum(fence(sum_qkv, sum_gate_up))
    bias_sums = jnp.sum(grad_proj, axis=0, dtype=F32).reshape(-1, 128)
    sum_qkv.send()
    sum_qkv.arrive()
    normed_partial, attn_sum, bias_sums = fence(
        (normed_partial, attn_sum, bias_sums), sum_qkv
    )
    grad_normed = scattered(normed_partial)
    sum_gate_up.send()
    sum_qkv.send()
    bias_sums = sum_small(bias_sums, "dp", [0])
    mlp_part = mlp_sum.astype(F32)
    attn_part = attn_sum.astype(F32)
    layer_out = (residual + attn_part + mlp_part).astype(BF16)
    statistics = jnp.stack(
        [
            jnp.sum(valid_here * jnp.sum(residual * residual, -1)),
            jnp.sum(valid_here * jnp.sum(attn_part * attn_part, -1)),
            jnp.sum(valid_here * jnp.sum(mlp_part * mlp_part, -1)),
            jnp.sum(valid_here),
        ]
    )
    stat_row = jnp.pad(statistics, (0, model_width - 4)).reshape(1, model_width)
    fresh = sum_gate_up.fresh()
    sum_gate_up.arrive()
    sum_qkv.arrive()
    bias_sums, layer_out, stat_row, _ = fence((bias_sums, layer_out, stat_row, fresh), sum_qkv)
    sum_qkv.send()
    bias_sums = sum_small(bias_sums, "dp", range(1, sum_qkv.count))
    down_sums = sum_down.result(write_rows)
    sum_qkv.arrive()
    while sum_gate_up.level < 2 * sum_gate_up.count:
        sum_gate_up.send()
        sum_gate_up.arrive()
    down_sums, bias_sums = fence((down_sums, bias_sums), sum_gate_up, sum_qkv)
    while sum_qkv.level < 2 * sum_qkv.count:
        sum_qkv.send()
        sum_qkv.arrive()
    (grad_w_gate_up,) = sum_gate_up.result(write_stacked)
    grad_w_gate_up = fence(grad_w_gate_up, sum_qkv)
    (grad_w_qkv,) = sum_qkv.result(write_lanes)
    grad_w_down, grad_w_out = down_sums
    grad_normed, grad_w_gate_up, grad_w_qkv = fence(
        (grad_normed, grad_w_gate_up, grad_w_qkv)
    )
    input_grad, small = tail(layer_in, grad_normed, cot_here, norm_gain, stat_row)
    small = sum_small(sum_small(small, "mp"), "dp")
    totals = small[2]
    return (
        layer_out[:, None],
        input_grad,
        small[0],
        small[1],
        jnp.transpose(grad_w_qkv, (1, 0, 2)),
        bias_sums.reshape(3, col_qkv),
        grad_w_out,
        jnp.transpose(grad_w_gate_up, (2, 0, 1)),
        grad_w_down,
        jnp.sqrt(totals[:3] / (totals[3] * model_width)),
    )


def solution(mesh):
    placed = (
        P("mp", "dp", None),
        P("dp", None),
        P("dp"),
        P(),
        P(),
        P(None, None, "mp"),
        P(None, "mp"),
        P("mp", None),
        P(None, None, "mp"),
        P("mp", None),
        P("mp", "dp", None),
    )
    return jax.shard_map(
        local,
        mesh=mesh,
        in_specs=placed,
        out_specs=(
            P("mp", "dp", None),
            P("mp", "dp", None),
            P(),
            P(),
            P(None, None, "mp"),
            P(None, "mp"),
            P("mp", None),
            P(None, None, "mp"),
            P("mp", None),
            P(),
        ),
        check_vma=False,
    )
```

```python
import functools

import jax
import jax.numpy as jnp
from jax import lax
from jax.experimental import pallas as pl
from jax.experimental.pallas import tpu as pltpu
from jax.sharding import PartitionSpec as P

HEAD_DIM = 64
ROT = 16
EPSILON = 1e-05
BQ = 128
BK = 256
NEG = -1e30
F32 = jnp.float32
BF16 = jnp.bfloat16


def starts_of(segment_ids):
    length = segment_ids.shape[1]
    steps_all = jnp.arange(length, dtype=jnp.int32)[None, :]
    change = jnp.concatenate(
        [
            jnp.ones_like(segment_ids[:, :1]),
            (segment_ids[:, 1:] != segment_ids[:, :-1]).astype(jnp.int32),
        ],
        axis=1,
    )
    return lax.cummax(jnp.where(change > 0, steps_all, jnp.zeros_like(change)), axis=1)


def rotary_lanes(positions):
    half_rot = ROT // 2
    lane = jnp.arange(2 * HEAD_DIM, dtype=jnp.int32) % HEAD_DIM
    power = (lane % half_rot).astype(F32)
    frequency = jnp.where(lane < ROT, 10000.0 ** (-(power * 2.0) / ROT), 0.0)
    angles = positions.astype(F32)[:, None] * frequency
    sine = jnp.sin(angles)
    low = jnp.where(lane < half_rot, -sine, 0.0)
    high = jnp.where((lane >= half_rot) & (lane < ROT), sine, 0.0)
    return jnp.cos(angles), low, high


def lane_tile(table, columns):
    return jnp.concatenate([table] * (columns // table.shape[1]), axis=1)


def turn(values, cosine, low, high):
    columns = values.shape[1]
    half_rot = ROT // 2
    return (
        values * lane_tile(cosine, columns)
        + pltpu.roll(values, columns - half_rot, 1) * lane_tile(low, columns)
        + pltpu.roll(values, half_rot, 1) * lane_tile(high, columns)
    )


def project_kernel(x_ref, w_ref, b_ref, cos_ref, low_ref, high_ref, q_ref, k_ref, v_ref):
    tables = (cos_ref[...], low_ref[...], high_ref[...])

    def part(number):
        flat = jnp.dot(x_ref[...], w_ref[number], preferred_element_type=F32)
        return flat + b_ref[number : number + 1, :].astype(F32)

    queries = turn(part(0), *tables).astype(BF16)
    q_ref[...] = (queries.astype(F32) * HEAD_DIM**-0.5).astype(BF16)
    k_ref[...] = turn(part(1), *tables).astype(BF16)
    v_ref[...] = part(2).astype(BF16)


def project(gathered, w_qkv, b_qkv, tables):
    length, width = gathered.shape
    columns = w_qkv.shape[2]
    rows = min(256, length)
    table_spec = pl.BlockSpec((rows, tables[0].shape[1]), lambda i: (i, 0))
    out_spec = pl.BlockSpec((rows, columns), lambda i: (i, 0))
    return pl.pallas_call(
        project_kernel,
        grid=(length // rows,),
        in_specs=[
            pl.BlockSpec((rows, width), lambda i: (i, 0)),
            pl.BlockSpec(w_qkv.shape, lambda i: (0, 0, 0)),
            pl.BlockSpec(b_qkv.shape, lambda i: (0, 0)),
            table_spec,
            table_spec,
            table_spec,
        ],
        out_specs=[out_spec] * 3,
        out_shape=[jax.ShapeDtypeStruct((length, columns), BF16)] * 3,
        cost_estimate=pl.CostEstimate(
            flops=6 * length * width * columns,
            bytes_accessed=2 * (length * width + 3 * width * columns + 3 * length * columns),
            transcendentals=0,
        ),
        name="project",
    )(gathered, w_qkv, b_qkv, *tables)


def stack_heads(block):
    columns = block.shape[1]
    head_of = lax.broadcasted_iota(jnp.int32, block.shape, 1) // HEAD_DIM
    return jnp.concatenate(
        [
            jnp.where(head_of == head, block, jnp.zeros_like(block))
            for head in range(columns // HEAD_DIM)
        ],
        axis=0,
    )


def unstack_heads(stacked, block):
    heads = stacked.shape[1] // block
    return jnp.concatenate(
        [
            stacked[head * HEAD_DIM : (head + 1) * HEAD_DIM, head * block : (head + 1) * block]
            for head in range(heads)
        ],
        axis=0,
    ).T


def score_block(key_block, stacked_queries, key_at, start_row, query_row):
    scores = lax.dot_general(
        key_block, stacked_queries, (((1,), (1,)), ((), ())), preferred_element_type=F32
    )
    key_pos = key_at + lax.broadcasted_iota(jnp.int32, scores.shape, 0)
    allowed = (key_pos >= start_row) & (key_pos <= query_row)
    return scores, allowed


def query_rows(start_ref, block, heads):
    start_row = jnp.concatenate([start_ref[0]] * heads, axis=1)
    query_row = pl.program_id(0) * block + lax.broadcasted_iota(jnp.int32, (1, block), 1)
    return start_row, jnp.concatenate([query_row] * heads, axis=1)


def attend_kernel(first_ref, q_ref, k_ref, v_ref, start_ref, o_ref, lse_ref, acc_ref):
    block, columns = q_ref.shape
    heads = columns // HEAD_DIM
    index = pl.program_id(0)
    stacked = stack_heads(q_ref[...])
    start_row, query_row = query_rows(start_ref, block, heads)
    acc_ref[...] = jnp.zeros_like(acc_ref)

    def body(step, carry):
        highest, total = carry
        at = pl.multiple_of(step * BK, BK)
        scores, allowed = score_block(
            k_ref[pl.ds(at, BK), :], stacked, at, start_row, query_row
        )
        scores = jnp.where(allowed, scores, NEG)
        newest = jnp.maximum(highest, jnp.max(scores, axis=0, keepdims=True))
        weights = jnp.exp(scores - newest)
        scale = jnp.exp(highest - newest)
        total = total * scale + jnp.sum(weights, axis=0, keepdims=True)
        acc_ref[...] = acc_ref[...] * scale + lax.dot_general(
            v_ref[pl.ds(at, BK), :],
            weights.astype(BF16),
            (((0,), (0,)), ((), ())),
            preferred_element_type=F32,
        )
        return newest, total

    highest, total = lax.fori_loop(
        first_ref[index],
        (index * block + block - 1) // BK + 1,
        body,
        (jnp.full((1, heads * block), NEG, F32), jnp.zeros((1, heads * block), F32)),
    )
    o_ref[...] = unstack_heads(acc_ref[...] / total, block).astype(BF16)
    lse_ref[0] = highest + jnp.log(total)


def attend(first, queries, key_rows, value_rows, start_blocks):
    length, columns = queries.shape
    blocks = length // BQ
    heads = columns // HEAD_DIM
    row_spec = pl.BlockSpec((BQ, columns), lambda i, f: (i, 0))
    whole = pl.BlockSpec((length, columns), lambda i, f: (0, 0))
    return pl.pallas_call(
        attend_kernel,
        grid_spec=pltpu.PrefetchScalarGridSpec(
            num_scalar_prefetch=1,
            grid=(blocks,),
            in_specs=[
                row_spec,
                whole,
                whole,
                pl.BlockSpec((1, 1, BQ), lambda i, f: (i, 0, 0)),
            ],
            out_specs=[
                row_spec,
                pl.BlockSpec((1, 1, heads * BQ), lambda i, f: (i, 0, 0)),
            ],
            scratch_shapes=[pltpu.VMEM((columns, heads * BQ), F32)],
        ),
        out_shape=[
            jax.ShapeDtypeStruct((length, columns), BF16),
            jax.ShapeDtypeStruct((blocks, 1, heads * BQ), F32),
        ],
        cost_estimate=pl.CostEstimate(
            flops=4 * length * 1024 * columns * heads,
            bytes_accessed=8 * length * columns,
            transcendentals=length * 1024 * heads,
        ),
        name="attend",
    )(first, queries, key_rows, value_rows, start_blocks)


def attend_back_kernel(
    first_ref,
    q_ref,
    k_ref,
    v_ref,
    do_ref,
    o_ref,
    lse_ref,
    start_ref,
    cos_ref,
    low_ref,
    high_ref,
    grad_ref,
    key_acc,
    value_acc,
    query_acc,
):
    block, columns = q_ref.shape
    heads = columns // HEAD_DIM
    length = k_ref.shape[0]
    index = pl.program_id(0)

    @pl.when(index == 0)
    def _():
        key_acc[...] = jnp.zeros_like(key_acc)
        value_acc[...] = jnp.zeros_like(value_acc)

    stacked = stack_heads(q_ref[...])
    stacked_do = stack_heads(do_ref[...])
    start_row, query_row = query_rows(start_ref, block, heads)
    lse_row = lse_ref[0]
    products = do_ref[...].astype(F32) * o_ref[...].astype(F32)
    head_rows = lax.broadcasted_iota(jnp.int32, (8, columns), 0)
    head_lanes = lax.broadcasted_iota(jnp.int32, (8, columns), 1) // HEAD_DIM
    picked = lax.dot_general(
        (head_rows == head_lanes).astype(F32),
        products,
        (((1,), (1,)), ((), ())),
        precision=lax.Precision.HIGHEST,
        preferred_element_type=F32,
    )
    inner_row = jnp.concatenate([picked[head : head + 1, :] for head in range(heads)], axis=1)
    query_acc[...] = jnp.zeros_like(query_acc)

    def body(step, carry):
        at = pl.multiple_of(step * BK, BK)
        key_block = k_ref[pl.ds(at, BK), :]
        scores, allowed = score_block(key_block, stacked, at, start_row, query_row)
        weights = jnp.where(allowed, jnp.exp(scores - lse_row), 0.0)
        grad_weights = lax.dot_general(
            v_ref[pl.ds(at, BK), :],
            stacked_do,
            (((1,), (1,)), ((), ())),
            preferred_element_type=F32,
        )
        grad_scores = (weights * (grad_weights - inner_row)).astype(BF16)
        value_acc[pl.ds(at, BK), :] += jnp.dot(
            weights.astype(BF16), stacked_do, preferred_element_type=F32
        )
        key_acc[pl.ds(at, BK), :] += jnp.dot(grad_scores, stacked, preferred_element_type=F32)
        query_acc[...] += lax.dot_general(
            key_block, grad_scores, (((0,), (0,)), ((), ())), preferred_element_type=F32
        )
        return carry

    lax.fori_loop(first_ref[index], (index * block + block - 1) // BK + 1, body, 0)

    def turn_back(grads, at, rows):
        kept = grads.astype(BF16).astype(F32)
        return turn(
            kept,
            cos_ref[pl.ds(at, rows), :],
            -low_ref[pl.ds(at, rows), :],
            -high_ref[pl.ds(at, rows), :],
        ).astype(BF16)

    at_query = pl.multiple_of(index * block, block)
    grad_ref[pl.ds(at_query, block), :columns] = turn_back(
        unstack_heads(query_acc[...], block) * HEAD_DIM**-0.5, at_query, block
    )

    @pl.when(index == pl.num_programs(0) - 1)
    def _():
        def finish(step, carry):
            at = pl.multiple_of(step * BK, BK)
            grad_ref[pl.ds(at, BK), columns : 2 * columns] = turn_back(
                key_acc[pl.ds(at, BK), :], at, BK
            )
            grad_ref[pl.ds(at, BK), 2 * columns :] = value_acc[pl.ds(at, BK), :].astype(BF16)
            return carry

        lax.fori_loop(0, length // BK, finish, 0)


def attend_back(first, queries, key_rows, value_rows, grad_att, attended, lse, start_blocks, tables):
    length, columns = queries.shape
    blocks = length // BQ
    heads = columns // HEAD_DIM
    row_spec = pl.BlockSpec((BQ, columns), lambda i, f: (i, 0))
    whole = pl.BlockSpec((length, columns), lambda i, f: (0, 0))
    table_spec = pl.BlockSpec(tables[0].shape, lambda i, f: (0, 0))
    return pl.pallas_call(
        attend_back_kernel,
        grid_spec=pltpu.PrefetchScalarGridSpec(
            num_scalar_prefetch=1,
            grid=(blocks,),
            in_specs=[
                row_spec,
                whole,
                whole,
                row_spec,
                row_spec,
                pl.BlockSpec((1, 1, heads * BQ), lambda i, f: (i, 0, 0)),
                pl.BlockSpec((1, 1, BQ), lambda i, f: (i, 0, 0)),
                table_spec,
                table_spec,
                table_spec,
            ],
            out_specs=pl.BlockSpec((length, 3 * columns), lambda i, f: (0, 0)),
            scratch_shapes=[
                pltpu.VMEM((length, columns), F32),
                pltpu.VMEM((length, columns), F32),
                pltpu.VMEM((columns, heads * BQ), F32),
            ],
        ),
        out_shape=jax.ShapeDtypeStruct((length, 3 * columns), BF16),
        cost_estimate=pl.CostEstimate(
            flops=10 * length * 1024 * columns * heads,
            bytes_accessed=16 * length * columns,
            transcendentals=length * 1024 * heads,
        ),
        name="attend_back",
    )(first, queries, key_rows, value_rows, grad_att, attended, lse, start_blocks, *tables)


def bits_of(name):
    size = lax.axis_size(name)
    count = size.bit_length() - 1
    return count if size == 1 << count else None


def swap(values, name, bit):
    size = lax.axis_size(name)
    return lax.ppermute(values, name, [(i, i ^ (1 << bit)) for i in range(size)])


def write_stacked(piece, outs):
    outs[0][0] = piece.astype(F32)


def write_rows(piece, outs):
    at = 0
    for out_ref in outs:
        size = out_ref.shape[0]
        out_ref[...] = piece[at : at + size, :].astype(F32)
        at += size


def write_lanes(piece, outs):
    parts, _, size = outs[0].shape
    for part in range(parts):
        outs[0][part] = piece[:, part * size : (part + 1) * size].astype(F32)


def place_kernel(write, count, color_ref, where_ref, *refs):
    step = pl.program_id(0)
    for number in range(count):

        @pl.when(step == number)
        def _(number=number):
            write(refs[number][...], refs[count:])


def place_blocks(write, color, where, pieces, out_shapes, out_specs):
    rows, columns = pieces[0].shape
    count = len(pieces)
    return pl.pallas_call(
        functools.partial(place_kernel, write, count),
        grid_spec=pltpu.PrefetchScalarGridSpec(
            num_scalar_prefetch=2,
            grid=(count,),
            in_specs=[pl.BlockSpec((rows, columns), lambda i, c, w: (0, 0))] * count,
            out_specs=out_specs,
        ),
        out_shape=[jax.ShapeDtypeStruct(shape, F32) for shape in out_shapes],
        cost_estimate=pl.CostEstimate(
            flops=0, bytes_accessed=6 * count * rows * columns, transcendentals=0
        ),
        name="place_blocks",
    )(color, where, *pieces)


class DpSum:
    def __init__(self, *grads, paired=False):
        self.grads = grads
        self.paired = paired
        self.count = bits_of("dp")
        pieces = (1 if paired else 2) << self.count
        self.axis = 0 if all(g.shape[0] % (8 * pieces) == 0 for g in grads) else 1
        self.sizes = [g.shape[self.axis] // pieces for g in grads]
        self.mine = lax.axis_index("dp")
        self.orders = [list(range(self.count)), list(range(self.count))[::-1]]
        self.level = 0
        if paired:
            self.state = [((grad,), self.sizes[:1], 0) for grad in grads]
        else:
            self.state = [(grads, self.sizes, color << self.count) for color in range(2)]
        self.held = None
        self.ready()

    def cut(self, color, side):
        grads, units, base = self.state[color]
        span = (1 << self.count) >> (self.level + 1)
        parts = []
        for grad, unit in zip(grads, units):
            at = (base + side * span) * unit
            parts.append(lax.dynamic_slice_in_dim(grad, at, span * unit, self.axis))
        if len(parts) == 1:
            return parts[0]
        if self.axis:
            return jnp.concatenate(parts, axis=0)
        parts = [p.reshape(span, unit, p.shape[1]) for p, unit in zip(parts, units)]
        joined = jnp.concatenate(parts, axis=1)
        return joined.reshape(-1, joined.shape[2])

    def side(self, color):
        return (self.mine >> self.orders[color][self.level]) & 1

    def ready(self):
        if self.level < self.count:
            self.out = [self.cut(color, 1 - self.side(color)) for color in range(2)]
        elif self.held is None:
            self.held = [[(self.state[color][0][0], 0)] for color in range(2)]

    def send(self):
        if self.level < self.count:
            self.got = [
                swap(self.out[color], "dp", self.orders[color][self.level])
                for color in range(2)
            ]
            return
        for color in range(2):
            bit = self.orders[color][2 * self.count - 1 - self.level]
            self.held[color] += [
                (swap(piece, "dp", bit), mask ^ (1 << bit)) for piece, mask in self.held[color]
            ]

    def arrive(self):
        if self.level < self.count:
            state = []
            for color in range(2):
                keep = self.cut(color, self.side(color))
                total = (keep.astype(F32) + self.got[color].astype(F32)).astype(BF16)
                whole = self.axis == 0 and not self.paired
                state.append(((total,), [sum(self.sizes) if whole else self.sizes[0]], 0))
            self.state = state
        self.level += 1
        self.ready()

    def moving(self):
        return self.out if self.held is None else self.held

    def fresh(self):
        return [held[len(held) // 2][0] for held in self.held]

    def result(self, write):
        pieces, colors, where = [], [], []
        for color in range(2):
            for piece, mask in self.held[color]:
                owner = self.mine ^ mask
                spot = 0 if self.paired else color
                for bit in self.orders[color]:
                    spot = spot * 2 + ((owner >> bit) & 1)
                pieces.append(piece)
                colors.append(color)
                where.append(spot)
        rows, columns = pieces[0].shape
        length, width = self.grads[0].shape
        if write is write_stacked:
            shapes = [(2, length, width)]
            blocks = [(1, rows, columns)]
        elif write is write_lanes:
            shapes = [(3, length, width // 3)]
            blocks = [(3, rows, columns // 3)]
        else:
            shapes = [g.shape for g in self.grads]
            blocks = [(rows * s[0] // sum(t[0] for t in shapes), columns) for s in shapes]
        lead = {write_stacked: lambda i, c: (c[i],), write_lanes: lambda i, c: (0,)}.get(
            write, lambda i, c: ()
        )

        def out_map(i, c, w):
            return lead(i, c) + ((w[i], 0) if self.axis == 0 else (0, w[i]))

        return place_blocks(
            write,
            jnp.array(colors, jnp.int32),
            jnp.stack(where).astype(jnp.int32),
            pieces,
            shapes,
            [pl.BlockSpec(block, out_map) for block in blocks],
        )


def fence(values, *sums):
    values, moving = lax.optimization_barrier((values, [item.moving() for item in sums]))
    for item, arrived in zip(sums, moving):
        if item.held is None:
            item.out = arrived
        else:
            item.held = arrived
    return values


def sum_small(values, name, bits=None):
    count = bits_of(name)
    if count is None:
        return lax.psum(values, name) if bits is None or 0 in bits else values
    for bit in range(count) if bits is None else bits:
        values = values + swap(values, name, bit)
    return values


def tail_kernel(x_ref, g_ref, c_ref, gain_ref, stat_ref, grad_ref, sums_ref):
    @pl.when(pl.program_id(0) == 0)
    def _():
        sums_ref[...] = jnp.zeros_like(sums_ref)
        sums_ref[2:3, :] = stat_ref[...]

    residual = x_ref[...].astype(F32)
    centered = residual - jnp.mean(residual, -1, keepdims=True)
    inv_std = lax.rsqrt(jnp.mean(centered * centered, -1, keepdims=True) + EPSILON)
    normalized = centered * inv_std
    grads = g_ref[...].astype(F32)
    sums_ref[0:1, :] += jnp.sum(grads * normalized, axis=0, keepdims=True)
    sums_ref[1:2, :] += jnp.sum(grads, axis=0, keepdims=True)
    scaled = grads * gain_ref[...]
    grad_ref[:, 0, :] = (
        inv_std
        * (
            scaled
            - jnp.mean(scaled, -1, keepdims=True)
            - normalized * jnp.mean(scaled * normalized, -1, keepdims=True)
        )
        + c_ref[...].astype(F32)
    )


def tail(layer_in, grad_normed, cot_here, norm_gain, stat_row):
    length, width = layer_in.shape
    rows = min(64, length)
    row_spec = pl.BlockSpec((rows, width), lambda i: (i, 0))
    one_spec = pl.BlockSpec((1, width), lambda i: (0, 0))
    return pl.pallas_call(
        tail_kernel,
        grid=(length // rows,),
        in_specs=[row_spec, row_spec, row_spec, one_spec, one_spec],
        out_specs=[
            pl.BlockSpec((rows, 1, width), lambda i: (i, 0, 0)),
            pl.BlockSpec((4, width), lambda i: (0, 0)),
        ],
        out_shape=[
            jax.ShapeDtypeStruct((length, 1, width), F32),
            jax.ShapeDtypeStruct((4, width), F32),
        ],
        name="tail",
    )(layer_in, grad_normed, cot_here, norm_gain.reshape(1, width), stat_row)


def back_products_kernel(p_ref, q_ref, g_ref, u_ref, w_ref, out_ref):
    turned = (((1,), (1,)), ((), ()))
    columns = q_ref.shape[2]
    total = jnp.dot(g_ref[...], w_ref[0], preferred_element_type=F32)
    total += jnp.dot(u_ref[...], w_ref[1], preferred_element_type=F32)
    for number in range(3):
        total += lax.dot_general(
            p_ref[:, number * columns : (number + 1) * columns],
            q_ref[number],
            turned,
            preferred_element_type=F32,
        )
    out_ref[...] = total.astype(BF16)


def back_products(grad_proj, w_qkv, grad_gate, grad_up, w_gate_up):
    length = grad_proj.shape[0]
    _, width, columns = w_qkv.shape
    hidden = grad_gate.shape[1]
    rows = min(256, length)
    return pl.pallas_call(
        back_products_kernel,
        grid=(length // rows,),
        in_specs=[
            pl.BlockSpec((rows, 3 * columns), lambda i: (i, 0)),
            pl.BlockSpec(w_qkv.shape, lambda i: (0, 0, 0)),
            pl.BlockSpec((rows, hidden), lambda i: (i, 0)),
            pl.BlockSpec((rows, hidden), lambda i: (i, 0)),
            pl.BlockSpec(w_gate_up.shape, lambda i: (0, 0, 0)),
        ],
        out_specs=pl.BlockSpec((rows, width), lambda i: (i, 0)),
        out_shape=jax.ShapeDtypeStruct((length, width), BF16),
        name="back_products",
    )(grad_proj, w_qkv, grad_gate, grad_up, w_gate_up)


def local(
    layer_in,
    segment_ids,
    valid_counts,
    norm_gain,
    norm_shift,
    w_qkv,
    b_qkv,
    w_out,
    w_gate_up,
    w_down,
    out_grad,
):
    local_len, row_count, model_width = layer_in.shape
    assert row_count == 1
    seq_len = local_len * lax.axis_size("mp")
    col_qkv = w_qkv.shape[2]
    ff_local = w_gate_up.shape[2]
    layer_in = layer_in[:, 0]
    position_here = lax.axis_index("mp") * local_len + jnp.arange(local_len, dtype=jnp.int32)
    valid_here = (position_here < valid_counts[0]).astype(F32)

    residual = layer_in.astype(F32)
    centered = residual - jnp.mean(residual, -1, keepdims=True)
    inv_std = lax.rsqrt(jnp.mean(centered * centered, -1, keepdims=True) + EPSILON)
    normalized = centered * inv_std
    normed = (normalized * norm_gain + norm_shift).astype(BF16)
    cot_here = jnp.where(valid_here[:, None] > 0, out_grad[:, 0], jnp.zeros((), BF16))
    gathered = lax.all_gather(normed, "mp", axis=0, tiled=True)
    cotangent = lax.all_gather(cot_here, "mp", axis=0, tiled=True)

    w_qkv = jnp.transpose(w_qkv, (1, 0, 2))
    w_gate_up = jnp.transpose(w_gate_up, (1, 2, 0))
    starts = starts_of(segment_ids)[0]
    tables = rotary_lanes(jnp.arange(seq_len, dtype=jnp.int32) - starts)
    start_blocks = starts.reshape(seq_len // BQ, 1, BQ)
    first = start_blocks[:, 0, 0] // BK
    gathered, tables, first, start_blocks = lax.optimization_barrier(
        (gathered, tables, first, start_blocks)
    )

    def product(left, right):
        return jnp.dot(left, right, preferred_element_type=F32).astype(BF16)

    def turned_product(left, right):
        return lax.dot_general(
            left, right, (((1,), (1,)), ((), ())), preferred_element_type=F32
        )

    def token_sum(left, right):
        return lax.dot_general(
            left, right, (((0,), (0,)), ((), ())), preferred_element_type=F32
        ).astype(BF16)

    def scattered(partial):
        return lax.psum_scatter(partial, "mp", scatter_dimension=0, tiled=True)

    gate = turned_product(gathered, w_gate_up[0])
    up = turned_product(gathered, w_gate_up[1])
    sigmoid_gate = jax.nn.sigmoid(gate)
    hidden = (gate * sigmoid_gate * up).astype(BF16)
    mlp_partial = product(hidden, w_down)
    mlp_sum = scattered(mlp_partial)
    gathered_next, mlp_partial = lax.optimization_barrier((gathered, mlp_partial))
    queries, key_rows, value_rows = project(gathered_next, w_qkv, b_qkv, tables)
    attended, lse = attend(first, queries, key_rows, value_rows, start_blocks)
    attn_partial = product(attended, w_out)
    attn_sum = scattered(attn_partial)

    cotangent, attn_partial = lax.optimization_barrier((cotangent, attn_partial))
    sum_down = DpSum(token_sum(hidden, cotangent), token_sum(attended, cotangent))
    cotangent = fence(cotangent, sum_down)
    sum_down.send()
    grad_hid = turned_product(cotangent, w_down).astype(BF16).astype(F32)
    grad_gate = (
        grad_hid * up * sigmoid_gate * (1.0 + gate * (1.0 - sigmoid_gate))
    ).astype(BF16)
    grad_up = (grad_hid * gate * sigmoid_gate).astype(BF16)
    grad_att = turned_product(cotangent, w_out).astype(BF16)
    sum_down.arrive()
    grad_gate, grad_up, grad_att = fence((grad_gate, grad_up, grad_att), sum_down)
    sum_down.send()
    sum_gate = token_sum(grad_gate, gathered)
    sum_down.arrive()
    sum_gate, grad_up = fence((sum_gate, grad_up), sum_down)
    sum_down.send()
    sum_gate_up = DpSum(sum_gate, token_sum(grad_up, gathered), paired=True)
    sum_down.arrive()
    grad_att = fence(grad_att, sum_gate_up, sum_down)
    sum_gate_up.send()
    sum_down.send()
    fresh = sum_down.fresh()
    grad_proj = attend_back(
        first, queries, key_rows, value_rows, grad_att, attended, lse, start_blocks, tables
    )
    sum_gate_up.arrive()
    sum_down.arrive()
    grad_proj, mlp_sum, _ = fence((grad_proj, mlp_sum, fresh), sum_gate_up)
    sum_gate_up.send()
    normed_partial = back_products(grad_proj, w_qkv, grad_gate, grad_up, w_gate_up)
    while sum_down.level < 2 * sum_down.count:
        sum_down.send()
        sum_down.arrive()
    sum_gate_up.arrive()
    grad_proj, normed_partial = fence((grad_proj, normed_partial), sum_gate_up, sum_down)
    sum_gate_up.send()
    sum_qkv = token_sum(gathered, grad_proj)
    sum_gate_up.arrive()
    sum_qkv = DpSum(fence(sum_qkv, sum_gate_up))
    bias_sums = jnp.sum(grad_proj, axis=0, dtype=F32).reshape(-1, 128)
    normed_partial, attn_sum, bias_sums, _ = fence(
        (normed_partial, attn_sum, bias_sums, sum_qkv.out)
    )
    grad_normed = scattered(normed_partial)
    sum_qkv.send()
    sum_qkv.arrive()
    fence((), sum_gate_up, sum_qkv)
    sum_gate_up.send()
    sum_qkv.send()
    bias_sums = sum_small(bias_sums, "dp", [0])
    mlp_part = mlp_sum.astype(F32)
    attn_part = attn_sum.astype(F32)
    layer_out = (residual + attn_part + mlp_part).astype(BF16)
    statistics = jnp.stack(
        [
            jnp.sum(valid_here * jnp.sum(residual * residual, -1)),
            jnp.sum(valid_here * jnp.sum(attn_part * attn_part, -1)),
            jnp.sum(valid_here * jnp.sum(mlp_part * mlp_part, -1)),
            jnp.sum(valid_here),
        ]
    )
    stat_row = jnp.pad(statistics, (0, model_width - 4)).reshape(1, model_width)
    fresh = sum_gate_up.fresh()
    sum_gate_up.arrive()
    sum_qkv.arrive()
    bias_sums, layer_out, stat_row, _ = fence((bias_sums, layer_out, stat_row, fresh), sum_qkv)
    sum_qkv.send()
    bias_sums = sum_small(bias_sums, "dp", range(1, sum_qkv.count))
    down_sums = sum_down.result(write_rows)
    sum_qkv.arrive()
    while sum_gate_up.level < 2 * sum_gate_up.count:
        sum_gate_up.send()
        sum_gate_up.arrive()
    down_sums, bias_sums = fence((down_sums, bias_sums), sum_gate_up, sum_qkv)
    while sum_qkv.level < 2 * sum_qkv.count:
        sum_qkv.send()
        sum_qkv.arrive()
    (grad_w_gate_up,) = sum_gate_up.result(write_stacked)
    grad_w_gate_up = fence(grad_w_gate_up, sum_qkv)
    (grad_w_qkv,) = sum_qkv.result(write_lanes)
    grad_w_down, grad_w_out = down_sums
    grad_normed, grad_w_gate_up, grad_w_qkv = fence(
        (grad_normed, grad_w_gate_up, grad_w_qkv)
    )
    input_grad, small = tail(layer_in, grad_normed, cot_here, norm_gain, stat_row)
    small = sum_small(sum_small(small, "mp"), "dp")
    totals = small[2]
    return (
        layer_out[:, None],
        input_grad,
        small[0],
        small[1],
        jnp.transpose(grad_w_qkv, (1, 0, 2)),
        bias_sums.reshape(3, col_qkv),
        grad_w_out,
        jnp.transpose(grad_w_gate_up, (2, 0, 1)),
        grad_w_down,
        jnp.sqrt(totals[:3] / (totals[3] * model_width)),
    )


def solution(mesh):
    placed = (
        P("mp", "dp", None),
        P("dp", None),
        P("dp"),
        P(),
        P(),
        P(None, None, "mp"),
        P(None, "mp"),
        P("mp", None),
        P(None, None, "mp"),
        P("mp", None),
        P("mp", "dp", None),
    )
    return jax.shard_map(
        local,
        mesh=mesh,
        in_specs=placed,
        out_specs=(
            P("mp", "dp", None),
            P("mp", "dp", None),
            P(),
            P(),
            P(None, None, "mp"),
            P(None, "mp"),
            P("mp", None),
            P(None, None, "mp"),
            P("mp", None),
            P(),
        ),
        check_vma=False,
    )
```

```python
import functools

import jax
import jax.numpy as jnp
from jax import lax
from jax.experimental import pallas as pl
from jax.experimental.pallas import tpu as pltpu
from jax.sharding import PartitionSpec as P

HEAD_DIM = 64
ROT = 16
EPSILON = 1e-05
BQ = 128
BK = 256
NEG = -1e30
F32 = jnp.float32
BF16 = jnp.bfloat16


def starts_of(segment_ids):
    length = segment_ids.shape[1]
    steps_all = jnp.arange(length, dtype=jnp.int32)[None, :]
    change = jnp.concatenate(
        [
            jnp.ones_like(segment_ids[:, :1]),
            (segment_ids[:, 1:] != segment_ids[:, :-1]).astype(jnp.int32),
        ],
        axis=1,
    )
    return lax.cummax(jnp.where(change > 0, steps_all, jnp.zeros_like(change)), axis=1)


def rotary_lanes(positions):
    half_rot = ROT // 2
    lane = jnp.arange(2 * HEAD_DIM, dtype=jnp.int32) % HEAD_DIM
    power = (lane % half_rot).astype(F32)
    frequency = jnp.where(lane < ROT, 10000.0 ** (-(power * 2.0) / ROT), 0.0)
    angles = positions.astype(F32)[:, None] * frequency
    sine = jnp.sin(angles)
    low = jnp.where(lane < half_rot, -sine, 0.0)
    high = jnp.where((lane >= half_rot) & (lane < ROT), sine, 0.0)
    return jnp.cos(angles), low, high


def lane_tile(table, columns):
    return jnp.concatenate([table] * (columns // table.shape[1]), axis=1)


def turn(values, cosine, low, high):
    columns = values.shape[1]
    half_rot = ROT // 2
    return (
        values * lane_tile(cosine, columns)
        + pltpu.roll(values, columns - half_rot, 1) * lane_tile(low, columns)
        + pltpu.roll(values, half_rot, 1) * lane_tile(high, columns)
    )


def project_kernel(x_ref, w_ref, b_ref, cos_ref, low_ref, high_ref, q_ref, k_ref, v_ref):
    tables = (cos_ref[...], low_ref[...], high_ref[...])

    def part(number):
        flat = jnp.dot(x_ref[...], w_ref[number], preferred_element_type=F32)
        return flat + b_ref[number : number + 1, :].astype(F32)

    queries = turn(part(0), *tables).astype(BF16)
    q_ref[...] = (queries.astype(F32) * HEAD_DIM**-0.5).astype(BF16)
    k_ref[...] = turn(part(1), *tables).astype(BF16)
    v_ref[...] = part(2).astype(BF16)


def project(gathered, w_qkv, b_qkv, tables):
    length, width = gathered.shape
    columns = w_qkv.shape[2]
    rows = min(256, length)
    table_spec = pl.BlockSpec((rows, tables[0].shape[1]), lambda i: (i, 0))
    out_spec = pl.BlockSpec((rows, columns), lambda i: (i, 0))
    return pl.pallas_call(
        project_kernel,
        grid=(length // rows,),
        in_specs=[
            pl.BlockSpec((rows, width), lambda i: (i, 0)),
            pl.BlockSpec(w_qkv.shape, lambda i: (0, 0, 0)),
            pl.BlockSpec(b_qkv.shape, lambda i: (0, 0)),
            table_spec,
            table_spec,
            table_spec,
        ],
        out_specs=[out_spec] * 3,
        out_shape=[jax.ShapeDtypeStruct((length, columns), BF16)] * 3,
        cost_estimate=pl.CostEstimate(
            flops=6 * length * width * columns,
            bytes_accessed=2 * (length * width + 3 * width * columns + 3 * length * columns),
            transcendentals=0,
        ),
        name="project",
    )(gathered, w_qkv, b_qkv, *tables)


def stack_heads(block):
    columns = block.shape[1]
    head_of = lax.broadcasted_iota(jnp.int32, block.shape, 1) // HEAD_DIM
    return jnp.concatenate(
        [
            jnp.where(head_of == head, block, jnp.zeros_like(block))
            for head in range(columns // HEAD_DIM)
        ],
        axis=0,
    )


def unstack_heads(stacked, block):
    heads = stacked.shape[1] // block
    return jnp.concatenate(
        [
            stacked[head * HEAD_DIM : (head + 1) * HEAD_DIM, head * block : (head + 1) * block]
            for head in range(heads)
        ],
        axis=0,
    ).T


def score_block(key_block, stacked_queries, key_at, start_row, query_row):
    scores = lax.dot_general(
        key_block, stacked_queries, (((1,), (1,)), ((), ())), preferred_element_type=F32
    )
    key_pos = key_at + lax.broadcasted_iota(jnp.int32, scores.shape, 0)
    allowed = (key_pos >= start_row) & (key_pos <= query_row)
    return scores, allowed


def query_rows(start_ref, block, heads):
    start_row = jnp.concatenate([start_ref[0]] * heads, axis=1)
    query_row = pl.program_id(0) * block + lax.broadcasted_iota(jnp.int32, (1, block), 1)
    return start_row, jnp.concatenate([query_row] * heads, axis=1)


def attend_kernel(first_ref, q_ref, k_ref, v_ref, start_ref, o_ref, lse_ref, acc_ref):
    block, columns = q_ref.shape
    heads = columns // HEAD_DIM
    index = pl.program_id(0)
    stacked = stack_heads(q_ref[...])
    start_row, query_row = query_rows(start_ref, block, heads)
    acc_ref[...] = jnp.zeros_like(acc_ref)

    def body(step, carry):
        highest, total = carry
        at = pl.multiple_of(step * BK, BK)
        scores, allowed = score_block(
            k_ref[pl.ds(at, BK), :], stacked, at, start_row, query_row
        )
        scores = jnp.where(allowed, scores, NEG)
        newest = jnp.maximum(highest, jnp.max(scores, axis=0, keepdims=True))
        weights = jnp.exp(scores - newest)
        scale = jnp.exp(highest - newest)
        total = total * scale + jnp.sum(weights, axis=0, keepdims=True)
        acc_ref[...] = acc_ref[...] * scale + lax.dot_general(
            v_ref[pl.ds(at, BK), :],
            weights.astype(BF16),
            (((0,), (0,)), ((), ())),
            preferred_element_type=F32,
        )
        return newest, total

    highest, total = lax.fori_loop(
        first_ref[index],
        (index * block + block - 1) // BK + 1,
        body,
        (jnp.full((1, heads * block), NEG, F32), jnp.zeros((1, heads * block), F32)),
    )
    o_ref[...] = unstack_heads(acc_ref[...] / total, block).astype(BF16)
    lse_ref[0] = highest + jnp.log(total)


def attend(first, queries, key_rows, value_rows, start_blocks):
    length, columns = queries.shape
    blocks = length // BQ
    heads = columns // HEAD_DIM
    row_spec = pl.BlockSpec((BQ, columns), lambda i, f: (i, 0))
    whole = pl.BlockSpec((length, columns), lambda i, f: (0, 0))
    return pl.pallas_call(
        attend_kernel,
        grid_spec=pltpu.PrefetchScalarGridSpec(
            num_scalar_prefetch=1,
            grid=(blocks,),
            in_specs=[
                row_spec,
                whole,
                whole,
                pl.BlockSpec((1, 1, BQ), lambda i, f: (i, 0, 0)),
            ],
            out_specs=[
                row_spec,
                pl.BlockSpec((1, 1, heads * BQ), lambda i, f: (i, 0, 0)),
            ],
            scratch_shapes=[pltpu.VMEM((columns, heads * BQ), F32)],
        ),
        out_shape=[
            jax.ShapeDtypeStruct((length, columns), BF16),
            jax.ShapeDtypeStruct((blocks, 1, heads * BQ), F32),
        ],
        cost_estimate=pl.CostEstimate(
            flops=4 * length * 1024 * columns * heads,
            bytes_accessed=8 * length * columns,
            transcendentals=length * 1024 * heads,
        ),
        name="attend",
    )(first, queries, key_rows, value_rows, start_blocks)


def attend_back_kernel(
    first_ref,
    q_ref,
    k_ref,
    v_ref,
    do_ref,
    o_ref,
    lse_ref,
    start_ref,
    cos_ref,
    low_ref,
    high_ref,
    grad_ref,
    key_acc,
    value_acc,
    query_acc,
):
    block, columns = q_ref.shape
    heads = columns // HEAD_DIM
    length = k_ref.shape[0]
    index = pl.program_id(0)

    @pl.when(index == 0)
    def _():
        key_acc[...] = jnp.zeros_like(key_acc)
        value_acc[...] = jnp.zeros_like(value_acc)

    stacked = stack_heads(q_ref[...])
    stacked_do = stack_heads(do_ref[...])
    start_row, query_row = query_rows(start_ref, block, heads)
    lse_row = lse_ref[0]
    products = do_ref[...].astype(F32) * o_ref[...].astype(F32)
    head_rows = lax.broadcasted_iota(jnp.int32, (8, columns), 0)
    head_lanes = lax.broadcasted_iota(jnp.int32, (8, columns), 1) // HEAD_DIM
    picked = lax.dot_general(
        (head_rows == head_lanes).astype(F32),
        products,
        (((1,), (1,)), ((), ())),
        precision=lax.Precision.HIGHEST,
        preferred_element_type=F32,
    )
    inner_row = jnp.concatenate([picked[head : head + 1, :] for head in range(heads)], axis=1)
    query_acc[...] = jnp.zeros_like(query_acc)

    def body(step, carry):
        at = pl.multiple_of(step * BK, BK)
        key_block = k_ref[pl.ds(at, BK), :]
        scores, allowed = score_block(key_block, stacked, at, start_row, query_row)
        weights = jnp.where(allowed, jnp.exp(scores - lse_row), 0.0)
        grad_weights = lax.dot_general(
            v_ref[pl.ds(at, BK), :],
            stacked_do,
            (((1,), (1,)), ((), ())),
            preferred_element_type=F32,
        )
        grad_scores = (weights * (grad_weights - inner_row)).astype(BF16)
        value_acc[pl.ds(at, BK), :] += jnp.dot(
            weights.astype(BF16), stacked_do, preferred_element_type=F32
        )
        key_acc[pl.ds(at, BK), :] += jnp.dot(grad_scores, stacked, preferred_element_type=F32)
        query_acc[...] += lax.dot_general(
            key_block, grad_scores, (((0,), (0,)), ((), ())), preferred_element_type=F32
        )
        return carry

    lax.fori_loop(first_ref[index], (index * block + block - 1) // BK + 1, body, 0)

    def turn_back(grads, at, rows):
        kept = grads.astype(BF16).astype(F32)
        return turn(
            kept,
            cos_ref[pl.ds(at, rows), :],
            -low_ref[pl.ds(at, rows), :],
            -high_ref[pl.ds(at, rows), :],
        ).astype(BF16)

    at_query = pl.multiple_of(index * block, block)
    grad_ref[pl.ds(at_query, block), :columns] = turn_back(
        unstack_heads(query_acc[...], block) * HEAD_DIM**-0.5, at_query, block
    )

    @pl.when(index == pl.num_programs(0) - 1)
    def _():
        def finish(step, carry):
            at = pl.multiple_of(step * BK, BK)
            grad_ref[pl.ds(at, BK), columns : 2 * columns] = turn_back(
                key_acc[pl.ds(at, BK), :], at, BK
            )
            grad_ref[pl.ds(at, BK), 2 * columns :] = value_acc[pl.ds(at, BK), :].astype(BF16)
            return carry

        lax.fori_loop(0, length // BK, finish, 0)


def attend_back(first, queries, key_rows, value_rows, grad_att, attended, lse, start_blocks, tables):
    length, columns = queries.shape
    blocks = length // BQ
    heads = columns // HEAD_DIM
    row_spec = pl.BlockSpec((BQ, columns), lambda i, f: (i, 0))
    whole = pl.BlockSpec((length, columns), lambda i, f: (0, 0))
    table_spec = pl.BlockSpec(tables[0].shape, lambda i, f: (0, 0))
    return pl.pallas_call(
        attend_back_kernel,
        grid_spec=pltpu.PrefetchScalarGridSpec(
            num_scalar_prefetch=1,
            grid=(blocks,),
            in_specs=[
                row_spec,
                whole,
                whole,
                row_spec,
                row_spec,
                pl.BlockSpec((1, 1, heads * BQ), lambda i, f: (i, 0, 0)),
                pl.BlockSpec((1, 1, BQ), lambda i, f: (i, 0, 0)),
                table_spec,
                table_spec,
                table_spec,
            ],
            out_specs=pl.BlockSpec((length, 3 * columns), lambda i, f: (0, 0)),
            scratch_shapes=[
                pltpu.VMEM((length, columns), F32),
                pltpu.VMEM((length, columns), F32),
                pltpu.VMEM((columns, heads * BQ), F32),
            ],
        ),
        out_shape=jax.ShapeDtypeStruct((length, 3 * columns), BF16),
        cost_estimate=pl.CostEstimate(
            flops=10 * length * 1024 * columns * heads,
            bytes_accessed=16 * length * columns,
            transcendentals=length * 1024 * heads,
        ),
        name="attend_back",
    )(first, queries, key_rows, value_rows, grad_att, attended, lse, start_blocks, *tables)


def bits_of(name):
    size = lax.axis_size(name)
    count = size.bit_length() - 1
    return count if size == 1 << count else None


def swap(values, name, bit):
    size = lax.axis_size(name)
    return lax.ppermute(values, name, [(i, i ^ (1 << bit)) for i in range(size)])


def write_stacked(piece, outs):
    outs[0][0] = piece.astype(F32)


def write_rows(piece, outs):
    at = 0
    for out_ref in outs:
        size = out_ref.shape[0]
        out_ref[...] = piece[at : at + size, :].astype(F32)
        at += size


def write_lanes(piece, outs):
    parts, _, size = outs[0].shape
    for part in range(parts):
        outs[0][part] = piece[:, part * size : (part + 1) * size].astype(F32)


def place_kernel(write, count, color_ref, where_ref, *refs):
    step = pl.program_id(0)
    for number in range(count):

        @pl.when(step == number)
        def _(number=number):
            write(refs[number][...], refs[count:])


def place_blocks(write, color, where, pieces, out_shapes, out_specs):
    rows, columns = pieces[0].shape
    count = len(pieces)
    return pl.pallas_call(
        functools.partial(place_kernel, write, count),
        grid_spec=pltpu.PrefetchScalarGridSpec(
            num_scalar_prefetch=2,
            grid=(count,),
            in_specs=[pl.BlockSpec((rows, columns), lambda i, c, w: (0, 0))] * count,
            out_specs=out_specs,
        ),
        out_shape=[jax.ShapeDtypeStruct(shape, F32) for shape in out_shapes],
        cost_estimate=pl.CostEstimate(
            flops=0, bytes_accessed=6 * count * rows * columns, transcendentals=0
        ),
        name="place_blocks",
    )(color, where, *pieces)


class DpSum:
    def __init__(self, *grads, paired=False):
        self.grads = grads
        self.paired = paired
        self.count = bits_of("dp")
        pieces = (1 if paired else 2) << self.count
        self.axis = 0 if all(g.shape[0] % (8 * pieces) == 0 for g in grads) else 1
        self.sizes = [g.shape[self.axis] // pieces for g in grads]
        self.mine = lax.axis_index("dp")
        self.orders = [list(range(self.count)), list(range(self.count))[::-1]]
        self.level = 0
        if paired:
            self.state = [((grad,), self.sizes[:1], 0) for grad in grads]
        else:
            self.state = [(grads, self.sizes, color << self.count) for color in range(2)]
        self.held = None
        self.ready()

    def cut(self, color, side):
        grads, units, base = self.state[color]
        span = (1 << self.count) >> (self.level + 1)
        parts = []
        for grad, unit in zip(grads, units):
            at = (base + side * span) * unit
            parts.append(lax.dynamic_slice_in_dim(grad, at, span * unit, self.axis))
        if len(parts) == 1:
            return parts[0]
        if self.axis:
            return jnp.concatenate(parts, axis=0)
        parts = [p.reshape(span, unit, p.shape[1]) for p, unit in zip(parts, units)]
        joined = jnp.concatenate(parts, axis=1)
        return joined.reshape(-1, joined.shape[2])

    def side(self, color):
        return (self.mine >> self.orders[color][self.level]) & 1

    def ready(self):
        if self.level < self.count:
            self.out = [self.cut(color, 1 - self.side(color)) for color in range(2)]
        elif self.held is None:
            self.held = [[(self.state[color][0][0], 0)] for color in range(2)]

    def send(self):
        if self.level < self.count:
            self.got = [
                swap(self.out[color], "dp", self.orders[color][self.level])
                for color in range(2)
            ]
            return
        for color in range(2):
            bit = self.orders[color][2 * self.count - 1 - self.level]
            self.held[color] += [
                (swap(piece, "dp", bit), mask ^ (1 << bit)) for piece, mask in self.held[color]
            ]

    def arrive(self):
        if self.level < self.count:
            state = []
            for color in range(2):
                keep = self.cut(color, self.side(color))
                total = (keep.astype(F32) + self.got[color].astype(F32)).astype(BF16)
                whole = self.axis == 0 and not self.paired
                state.append(((total,), [sum(self.sizes) if whole else self.sizes[0]], 0))
            self.state = state
        self.level += 1
        self.ready()

    def moving(self):
        return self.out if self.held is None else self.held

    def fresh(self):
        return [held[len(held) // 2][0] for held in self.held]

    def result(self, write):
        pieces, colors, where = [], [], []
        for color in range(2):
            for piece, mask in self.held[color]:
                owner = self.mine ^ mask
                spot = 0 if self.paired else color
                for bit in self.orders[color]:
                    spot = spot * 2 + ((owner >> bit) & 1)
                pieces.append(piece)
                colors.append(color)
                where.append(spot)
        rows, columns = pieces[0].shape
        length, width = self.grads[0].shape
        if write is write_stacked:
            shapes = [(2, length, width)]
            blocks = [(1, rows, columns)]
        elif write is write_lanes:
            shapes = [(3, length, width // 3)]
            blocks = [(3, rows, columns // 3)]
        else:
            shapes = [g.shape for g in self.grads]
            blocks = [(rows * s[0] // sum(t[0] for t in shapes), columns) for s in shapes]
        lead = {write_stacked: lambda i, c: (c[i],), write_lanes: lambda i, c: (0,)}.get(
            write, lambda i, c: ()
        )

        def out_map(i, c, w):
            return lead(i, c) + ((w[i], 0) if self.axis == 0 else (0, w[i]))

        return place_blocks(
            write,
            jnp.array(colors, jnp.int32),
            jnp.stack(where).astype(jnp.int32),
            pieces,
            shapes,
            [pl.BlockSpec(block, out_map) for block in blocks],
        )


def fence(values, *sums):
    values, moving = lax.optimization_barrier((values, [item.moving() for item in sums]))
    for item, arrived in zip(sums, moving):
        if item.held is None:
            item.out = arrived
        else:
            item.held = arrived
    return values


def sum_small(values, name, bits=None):
    count = bits_of(name)
    if count is None:
        return lax.psum(values, name) if bits is None or 0 in bits else values
    for bit in range(count) if bits is None else bits:
        values = values + swap(values, name, bit)
    return values


def norm_kernel(x_ref, gain_ref, shift_ref, out_ref):
    residual = x_ref[...].astype(F32)
    centered = residual - jnp.mean(residual, -1, keepdims=True)
    inv_std = lax.rsqrt(jnp.mean(centered * centered, -1, keepdims=True) + EPSILON)
    out_ref[...] = (centered * inv_std * gain_ref[...] + shift_ref[...]).astype(BF16)


def norm(layer_in, norm_gain, norm_shift):
    length, width = layer_in.shape
    rows = min(64, length)
    row_spec = pl.BlockSpec((rows, width), lambda i: (i, 0))
    one_spec = pl.BlockSpec((1, width), lambda i: (0, 0))
    return pl.pallas_call(
        norm_kernel,
        grid=(length // rows,),
        in_specs=[row_spec, one_spec, one_spec],
        out_specs=row_spec,
        out_shape=jax.ShapeDtypeStruct((length, width), BF16),
        name="norm",
    )(layer_in, norm_gain.reshape(1, width), norm_shift.reshape(1, width))


def tail_kernel(x_ref, g_ref, c_ref, gain_ref, stat_ref, grad_ref, sums_ref):
    @pl.when(pl.program_id(0) == 0)
    def _():
        sums_ref[...] = jnp.zeros_like(sums_ref)
        sums_ref[2:3, :] = stat_ref[...]

    residual = x_ref[...].astype(F32)
    centered = residual - jnp.mean(residual, -1, keepdims=True)
    inv_std = lax.rsqrt(jnp.mean(centered * centered, -1, keepdims=True) + EPSILON)
    normalized = centered * inv_std
    grads = g_ref[...].astype(F32)
    sums_ref[0:1, :] += jnp.sum(grads * normalized, axis=0, keepdims=True)
    sums_ref[1:2, :] += jnp.sum(grads, axis=0, keepdims=True)
    scaled = grads * gain_ref[...]
    grad_ref[:, 0, :] = (
        inv_std
        * (
            scaled
            - jnp.mean(scaled, -1, keepdims=True)
            - normalized * jnp.mean(scaled * normalized, -1, keepdims=True)
        )
        + c_ref[...].astype(F32)
    )


def tail(layer_in, grad_normed, cot_here, norm_gain, stat_row):
    length, width = layer_in.shape
    rows = min(64, length)
    row_spec = pl.BlockSpec((rows, width), lambda i: (i, 0))
    one_spec = pl.BlockSpec((1, width), lambda i: (0, 0))
    return pl.pallas_call(
        tail_kernel,
        grid=(length // rows,),
        in_specs=[row_spec, row_spec, row_spec, one_spec, one_spec],
        out_specs=[
            pl.BlockSpec((rows, 1, width), lambda i: (i, 0, 0)),
            pl.BlockSpec((4, width), lambda i: (0, 0)),
        ],
        out_shape=[
            jax.ShapeDtypeStruct((length, 1, width), F32),
            jax.ShapeDtypeStruct((4, width), F32),
        ],
        name="tail",
    )(layer_in, grad_normed, cot_here, norm_gain.reshape(1, width), stat_row)


def back_products_kernel(p_ref, q_ref, g_ref, u_ref, w_ref, out_ref):
    turned = (((1,), (1,)), ((), ()))
    columns = q_ref.shape[2]
    total = jnp.dot(g_ref[...], w_ref[0], preferred_element_type=F32)
    total += jnp.dot(u_ref[...], w_ref[1], preferred_element_type=F32)
    for number in range(3):
        total += lax.dot_general(
            p_ref[:, number * columns : (number + 1) * columns],
            q_ref[number],
            turned,
            preferred_element_type=F32,
        )
    out_ref[...] = total.astype(BF16)


def back_products(grad_proj, w_qkv, grad_gate, grad_up, w_gate_up):
    length = grad_proj.shape[0]
    _, width, columns = w_qkv.shape
    hidden = grad_gate.shape[1]
    rows = min(256, length)
    return pl.pallas_call(
        back_products_kernel,
        grid=(length // rows,),
        in_specs=[
            pl.BlockSpec((rows, 3 * columns), lambda i: (i, 0)),
            pl.BlockSpec(w_qkv.shape, lambda i: (0, 0, 0)),
            pl.BlockSpec((rows, hidden), lambda i: (i, 0)),
            pl.BlockSpec((rows, hidden), lambda i: (i, 0)),
            pl.BlockSpec(w_gate_up.shape, lambda i: (0, 0, 0)),
        ],
        out_specs=pl.BlockSpec((rows, width), lambda i: (i, 0)),
        out_shape=jax.ShapeDtypeStruct((length, width), BF16),
        name="back_products",
    )(grad_proj, w_qkv, grad_gate, grad_up, w_gate_up)


def local(
    layer_in,
    segment_ids,
    valid_counts,
    norm_gain,
    norm_shift,
    w_qkv,
    b_qkv,
    w_out,
    w_gate_up,
    w_down,
    out_grad,
):
    local_len, row_count, model_width = layer_in.shape
    assert row_count == 1
    seq_len = local_len * lax.axis_size("mp")
    col_qkv = w_qkv.shape[2]
    ff_local = w_gate_up.shape[2]
    layer_in = layer_in[:, 0]
    position_here = lax.axis_index("mp") * local_len + jnp.arange(local_len, dtype=jnp.int32)
    valid_here = (position_here < valid_counts[0]).astype(F32)

    residual = layer_in.astype(F32)
    normed = norm(layer_in, norm_gain, norm_shift)
    cot_here = jnp.where(valid_here[:, None] > 0, out_grad[:, 0], jnp.zeros((), BF16))
    gathered = lax.all_gather(normed, "mp", axis=0, tiled=True)
    cotangent = lax.all_gather(cot_here, "mp", axis=0, tiled=True)

    w_qkv = jnp.transpose(w_qkv, (1, 0, 2))
    w_gate_up = jnp.transpose(w_gate_up, (1, 2, 0))
    starts = starts_of(segment_ids)[0]
    tables = rotary_lanes(jnp.arange(seq_len, dtype=jnp.int32) - starts)
    start_blocks = starts.reshape(seq_len // BQ, 1, BQ)
    first = start_blocks[:, 0, 0] // BK
    gathered, tables, first, start_blocks = lax.optimization_barrier(
        (gathered, tables, first, start_blocks)
    )

    def product(left, right):
        return jnp.dot(left, right, preferred_element_type=F32).astype(BF16)

    def turned_product(left, right):
        return lax.dot_general(
            left, right, (((1,), (1,)), ((), ())), preferred_element_type=F32
        )

    def token_sum(left, right):
        return lax.dot_general(
            left, right, (((0,), (0,)), ((), ())), preferred_element_type=F32
        ).astype(BF16)

    def scattered(partial):
        return lax.psum_scatter(partial, "mp", scatter_dimension=0, tiled=True)

    gate = turned_product(gathered, w_gate_up[0])
    up = turned_product(gathered, w_gate_up[1])
    sigmoid_gate = jax.nn.sigmoid(gate)
    hidden = (gate * sigmoid_gate * up).astype(BF16)
    mlp_partial = product(hidden, w_down)
    mlp_sum = scattered(mlp_partial)
    gathered_next, mlp_partial = lax.optimization_barrier((gathered, mlp_partial))
    queries, key_rows, value_rows = project(gathered_next, w_qkv, b_qkv, tables)
    attended, lse = attend(first, queries, key_rows, value_rows, start_blocks)
    attn_partial = product(attended, w_out)
    attn_sum = scattered(attn_partial)

    cotangent, attn_partial = lax.optimization_barrier((cotangent, attn_partial))
    sum_down = DpSum(token_sum(hidden, cotangent), token_sum(attended, cotangent))
    cotangent = fence(cotangent, sum_down)
    sum_down.send()
    grad_hid = turned_product(cotangent, w_down).astype(BF16).astype(F32)
    grad_gate = (
        grad_hid * up * sigmoid_gate * (1.0 + gate * (1.0 - sigmoid_gate))
    ).astype(BF16)
    grad_up = (grad_hid * gate * sigmoid_gate).astype(BF16)
    grad_att = turned_product(cotangent, w_out).astype(BF16)
    sum_down.arrive()
    grad_gate, grad_up, grad_att = fence((grad_gate, grad_up, grad_att), sum_down)
    sum_down.send()
    sum_gate = token_sum(grad_gate, gathered)
    sum_down.arrive()
    sum_gate, grad_up = fence((sum_gate, grad_up), sum_down)
    sum_down.send()
    sum_gate_up = DpSum(sum_gate, token_sum(grad_up, gathered), paired=True)
    sum_down.arrive()
    grad_att = fence(grad_att, sum_gate_up, sum_down)
    sum_gate_up.send()
    sum_down.send()
    fresh = sum_down.fresh()
    grad_proj = attend_back(
        first, queries, key_rows, value_rows, grad_att, attended, lse, start_blocks, tables
    )
    sum_gate_up.arrive()
    sum_down.arrive()
    grad_proj, mlp_sum, _ = fence((grad_proj, mlp_sum, fresh), sum_gate_up)
    sum_gate_up.send()
    sum_qkv = token_sum(gathered, grad_proj)
    while sum_down.level < 2 * sum_down.count:
        sum_down.send()
        sum_down.arrive()
    sum_gate_up.arrive()
    sum_qkv = DpSum(sum_qkv)
    grad_proj = fence(grad_proj, sum_gate_up, sum_down, sum_qkv)
    sum_qkv.send()
    sum_gate_up.send()
    normed_partial = back_products(grad_proj, w_qkv, grad_gate, grad_up, w_gate_up)
    bias_sums = jnp.sum(grad_proj, axis=0, dtype=F32).reshape(-1, 128)
    sum_gate_up.arrive()
    sum_qkv.got = fence(sum_qkv.got, sum_gate_up)
    sum_qkv.arrive()
    normed_partial, attn_sum = fence((normed_partial, attn_sum), sum_qkv)
    grad_normed = scattered(normed_partial)
    sum_gate_up.send()
    sum_qkv.send()
    mlp_part = mlp_sum.astype(F32)
    attn_part = attn_sum.astype(F32)
    layer_out = (residual + attn_part + mlp_part).astype(BF16)
    statistics = jnp.stack(
        [
            jnp.sum(valid_here * jnp.sum(residual * residual, -1)),
            jnp.sum(valid_here * jnp.sum(attn_part * attn_part, -1)),
            jnp.sum(valid_here * jnp.sum(mlp_part * mlp_part, -1)),
            jnp.sum(valid_here),
        ]
    )
    stat_row = jnp.pad(statistics, (0, model_width - 4)).reshape(1, model_width)
    fresh = sum_gate_up.fresh()
    sum_gate_up.arrive()
    sum_qkv.arrive()
    bias_sums, layer_out, stat_row, _ = fence((bias_sums, layer_out, stat_row, fresh), sum_qkv)
    bias_sums = sum_small(bias_sums, "dp", [0])
    sum_qkv.send()
    down_sums = sum_down.result(write_rows)
    sum_qkv.arrive()
    while sum_gate_up.level < 2 * sum_gate_up.count:
        sum_gate_up.send()
        sum_gate_up.arrive()
    down_sums, bias_sums = fence((down_sums, bias_sums), sum_gate_up, sum_qkv)
    while sum_qkv.level < 2 * sum_qkv.count:
        sum_qkv.send()
        sum_qkv.arrive()
    (grad_w_gate_up,) = sum_gate_up.result(write_stacked)
    bias_sums = sum_small(bias_sums, "dp", range(1, sum_qkv.count))
    grad_w_gate_up, bias_sums = fence((grad_w_gate_up, bias_sums), sum_qkv)
    (grad_w_qkv,) = sum_qkv.result(write_lanes)
    grad_w_down, grad_w_out = down_sums
    grad_normed, grad_w_gate_up, grad_w_qkv = fence(
        (grad_normed, grad_w_gate_up, grad_w_qkv)
    )
    input_grad, small = tail(layer_in, grad_normed, cot_here, norm_gain, stat_row)
    small = sum_small(sum_small(small, "mp"), "dp")
    totals = small[2]
    return (
        layer_out[:, None],
        input_grad,
        small[0],
        small[1],
        jnp.transpose(grad_w_qkv, (1, 0, 2)),
        bias_sums.reshape(3, col_qkv),
        grad_w_out,
        jnp.transpose(grad_w_gate_up, (2, 0, 1)),
        grad_w_down,
        jnp.sqrt(totals[:3] / (totals[3] * model_width)),
    )


def solution(mesh):
    placed = (
        P("mp", "dp", None),
        P("dp", None),
        P("dp"),
        P(),
        P(),
        P(None, None, "mp"),
        P(None, "mp"),
        P("mp", None),
        P(None, None, "mp"),
        P("mp", None),
        P("mp", "dp", None),
    )
    return jax.shard_map(
        local,
        mesh=mesh,
        in_specs=placed,
        out_specs=(
            P("mp", "dp", None),
            P("mp", "dp", None),
            P(),
            P(),
            P(None, None, "mp"),
            P(None, "mp"),
            P("mp", None),
            P(None, None, "mp"),
            P("mp", None),
            P(),
        ),
        check_vma=False,
    )
```

```python
import functools

import jax
import jax.numpy as jnp
from jax import lax
from jax.experimental import pallas as pl
from jax.experimental.pallas import tpu as pltpu
from jax.sharding import PartitionSpec as P

HEAD_DIM = 64
ROT = 16
EPSILON = 1e-05
BQ = 128
BK = 256
NEG = -1e30
F32 = jnp.float32
BF16 = jnp.bfloat16


def starts_of(segment_ids):
    length = segment_ids.shape[1]
    steps_all = jnp.arange(length, dtype=jnp.int32)[None, :]
    change = jnp.concatenate(
        [
            jnp.ones_like(segment_ids[:, :1]),
            (segment_ids[:, 1:] != segment_ids[:, :-1]).astype(jnp.int32),
        ],
        axis=1,
    )
    return lax.cummax(jnp.where(change > 0, steps_all, jnp.zeros_like(change)), axis=1)


def rotary_lanes(positions):
    half_rot = ROT // 2
    lane = jnp.arange(2 * HEAD_DIM, dtype=jnp.int32) % HEAD_DIM
    power = (lane % half_rot).astype(F32)
    frequency = jnp.where(lane < ROT, 10000.0 ** (-(power * 2.0) / ROT), 0.0)
    angles = positions.astype(F32)[:, None] * frequency
    sine = jnp.sin(angles)
    low = jnp.where(lane < half_rot, -sine, 0.0)
    high = jnp.where((lane >= half_rot) & (lane < ROT), sine, 0.0)
    return jnp.cos(angles), low, high


def lane_tile(table, columns):
    return jnp.concatenate([table] * (columns // table.shape[1]), axis=1)


def turn(values, cosine, low, high):
    columns = values.shape[1]
    half_rot = ROT // 2
    return (
        values * lane_tile(cosine, columns)
        + pltpu.roll(values, columns - half_rot, 1) * lane_tile(low, columns)
        + pltpu.roll(values, half_rot, 1) * lane_tile(high, columns)
    )


def project_kernel(x_ref, w_ref, b_ref, cos_ref, low_ref, high_ref, q_ref, k_ref, v_ref):
    tables = (cos_ref[...], low_ref[...], high_ref[...])

    def part(number):
        flat = jnp.dot(x_ref[...], w_ref[number], preferred_element_type=F32)
        return flat + b_ref[number : number + 1, :].astype(F32)

    queries = turn(part(0), *tables).astype(BF16)
    q_ref[...] = (queries.astype(F32) * HEAD_DIM**-0.5).astype(BF16)
    k_ref[...] = turn(part(1), *tables).astype(BF16)
    v_ref[...] = part(2).astype(BF16)


def project(gathered, w_qkv, b_qkv, tables):
    length, width = gathered.shape
    columns = w_qkv.shape[2]
    rows = min(256, length)
    table_spec = pl.BlockSpec((rows, tables[0].shape[1]), lambda i: (i, 0))
    out_spec = pl.BlockSpec((rows, columns), lambda i: (i, 0))
    return pl.pallas_call(
        project_kernel,
        grid=(length // rows,),
        in_specs=[
            pl.BlockSpec((rows, width), lambda i: (i, 0)),
            pl.BlockSpec(w_qkv.shape, lambda i: (0, 0, 0)),
            pl.BlockSpec(b_qkv.shape, lambda i: (0, 0)),
            table_spec,
            table_spec,
            table_spec,
        ],
        out_specs=[out_spec] * 3,
        out_shape=[jax.ShapeDtypeStruct((length, columns), BF16)] * 3,
        cost_estimate=pl.CostEstimate(
            flops=6 * length * width * columns,
            bytes_accessed=2 * (length * width + 3 * width * columns + 3 * length * columns),
            transcendentals=0,
        ),
        name="project",
    )(gathered, w_qkv, b_qkv, *tables)


def stack_heads(block):
    columns = block.shape[1]
    head_of = lax.broadcasted_iota(jnp.int32, block.shape, 1) // HEAD_DIM
    return jnp.concatenate(
        [
            jnp.where(head_of == head, block, jnp.zeros_like(block))
            for head in range(columns // HEAD_DIM)
        ],
        axis=0,
    )


def unstack_heads(stacked, block):
    heads = stacked.shape[1] // block
    return jnp.concatenate(
        [
            stacked[head * HEAD_DIM : (head + 1) * HEAD_DIM, head * block : (head + 1) * block]
            for head in range(heads)
        ],
        axis=0,
    ).T


def score_block(key_block, stacked_queries, key_at, start_row, query_row):
    scores = lax.dot_general(
        key_block, stacked_queries, (((1,), (1,)), ((), ())), preferred_element_type=F32
    )
    key_pos = key_at + lax.broadcasted_iota(jnp.int32, scores.shape, 0)
    allowed = (key_pos >= start_row) & (key_pos <= query_row)
    return scores, allowed


def query_rows(start_ref, block, heads):
    start_row = jnp.concatenate([start_ref[0]] * heads, axis=1)
    query_row = pl.program_id(0) * block + lax.broadcasted_iota(jnp.int32, (1, block), 1)
    return start_row, jnp.concatenate([query_row] * heads, axis=1)


def attend_kernel(first_ref, q_ref, k_ref, v_ref, start_ref, o_ref, lse_ref, acc_ref):
    block, columns = q_ref.shape
    heads = columns // HEAD_DIM
    index = pl.program_id(0)
    stacked = stack_heads(q_ref[...])
    start_row, query_row = query_rows(start_ref, block, heads)
    acc_ref[...] = jnp.zeros_like(acc_ref)

    def body(step, carry):
        highest, total = carry
        at = pl.multiple_of(step * BK, BK)
        scores, allowed = score_block(
            k_ref[pl.ds(at, BK), :], stacked, at, start_row, query_row
        )
        scores = jnp.where(allowed, scores, NEG)
        newest = jnp.maximum(highest, jnp.max(scores, axis=0, keepdims=True))
        weights = jnp.exp(scores - newest)
        scale = jnp.exp(highest - newest)
        total = total * scale + jnp.sum(weights, axis=0, keepdims=True)
        acc_ref[...] = acc_ref[...] * scale + lax.dot_general(
            v_ref[pl.ds(at, BK), :],
            weights.astype(BF16),
            (((0,), (0,)), ((), ())),
            preferred_element_type=F32,
        )
        return newest, total

    highest, total = lax.fori_loop(
        first_ref[index],
        (index * block + block - 1) // BK + 1,
        body,
        (jnp.full((1, heads * block), NEG, F32), jnp.zeros((1, heads * block), F32)),
    )
    o_ref[...] = unstack_heads(acc_ref[...] / total, block).astype(BF16)
    lse_ref[0] = highest + jnp.log(total)


def attend(first, queries, key_rows, value_rows, start_blocks):
    length, columns = queries.shape
    blocks = length // BQ
    heads = columns // HEAD_DIM
    row_spec = pl.BlockSpec((BQ, columns), lambda i, f: (i, 0))
    whole = pl.BlockSpec((length, columns), lambda i, f: (0, 0))
    return pl.pallas_call(
        attend_kernel,
        grid_spec=pltpu.PrefetchScalarGridSpec(
            num_scalar_prefetch=1,
            grid=(blocks,),
            in_specs=[
                row_spec,
                whole,
                whole,
                pl.BlockSpec((1, 1, BQ), lambda i, f: (i, 0, 0)),
            ],
            out_specs=[
                row_spec,
                pl.BlockSpec((1, 1, heads * BQ), lambda i, f: (i, 0, 0)),
            ],
            scratch_shapes=[pltpu.VMEM((columns, heads * BQ), F32)],
        ),
        out_shape=[
            jax.ShapeDtypeStruct((length, columns), BF16),
            jax.ShapeDtypeStruct((blocks, 1, heads * BQ), F32),
        ],
        cost_estimate=pl.CostEstimate(
            flops=4 * length * 1024 * columns * heads,
            bytes_accessed=8 * length * columns,
            transcendentals=length * 1024 * heads,
        ),
        name="attend",
    )(first, queries, key_rows, value_rows, start_blocks)


def attend_back_kernel(
    first_ref,
    q_ref,
    k_ref,
    v_ref,
    do_ref,
    o_ref,
    lse_ref,
    start_ref,
    cos_ref,
    low_ref,
    high_ref,
    grad_ref,
    key_acc,
    value_acc,
    query_acc,
):
    block, columns = q_ref.shape
    heads = columns // HEAD_DIM
    length = k_ref.shape[0]
    index = pl.program_id(0)

    @pl.when(index == 0)
    def _():
        key_acc[...] = jnp.zeros_like(key_acc)
        value_acc[...] = jnp.zeros_like(value_acc)

    stacked = stack_heads(q_ref[...])
    stacked_do = stack_heads(do_ref[...])
    start_row, query_row = query_rows(start_ref, block, heads)
    lse_row = lse_ref[0]
    products = do_ref[...].astype(F32) * o_ref[...].astype(F32)
    head_rows = lax.broadcasted_iota(jnp.int32, (8, columns), 0)
    head_lanes = lax.broadcasted_iota(jnp.int32, (8, columns), 1) // HEAD_DIM
    picked = lax.dot_general(
        (head_rows == head_lanes).astype(F32),
        products,
        (((1,), (1,)), ((), ())),
        precision=lax.Precision.HIGHEST,
        preferred_element_type=F32,
    )
    inner_row = jnp.concatenate([picked[head : head + 1, :] for head in range(heads)], axis=1)
    query_acc[...] = jnp.zeros_like(query_acc)

    def body(step, carry):
        at = pl.multiple_of(step * BK, BK)
        key_block = k_ref[pl.ds(at, BK), :]
        scores, allowed = score_block(key_block, stacked, at, start_row, query_row)
        weights = jnp.where(allowed, jnp.exp(scores - lse_row), 0.0)
        grad_weights = lax.dot_general(
            v_ref[pl.ds(at, BK), :],
            stacked_do,
            (((1,), (1,)), ((), ())),
            preferred_element_type=F32,
        )
        grad_scores = (weights * (grad_weights - inner_row)).astype(BF16)
        value_acc[pl.ds(at, BK), :] += jnp.dot(
            weights.astype(BF16), stacked_do, preferred_element_type=F32
        )
        key_acc[pl.ds(at, BK), :] += jnp.dot(grad_scores, stacked, preferred_element_type=F32)
        query_acc[...] += lax.dot_general(
            key_block, grad_scores, (((0,), (0,)), ((), ())), preferred_element_type=F32
        )
        return carry

    lax.fori_loop(first_ref[index], (index * block + block - 1) // BK + 1, body, 0)

    def turn_back(grads, at, rows):
        kept = grads.astype(BF16).astype(F32)
        return turn(
            kept,
            cos_ref[pl.ds(at, rows), :],
            -low_ref[pl.ds(at, rows), :],
            -high_ref[pl.ds(at, rows), :],
        ).astype(BF16)

    at_query = pl.multiple_of(index * block, block)
    grad_ref[pl.ds(at_query, block), :columns] = turn_back(
        unstack_heads(query_acc[...], block) * HEAD_DIM**-0.5, at_query, block
    )

    @pl.when(index == pl.num_programs(0) - 1)
    def _():
        def finish(step, carry):
            at = pl.multiple_of(step * BK, BK)
            grad_ref[pl.ds(at, BK), columns : 2 * columns] = turn_back(
                key_acc[pl.ds(at, BK), :], at, BK
            )
            grad_ref[pl.ds(at, BK), 2 * columns :] = value_acc[pl.ds(at, BK), :].astype(BF16)
            return carry

        lax.fori_loop(0, length // BK, finish, 0)


def attend_back(first, queries, key_rows, value_rows, grad_att, attended, lse, start_blocks, tables):
    length, columns = queries.shape
    blocks = length // BQ
    heads = columns // HEAD_DIM
    row_spec = pl.BlockSpec((BQ, columns), lambda i, f: (i, 0))
    whole = pl.BlockSpec((length, columns), lambda i, f: (0, 0))
    table_spec = pl.BlockSpec(tables[0].shape, lambda i, f: (0, 0))
    return pl.pallas_call(
        attend_back_kernel,
        grid_spec=pltpu.PrefetchScalarGridSpec(
            num_scalar_prefetch=1,
            grid=(blocks,),
            in_specs=[
                row_spec,
                whole,
                whole,
                row_spec,
                row_spec,
                pl.BlockSpec((1, 1, heads * BQ), lambda i, f: (i, 0, 0)),
                pl.BlockSpec((1, 1, BQ), lambda i, f: (i, 0, 0)),
                table_spec,
                table_spec,
                table_spec,
            ],
            out_specs=pl.BlockSpec((length, 3 * columns), lambda i, f: (0, 0)),
            scratch_shapes=[
                pltpu.VMEM((length, columns), F32),
                pltpu.VMEM((length, columns), F32),
                pltpu.VMEM((columns, heads * BQ), F32),
            ],
        ),
        out_shape=jax.ShapeDtypeStruct((length, 3 * columns), BF16),
        cost_estimate=pl.CostEstimate(
            flops=10 * length * 1024 * columns * heads,
            bytes_accessed=16 * length * columns,
            transcendentals=length * 1024 * heads,
        ),
        name="attend_back",
    )(first, queries, key_rows, value_rows, grad_att, attended, lse, start_blocks, *tables)


def bits_of(name):
    size = lax.axis_size(name)
    count = size.bit_length() - 1
    return count if size == 1 << count else None


def swap(values, name, bit):
    size = lax.axis_size(name)
    return lax.ppermute(values, name, [(i, i ^ (1 << bit)) for i in range(size)])


def write_stacked(piece, outs):
    outs[0][0] = piece.astype(F32)


def write_rows(piece, outs):
    at = 0
    for out_ref in outs:
        size = out_ref.shape[0]
        out_ref[...] = piece[at : at + size, :].astype(F32)
        at += size


def write_lanes(piece, outs):
    parts, _, size = outs[0].shape
    for part in range(parts):
        outs[0][part] = piece[:, part * size : (part + 1) * size].astype(F32)


def place_kernel(write, count, color_ref, where_ref, *refs):
    step = pl.program_id(0)
    for number in range(count):

        @pl.when(step == number)
        def _(number=number):
            write(refs[number][...], refs[count:])


def place_blocks(write, color, where, pieces, out_shapes, out_specs):
    rows, columns = pieces[0].shape
    count = len(pieces)
    return pl.pallas_call(
        functools.partial(place_kernel, write, count),
        grid_spec=pltpu.PrefetchScalarGridSpec(
            num_scalar_prefetch=2,
            grid=(count,),
            in_specs=[pl.BlockSpec((rows, columns), lambda i, c, w: (0, 0))] * count,
            out_specs=out_specs,
        ),
        out_shape=[jax.ShapeDtypeStruct(shape, F32) for shape in out_shapes],
        cost_estimate=pl.CostEstimate(
            flops=0, bytes_accessed=6 * count * rows * columns, transcendentals=0
        ),
        name="place_blocks",
    )(color, where, *pieces)


class DpSum:
    def __init__(self, *grads, paired=False):
        self.grads = grads
        self.paired = paired
        self.count = bits_of("dp")
        pieces = (1 if paired else 2) << self.count
        self.axis = 0 if all(g.shape[0] % (8 * pieces) == 0 for g in grads) else 1
        self.sizes = [g.shape[self.axis] // pieces for g in grads]
        self.mine = lax.axis_index("dp")
        self.orders = [list(range(self.count)), list(range(self.count))[::-1]]
        self.level = 0
        if paired:
            self.state = [((grad,), self.sizes[:1], 0) for grad in grads]
        else:
            self.state = [(grads, self.sizes, color << self.count) for color in range(2)]
        self.held = None
        self.ready()

    def cut(self, color, side):
        grads, units, base = self.state[color]
        span = (1 << self.count) >> (self.level + 1)
        parts = []
        for grad, unit in zip(grads, units):
            at = (base + side * span) * unit
            parts.append(lax.dynamic_slice_in_dim(grad, at, span * unit, self.axis))
        if len(parts) == 1:
            return parts[0]
        if self.axis:
            return jnp.concatenate(parts, axis=0)
        parts = [p.reshape(span, unit, p.shape[1]) for p, unit in zip(parts, units)]
        joined = jnp.concatenate(parts, axis=1)
        return joined.reshape(-1, joined.shape[2])

    def side(self, color):
        return (self.mine >> self.orders[color][self.level]) & 1

    def ready(self):
        if self.level < self.count:
            self.out = [self.cut(color, 1 - self.side(color)) for color in range(2)]
        elif self.held is None:
            self.held = [[(self.state[color][0][0], 0)] for color in range(2)]

    def send_half(self, half):
        for color in range(2):
            bit = self.orders[color][2 * self.count - 1 - self.level]
            blocks = 1 << (self.level - self.count)
            middle = max(blocks // 2, 1)
            chosen = self.held[color][:middle] if half == 0 else self.held[color][middle:blocks]
            self.held[color] += [
                (swap(piece, "dp", bit), mask ^ (1 << bit)) for piece, mask in chosen
            ]

    def send(self):
        if self.level < self.count:
            self.got = [
                swap(self.out[color], "dp", self.orders[color][self.level])
                for color in range(2)
            ]
            return
        for color in range(2):
            bit = self.orders[color][2 * self.count - 1 - self.level]
            self.held[color] += [
                (swap(piece, "dp", bit), mask ^ (1 << bit)) for piece, mask in self.held[color]
            ]

    def arrive(self):
        if self.level < self.count:
            state = []
            for color in range(2):
                keep = self.cut(color, self.side(color))
                total = (keep.astype(F32) + self.got[color].astype(F32)).astype(BF16)
                whole = self.axis == 0 and not self.paired
                state.append(((total,), [sum(self.sizes) if whole else self.sizes[0]], 0))
            self.state = state
        self.level += 1
        self.ready()

    def moving(self):
        return self.out if self.held is None else self.held

    def fresh(self):
        return [held[len(held) // 2][0] for held in self.held]

    def result(self, write):
        pieces, colors, where = [], [], []
        for color in range(2):
            for piece, mask in self.held[color]:
                owner = self.mine ^ mask
                spot = 0 if self.paired else color
                for bit in self.orders[color]:
                    spot = spot * 2 + ((owner >> bit) & 1)
                pieces.append(piece)
                colors.append(color)
                where.append(spot)
        rows, columns = pieces[0].shape
        length, width = self.grads[0].shape
        if write is write_stacked:
            shapes = [(2, length, width)]
            blocks = [(1, rows, columns)]
        elif write is write_lanes:
            shapes = [(3, length, width // 3)]
            blocks = [(3, rows, columns // 3)]
        else:
            shapes = [g.shape for g in self.grads]
            blocks = [(rows * s[0] // sum(t[0] for t in shapes), columns) for s in shapes]
        lead = {write_stacked: lambda i, c: (c[i],), write_lanes: lambda i, c: (0,)}.get(
            write, lambda i, c: ()
        )

        def out_map(i, c, w):
            return lead(i, c) + ((w[i], 0) if self.axis == 0 else (0, w[i]))

        return place_blocks(
            write,
            jnp.array(colors, jnp.int32),
            jnp.stack(where).astype(jnp.int32),
            pieces,
            shapes,
            [pl.BlockSpec(block, out_map) for block in blocks],
        )


def fence(values, *sums):
    values, moving = lax.optimization_barrier((values, [item.moving() for item in sums]))
    for item, arrived in zip(sums, moving):
        if item.held is None:
            item.out = arrived
        else:
            item.held = arrived
    return values


def sum_small(values, name, bits=None):
    count = bits_of(name)
    if count is None:
        return lax.psum(values, name) if bits is None or 0 in bits else values
    for bit in range(count) if bits is None else bits:
        values = values + swap(values, name, bit)
    return values


def norm_kernel(x_ref, gain_ref, shift_ref, out_ref):
    residual = x_ref[...].astype(F32)
    centered = residual - jnp.mean(residual, -1, keepdims=True)
    inv_std = lax.rsqrt(jnp.mean(centered * centered, -1, keepdims=True) + EPSILON)
    out_ref[...] = (centered * inv_std * gain_ref[...] + shift_ref[...]).astype(BF16)


def norm(layer_in, norm_gain, norm_shift):
    length, width = layer_in.shape
    rows = min(64, length)
    row_spec = pl.BlockSpec((rows, width), lambda i: (i, 0))
    one_spec = pl.BlockSpec((1, width), lambda i: (0, 0))
    return pl.pallas_call(
        norm_kernel,
        grid=(length // rows,),
        in_specs=[row_spec, one_spec, one_spec],
        out_specs=row_spec,
        out_shape=jax.ShapeDtypeStruct((length, width), BF16),
        name="norm",
    )(layer_in, norm_gain.reshape(1, width), norm_shift.reshape(1, width))


def tail_kernel(x_ref, g_ref, c_ref, gain_ref, stat_ref, grad_ref, sums_ref):
    @pl.when(pl.program_id(0) == 0)
    def _():
        sums_ref[...] = jnp.zeros_like(sums_ref)
        sums_ref[2:3, :] = stat_ref[...]

    residual = x_ref[...].astype(F32)
    centered = residual - jnp.mean(residual, -1, keepdims=True)
    inv_std = lax.rsqrt(jnp.mean(centered * centered, -1, keepdims=True) + EPSILON)
    normalized = centered * inv_std
    grads = g_ref[...].astype(F32)
    sums_ref[0:1, :] += jnp.sum(grads * normalized, axis=0, keepdims=True)
    sums_ref[1:2, :] += jnp.sum(grads, axis=0, keepdims=True)
    scaled = grads * gain_ref[...]
    grad_ref[:, 0, :] = (
        inv_std
        * (
            scaled
            - jnp.mean(scaled, -1, keepdims=True)
            - normalized * jnp.mean(scaled * normalized, -1, keepdims=True)
        )
        + c_ref[...].astype(F32)
    )


def tail(layer_in, grad_normed, cot_here, norm_gain, stat_row):
    length, width = layer_in.shape
    rows = min(64, length)
    row_spec = pl.BlockSpec((rows, width), lambda i: (i, 0))
    one_spec = pl.BlockSpec((1, width), lambda i: (0, 0))
    return pl.pallas_call(
        tail_kernel,
        grid=(length // rows,),
        in_specs=[row_spec, row_spec, row_spec, one_spec, one_spec],
        out_specs=[
            pl.BlockSpec((rows, 1, width), lambda i: (i, 0, 0)),
            pl.BlockSpec((4, width), lambda i: (0, 0)),
        ],
        out_shape=[
            jax.ShapeDtypeStruct((length, 1, width), F32),
            jax.ShapeDtypeStruct((4, width), F32),
        ],
        name="tail",
    )(layer_in, grad_normed, cot_here, norm_gain.reshape(1, width), stat_row)


def back_products_kernel(p_ref, q_ref, g_ref, u_ref, w_ref, out_ref):
    turned = (((1,), (1,)), ((), ()))
    columns = q_ref.shape[2]
    total = jnp.dot(g_ref[...], w_ref[0], preferred_element_type=F32)
    total += jnp.dot(u_ref[...], w_ref[1], preferred_element_type=F32)
    for number in range(3):
        total += lax.dot_general(
            p_ref[:, number * columns : (number + 1) * columns],
            q_ref[number],
            turned,
            preferred_element_type=F32,
        )
    out_ref[...] = total.astype(BF16)


def back_products(grad_proj, w_qkv, grad_gate, grad_up, w_gate_up):
    length = grad_proj.shape[0]
    _, width, columns = w_qkv.shape
    hidden = grad_gate.shape[1]
    rows = min(256, length)
    return pl.pallas_call(
        back_products_kernel,
        grid=(length // rows,),
        in_specs=[
            pl.BlockSpec((rows, 3 * columns), lambda i: (i, 0)),
            pl.BlockSpec(w_qkv.shape, lambda i: (0, 0, 0)),
            pl.BlockSpec((rows, hidden), lambda i: (i, 0)),
            pl.BlockSpec((rows, hidden), lambda i: (i, 0)),
            pl.BlockSpec(w_gate_up.shape, lambda i: (0, 0, 0)),
        ],
        out_specs=pl.BlockSpec((rows, width), lambda i: (i, 0)),
        out_shape=jax.ShapeDtypeStruct((length, width), BF16),
        name="back_products",
    )(grad_proj, w_qkv, grad_gate, grad_up, w_gate_up)


def local(
    layer_in,
    segment_ids,
    valid_counts,
    norm_gain,
    norm_shift,
    w_qkv,
    b_qkv,
    w_out,
    w_gate_up,
    w_down,
    out_grad,
):
    local_len, row_count, model_width = layer_in.shape
    assert row_count == 1
    seq_len = local_len * lax.axis_size("mp")
    col_qkv = w_qkv.shape[2]
    ff_local = w_gate_up.shape[2]
    layer_in = layer_in[:, 0]
    position_here = lax.axis_index("mp") * local_len + jnp.arange(local_len, dtype=jnp.int32)
    valid_here = (position_here < valid_counts[0]).astype(F32)

    residual = layer_in.astype(F32)
    normed = norm(layer_in, norm_gain, norm_shift)
    cot_here = jnp.where(valid_here[:, None] > 0, out_grad[:, 0], jnp.zeros((), BF16))
    gathered = lax.all_gather(normed, "mp", axis=0, tiled=True)
    cotangent = lax.all_gather(cot_here, "mp", axis=0, tiled=True)

    w_qkv = jnp.transpose(w_qkv, (1, 0, 2))
    w_gate_up = jnp.transpose(w_gate_up, (1, 2, 0))
    starts = starts_of(segment_ids)[0]
    tables = rotary_lanes(jnp.arange(seq_len, dtype=jnp.int32) - starts)
    start_blocks = starts.reshape(seq_len // BQ, 1, BQ)
    first = start_blocks[:, 0, 0] // BK
    gathered, tables, first, start_blocks = lax.optimization_barrier(
        (gathered, tables, first, start_blocks)
    )

    def product(left, right):
        return jnp.dot(left, right, preferred_element_type=F32).astype(BF16)

    def turned_product(left, right):
        return lax.dot_general(
            left, right, (((1,), (1,)), ((), ())), preferred_element_type=F32
        )

    def token_sum(left, right):
        return lax.dot_general(
            left, right, (((0,), (0,)), ((), ())), preferred_element_type=F32
        ).astype(BF16)

    def scattered(partial):
        return lax.psum_scatter(partial, "mp", scatter_dimension=0, tiled=True)

    gate = turned_product(gathered, w_gate_up[0])
    up = turned_product(gathered, w_gate_up[1])
    sigmoid_gate = jax.nn.sigmoid(gate)
    hidden = (gate * sigmoid_gate * up).astype(BF16)
    mlp_partial = product(hidden, w_down)
    mlp_sum = scattered(mlp_partial)
    gathered_next, mlp_partial = lax.optimization_barrier((gathered, mlp_partial))
    queries, key_rows, value_rows = project(gathered_next, w_qkv, b_qkv, tables)
    attended, lse = attend(first, queries, key_rows, value_rows, start_blocks)
    attn_partial = product(attended, w_out)
    attn_sum = scattered(attn_partial)

    cotangent, attn_partial = lax.optimization_barrier((cotangent, attn_partial))
    sum_down = DpSum(token_sum(hidden, cotangent), token_sum(attended, cotangent))
    cotangent = fence(cotangent, sum_down)
    sum_down.send()
    grad_hid = turned_product(cotangent, w_down).astype(BF16).astype(F32)
    grad_gate = (
        grad_hid * up * sigmoid_gate * (1.0 + gate * (1.0 - sigmoid_gate))
    ).astype(BF16)
    grad_up = (grad_hid * gate * sigmoid_gate).astype(BF16)
    grad_att = turned_product(cotangent, w_out).astype(BF16)
    sum_down.arrive()
    grad_gate, grad_up, grad_att = fence((grad_gate, grad_up, grad_att), sum_down)
    sum_down.send()
    sum_gate = token_sum(grad_gate, gathered)
    sum_down.arrive()
    sum_gate, grad_up = fence((sum_gate, grad_up), sum_down)
    sum_down.send()
    sum_gate_up = DpSum(sum_gate, token_sum(grad_up, gathered), paired=True)
    sum_down.arrive()
    grad_att = fence(grad_att, sum_gate_up, sum_down)
    sum_gate_up.send()
    sum_down.send_half(0)
    grad_proj = attend_back(
        first, queries, key_rows, value_rows, grad_att, attended, lse, start_blocks, tables
    )
    sum_gate_up.arrive()
    grad_proj, mlp_sum = fence((grad_proj, mlp_sum), sum_gate_up, sum_down)
    sum_gate_up.send()
    sum_down.send_half(1)
    sum_down.arrive()
    normed_partial = back_products(grad_proj, w_qkv, grad_gate, grad_up, w_gate_up)
    while sum_down.level < 2 * sum_down.count:
        sum_down.send()
        sum_down.arrive()
    sum_gate_up.arrive()
    grad_proj, normed_partial = fence((grad_proj, normed_partial), sum_gate_up, sum_down)
    grad_normed = scattered(normed_partial)
    sum_gate_up.send()
    sum_qkv = token_sum(gathered, grad_proj)
    sum_gate_up.arrive()
    sum_qkv = DpSum(fence(sum_qkv, sum_gate_up))
    bias_sums = jnp.sum(grad_proj, axis=0, dtype=F32).reshape(-1, 128)
    sum_qkv.send()
    sum_qkv.arrive()
    attn_sum = fence(attn_sum, sum_gate_up, sum_qkv)
    sum_gate_up.send()
    sum_qkv.send()
    mlp_part = mlp_sum.astype(F32)
    attn_part = attn_sum.astype(F32)
    layer_out = (residual + attn_part + mlp_part).astype(BF16)
    statistics = jnp.stack(
        [
            jnp.sum(valid_here * jnp.sum(residual * residual, -1)),
            jnp.sum(valid_here * jnp.sum(attn_part * attn_part, -1)),
            jnp.sum(valid_here * jnp.sum(mlp_part * mlp_part, -1)),
            jnp.sum(valid_here),
        ]
    )
    stat_row = jnp.pad(statistics, (0, model_width - 4)).reshape(1, model_width)
    fresh = sum_gate_up.fresh()
    sum_gate_up.arrive()
    sum_qkv.arrive()
    bias_sums, layer_out, stat_row, _ = fence((bias_sums, layer_out, stat_row, fresh), sum_qkv)
    bias_sums = sum_small(bias_sums, "dp", [0])
    sum_qkv.send()
    down_sums = sum_down.result(write_rows)
    sum_qkv.arrive()
    while sum_gate_up.level < 2 * sum_gate_up.count:
        sum_gate_up.send()
        sum_gate_up.arrive()
    down_sums, bias_sums = fence((down_sums, bias_sums), sum_gate_up, sum_qkv)
    while sum_qkv.level < 2 * sum_qkv.count:
        sum_qkv.send()
        sum_qkv.arrive()
    (grad_w_gate_up,) = sum_gate_up.result(write_stacked)
    bias_sums = sum_small(bias_sums, "dp", range(1, sum_qkv.count))
    grad_w_gate_up, bias_sums = fence((grad_w_gate_up, bias_sums), sum_qkv)
    (grad_w_qkv,) = sum_qkv.result(write_lanes)
    grad_w_down, grad_w_out = down_sums
    grad_normed, grad_w_gate_up, grad_w_qkv = fence(
        (grad_normed, grad_w_gate_up, grad_w_qkv)
    )
    input_grad, small = tail(layer_in, grad_normed, cot_here, norm_gain, stat_row)
    small = sum_small(sum_small(small, "mp"), "dp")
    totals = small[2]
    return (
        layer_out[:, None],
        input_grad,
        small[0],
        small[1],
        jnp.transpose(grad_w_qkv, (1, 0, 2)),
        bias_sums.reshape(3, col_qkv),
        grad_w_out,
        jnp.transpose(grad_w_gate_up, (2, 0, 1)),
        grad_w_down,
        jnp.sqrt(totals[:3] / (totals[3] * model_width)),
    )


def solution(mesh):
    placed = (
        P("mp", "dp", None),
        P("dp", None),
        P("dp"),
        P(),
        P(),
        P(None, None, "mp"),
        P(None, "mp"),
        P("mp", None),
        P(None, None, "mp"),
        P("mp", None),
        P("mp", "dp", None),
    )
    return jax.shard_map(
        local,
        mesh=mesh,
        in_specs=placed,
        out_specs=(
            P("mp", "dp", None),
            P("mp", "dp", None),
            P(),
            P(),
            P(None, None, "mp"),
            P(None, "mp"),
            P("mp", None),
            P(None, None, "mp"),
            P("mp", None),
            P(),
        ),
        check_vma=False,
    )
```

```python
import functools

import jax
import jax.numpy as jnp
from jax import lax
from jax.experimental import pallas as pl
from jax.experimental.pallas import tpu as pltpu
from jax.sharding import PartitionSpec as P

HEAD_DIM = 64
ROT = 16
EPSILON = 1e-05
BQ = 128
BK = 256
NEG = -1e30
F32 = jnp.float32
BF16 = jnp.bfloat16


def starts_of(segment_ids):
    length = segment_ids.shape[1]
    steps_all = jnp.arange(length, dtype=jnp.int32)[None, :]
    change = jnp.concatenate(
        [
            jnp.ones_like(segment_ids[:, :1]),
            (segment_ids[:, 1:] != segment_ids[:, :-1]).astype(jnp.int32),
        ],
        axis=1,
    )
    return lax.cummax(jnp.where(change > 0, steps_all, jnp.zeros_like(change)), axis=1)


def rotary_lanes(positions):
    half_rot = ROT // 2
    lane = jnp.arange(2 * HEAD_DIM, dtype=jnp.int32) % HEAD_DIM
    power = (lane % half_rot).astype(F32)
    frequency = jnp.where(lane < ROT, 10000.0 ** (-(power * 2.0) / ROT), 0.0)
    angles = positions.astype(F32)[:, None] * frequency
    sine = jnp.sin(angles)
    low = jnp.where(lane < half_rot, -sine, 0.0)
    high = jnp.where((lane >= half_rot) & (lane < ROT), sine, 0.0)
    return jnp.cos(angles), low, high


def lane_tile(table, columns):
    return jnp.concatenate([table] * (columns // table.shape[1]), axis=1)


def turn(values, cosine, low, high):
    columns = values.shape[1]
    half_rot = ROT // 2
    return (
        values * lane_tile(cosine, columns)
        + pltpu.roll(values, columns - half_rot, 1) * lane_tile(low, columns)
        + pltpu.roll(values, half_rot, 1) * lane_tile(high, columns)
    )


def project_kernel(x_ref, w_ref, b_ref, cos_ref, low_ref, high_ref, q_ref, k_ref, v_ref):
    tables = (cos_ref[...], low_ref[...], high_ref[...])

    def part(number):
        flat = jnp.dot(x_ref[...], w_ref[number], preferred_element_type=F32)
        return flat + b_ref[number : number + 1, :].astype(F32)

    queries = turn(part(0), *tables).astype(BF16)
    q_ref[...] = (queries.astype(F32) * HEAD_DIM**-0.5).astype(BF16)
    k_ref[...] = turn(part(1), *tables).astype(BF16)
    v_ref[...] = part(2).astype(BF16)


def project(gathered, w_qkv, b_qkv, tables):
    length, width = gathered.shape
    columns = w_qkv.shape[2]
    rows = min(256, length)
    table_spec = pl.BlockSpec((rows, tables[0].shape[1]), lambda i: (i, 0))
    out_spec = pl.BlockSpec((rows, columns), lambda i: (i, 0))
    return pl.pallas_call(
        project_kernel,
        grid=(length // rows,),
        in_specs=[
            pl.BlockSpec((rows, width), lambda i: (i, 0)),
            pl.BlockSpec(w_qkv.shape, lambda i: (0, 0, 0)),
            pl.BlockSpec(b_qkv.shape, lambda i: (0, 0)),
            table_spec,
            table_spec,
            table_spec,
        ],
        out_specs=[out_spec] * 3,
        out_shape=[jax.ShapeDtypeStruct((length, columns), BF16)] * 3,
        cost_estimate=pl.CostEstimate(
            flops=6 * length * width * columns,
            bytes_accessed=2 * (length * width + 3 * width * columns + 3 * length * columns),
            transcendentals=0,
        ),
        name="project",
    )(gathered, w_qkv, b_qkv, *tables)


def stack_heads(block):
    columns = block.shape[1]
    head_of = lax.broadcasted_iota(jnp.int32, block.shape, 1) // HEAD_DIM
    return jnp.concatenate(
        [
            jnp.where(head_of == head, block, jnp.zeros_like(block))
            for head in range(columns // HEAD_DIM)
        ],
        axis=0,
    )


def unstack_heads(stacked, block):
    heads = stacked.shape[1] // block
    return jnp.concatenate(
        [
            stacked[head * HEAD_DIM : (head + 1) * HEAD_DIM, head * block : (head + 1) * block]
            for head in range(heads)
        ],
        axis=0,
    ).T


def score_block(key_block, stacked_queries, key_at, start_row, query_row):
    scores = lax.dot_general(
        key_block, stacked_queries, (((1,), (1,)), ((), ())), preferred_element_type=F32
    )
    key_pos = key_at + lax.broadcasted_iota(jnp.int32, scores.shape, 0)
    allowed = (key_pos >= start_row) & (key_pos <= query_row)
    return scores, allowed


def query_rows(start_ref, block, heads):
    start_row = jnp.concatenate([start_ref[0]] * heads, axis=1)
    query_row = pl.program_id(0) * block + lax.broadcasted_iota(jnp.int32, (1, block), 1)
    return start_row, jnp.concatenate([query_row] * heads, axis=1)


def attend_kernel(first_ref, q_ref, k_ref, v_ref, start_ref, o_ref, lse_ref, acc_ref):
    block, columns = q_ref.shape
    heads = columns // HEAD_DIM
    index = pl.program_id(0)
    stacked = stack_heads(q_ref[...])
    start_row, query_row = query_rows(start_ref, block, heads)
    acc_ref[...] = jnp.zeros_like(acc_ref)

    def body(step, carry):
        highest, total = carry
        at = pl.multiple_of(step * BK, BK)
        scores, allowed = score_block(
            k_ref[pl.ds(at, BK), :], stacked, at, start_row, query_row
        )
        scores = jnp.where(allowed, scores, NEG)
        newest = jnp.maximum(highest, jnp.max(scores, axis=0, keepdims=True))
        weights = jnp.exp(scores - newest)
        scale = jnp.exp(highest - newest)
        total = total * scale + jnp.sum(weights, axis=0, keepdims=True)
        acc_ref[...] = acc_ref[...] * scale + lax.dot_general(
            v_ref[pl.ds(at, BK), :],
            weights.astype(BF16),
            (((0,), (0,)), ((), ())),
            preferred_element_type=F32,
        )
        return newest, total

    highest, total = lax.fori_loop(
        first_ref[index],
        (index * block + block - 1) // BK + 1,
        body,
        (jnp.full((1, heads * block), NEG, F32), jnp.zeros((1, heads * block), F32)),
    )
    o_ref[...] = unstack_heads(acc_ref[...] / total, block).astype(BF16)
    lse_ref[0] = highest + jnp.log(total)


def attend(first, queries, key_rows, value_rows, start_blocks):
    length, columns = queries.shape
    blocks = length // BQ
    heads = columns // HEAD_DIM
    row_spec = pl.BlockSpec((BQ, columns), lambda i, f: (i, 0))
    whole = pl.BlockSpec((length, columns), lambda i, f: (0, 0))
    return pl.pallas_call(
        attend_kernel,
        grid_spec=pltpu.PrefetchScalarGridSpec(
            num_scalar_prefetch=1,
            grid=(blocks,),
            in_specs=[
                row_spec,
                whole,
                whole,
                pl.BlockSpec((1, 1, BQ), lambda i, f: (i, 0, 0)),
            ],
            out_specs=[
                row_spec,
                pl.BlockSpec((1, 1, heads * BQ), lambda i, f: (i, 0, 0)),
            ],
            scratch_shapes=[pltpu.VMEM((columns, heads * BQ), F32)],
        ),
        out_shape=[
            jax.ShapeDtypeStruct((length, columns), BF16),
            jax.ShapeDtypeStruct((blocks, 1, heads * BQ), F32),
        ],
        cost_estimate=pl.CostEstimate(
            flops=4 * length * 1024 * columns * heads,
            bytes_accessed=8 * length * columns,
            transcendentals=length * 1024 * heads,
        ),
        name="attend",
    )(first, queries, key_rows, value_rows, start_blocks)


def attend_back_kernel(
    first_ref,
    q_ref,
    k_ref,
    v_ref,
    do_ref,
    o_ref,
    lse_ref,
    start_ref,
    cos_ref,
    low_ref,
    high_ref,
    grad_ref,
    key_acc,
    value_acc,
    query_acc,
):
    block, columns = q_ref.shape
    heads = columns // HEAD_DIM
    length = k_ref.shape[0]
    index = pl.program_id(0)

    @pl.when(index == 0)
    def _():
        key_acc[...] = jnp.zeros_like(key_acc)
        value_acc[...] = jnp.zeros_like(value_acc)

    stacked = stack_heads(q_ref[...])
    stacked_do = stack_heads(do_ref[...])
    start_row, query_row = query_rows(start_ref, block, heads)
    lse_row = lse_ref[0]
    products = do_ref[...].astype(F32) * o_ref[...].astype(F32)
    head_rows = lax.broadcasted_iota(jnp.int32, (8, columns), 0)
    head_lanes = lax.broadcasted_iota(jnp.int32, (8, columns), 1) // HEAD_DIM
    picked = lax.dot_general(
        (head_rows == head_lanes).astype(F32),
        products,
        (((1,), (1,)), ((), ())),
        precision=lax.Precision.HIGHEST,
        preferred_element_type=F32,
    )
    inner_row = jnp.concatenate([picked[head : head + 1, :] for head in range(heads)], axis=1)
    query_acc[...] = jnp.zeros_like(query_acc)

    def body(step, carry):
        at = pl.multiple_of(step * BK, BK)
        key_block = k_ref[pl.ds(at, BK), :]
        scores, allowed = score_block(key_block, stacked, at, start_row, query_row)
        weights = jnp.where(allowed, jnp.exp(scores - lse_row), 0.0)
        grad_weights = lax.dot_general(
            v_ref[pl.ds(at, BK), :],
            stacked_do,
            (((1,), (1,)), ((), ())),
            preferred_element_type=F32,
        )
        grad_scores = (weights * (grad_weights - inner_row)).astype(BF16)
        value_acc[pl.ds(at, BK), :] += jnp.dot(
            weights.astype(BF16), stacked_do, preferred_element_type=F32
        )
        key_acc[pl.ds(at, BK), :] += jnp.dot(grad_scores, stacked, preferred_element_type=F32)
        query_acc[...] += lax.dot_general(
            key_block, grad_scores, (((0,), (0,)), ((), ())), preferred_element_type=F32
        )
        return carry

    lax.fori_loop(first_ref[index], (index * block + block - 1) // BK + 1, body, 0)

    def turn_back(grads, at, rows):
        kept = grads.astype(BF16).astype(F32)
        return turn(
            kept,
            cos_ref[pl.ds(at, rows), :],
            -low_ref[pl.ds(at, rows), :],
            -high_ref[pl.ds(at, rows), :],
        ).astype(BF16)

    at_query = pl.multiple_of(index * block, block)
    grad_ref[pl.ds(at_query, block), :columns] = turn_back(
        unstack_heads(query_acc[...], block) * HEAD_DIM**-0.5, at_query, block
    )

    @pl.when(index == pl.num_programs(0) - 1)
    def _():
        def finish(step, carry):
            at = pl.multiple_of(step * BK, BK)
            grad_ref[pl.ds(at, BK), columns : 2 * columns] = turn_back(
                key_acc[pl.ds(at, BK), :], at, BK
            )
            grad_ref[pl.ds(at, BK), 2 * columns :] = value_acc[pl.ds(at, BK), :].astype(BF16)
            return carry

        lax.fori_loop(0, length // BK, finish, 0)


def attend_back(first, queries, key_rows, value_rows, grad_att, attended, lse, start_blocks, tables):
    length, columns = queries.shape
    blocks = length // BQ
    heads = columns // HEAD_DIM
    row_spec = pl.BlockSpec((BQ, columns), lambda i, f: (i, 0))
    whole = pl.BlockSpec((length, columns), lambda i, f: (0, 0))
    table_spec = pl.BlockSpec(tables[0].shape, lambda i, f: (0, 0))
    return pl.pallas_call(
        attend_back_kernel,
        grid_spec=pltpu.PrefetchScalarGridSpec(
            num_scalar_prefetch=1,
            grid=(blocks,),
            in_specs=[
                row_spec,
                whole,
                whole,
                row_spec,
                row_spec,
                pl.BlockSpec((1, 1, heads * BQ), lambda i, f: (i, 0, 0)),
                pl.BlockSpec((1, 1, BQ), lambda i, f: (i, 0, 0)),
                table_spec,
                table_spec,
                table_spec,
            ],
            out_specs=pl.BlockSpec((length, 3 * columns), lambda i, f: (0, 0)),
            scratch_shapes=[
                pltpu.VMEM((length, columns), F32),
                pltpu.VMEM((length, columns), F32),
                pltpu.VMEM((columns, heads * BQ), F32),
            ],
        ),
        out_shape=jax.ShapeDtypeStruct((length, 3 * columns), BF16),
        cost_estimate=pl.CostEstimate(
            flops=10 * length * 1024 * columns * heads,
            bytes_accessed=16 * length * columns,
            transcendentals=length * 1024 * heads,
        ),
        name="attend_back",
    )(first, queries, key_rows, value_rows, grad_att, attended, lse, start_blocks, *tables)


def bits_of(name):
    size = lax.axis_size(name)
    count = size.bit_length() - 1
    return count if size == 1 << count else None


def swap(values, name, bit):
    return swap_mask(values, name, 1 << bit)


def swap_mask(values, name, mask):
    size = lax.axis_size(name)
    return lax.ppermute(values, name, [(i, i ^ mask) for i in range(size)])


def write_stacked(piece, outs):
    outs[0][0] = piece.astype(F32)


def write_rows(piece, outs):
    at = 0
    for out_ref in outs:
        size = out_ref.shape[0]
        out_ref[...] = piece[at : at + size, :].astype(F32)
        at += size


def write_lanes(piece, outs):
    parts, _, size = outs[0].shape
    for part in range(parts):
        outs[0][part] = piece[:, part * size : (part + 1) * size].astype(F32)


def place_kernel(write, count, outs_at, color_ref, where_ref, *refs):
    step = pl.program_id(0)
    for number in range(count):

        @pl.when(step == number)
        def _(number=number):
            write(refs[number][...], refs[outs_at:])


def place_blocks(write, color, where, pieces, out_shapes, out_specs, into):
    rows, columns = pieces[0].shape
    count = len(pieces)
    outs_at = count + len(into)
    return pl.pallas_call(
        functools.partial(place_kernel, write, count, outs_at),
        grid_spec=pltpu.PrefetchScalarGridSpec(
            num_scalar_prefetch=2,
            grid=(count,),
            in_specs=[pl.BlockSpec((rows, columns), lambda i, c, w: (0, 0))] * count
            + [pl.BlockSpec(memory_space=pl.ANY)] * len(into),
            out_specs=out_specs,
        ),
        out_shape=[jax.ShapeDtypeStruct(shape, F32) for shape in out_shapes],
        cost_estimate=pl.CostEstimate(
            flops=0, bytes_accessed=6 * count * rows * columns, transcendentals=0
        ),
        input_output_aliases={2 + count + number: number for number in range(len(into))},
        name="place_blocks",
    )(color, where, *pieces, *into)


class DpSum:
    def __init__(self, *grads, paired=False):
        self.grads = grads
        self.paired = paired
        self.count = bits_of("dp")
        pieces = (1 if paired else 2) << self.count
        self.axis = 0 if all(g.shape[0] % (8 * pieces) == 0 for g in grads) else 1
        self.sizes = [g.shape[self.axis] // pieces for g in grads]
        self.mine = lax.axis_index("dp")
        self.orders = [list(range(self.count)), list(range(self.count))[::-1]]
        self.level = 0
        if paired:
            self.state = [((grad,), self.sizes[:1], 0) for grad in grads]
        else:
            self.state = [(grads, self.sizes, color << self.count) for color in range(2)]
        self.held = None
        self.ready()

    def cut(self, color, side):
        grads, units, base = self.state[color]
        span = (1 << self.count) >> (self.level + 1)
        parts = []
        for grad, unit in zip(grads, units):
            at = (base + side * span) * unit
            parts.append(lax.dynamic_slice_in_dim(grad, at, span * unit, self.axis))
        if len(parts) == 1:
            return parts[0]
        if self.axis:
            return jnp.concatenate(parts, axis=0)
        parts = [p.reshape(span, unit, p.shape[1]) for p, unit in zip(parts, units)]
        joined = jnp.concatenate(parts, axis=1)
        return joined.reshape(-1, joined.shape[2])

    def side(self, color):
        return (self.mine >> self.orders[color][self.level]) & 1

    def ready(self):
        if self.level < self.count:
            self.out = [self.cut(color, 1 - self.side(color)) for color in range(2)]
        elif self.held is None:
            self.held = [[(self.state[color][0][0], 0)] for color in range(2)]

    def send_half(self, half):
        for color in range(2):
            bit = self.orders[color][2 * self.count - 1 - self.level]
            blocks = 1 << (self.level - self.count)
            middle = max(blocks // 2, 1)
            chosen = self.held[color][:middle] if half == 0 else self.held[color][middle:blocks]
            self.held[color] += [
                (swap(piece, "dp", bit), mask ^ (1 << bit)) for piece, mask in chosen
            ]

    def send(self):
        if self.level < self.count:
            self.got = [
                swap(self.out[color], "dp", self.orders[color][self.level])
                for color in range(2)
            ]
            return
        for color in range(2):
            bit = self.orders[color][2 * self.count - 1 - self.level]
            self.held[color] += [
                (swap(piece, "dp", bit), mask ^ (1 << bit)) for piece, mask in self.held[color]
            ]

    def arrive(self):
        if self.level < self.count:
            state = []
            for color in range(2):
                keep = self.cut(color, self.side(color))
                total = (keep.astype(F32) + self.got[color].astype(F32)).astype(BF16)
                whole = self.axis == 0 and not self.paired
                state.append(((total,), [sum(self.sizes) if whole else self.sizes[0]], 0))
            self.state = state
        self.level += 1
        self.ready()

    def moving(self):
        return self.out if self.held is None else self.held

    def fresh(self):
        return [held[len(held) // 2][0] for held in self.held]

    def result(self, write, skip=0, into=()):
        pieces, colors, where = [], [], []
        for color in range(2):
            for piece, mask in self.held[color][skip:]:
                owner = self.mine ^ mask
                spot = 0 if self.paired else color
                for bit in self.orders[color]:
                    spot = spot * 2 + ((owner >> bit) & 1)
                pieces.append(piece)
                colors.append(color)
                where.append(spot)
        rows, columns = pieces[0].shape
        length, width = self.grads[0].shape
        if write is write_stacked:
            shapes = [(2, length, width)]
            blocks = [(1, rows, columns)]
        elif write is write_lanes:
            shapes = [(3, length, width // 3)]
            blocks = [(3, rows, columns // 3)]
        else:
            shapes = [g.shape for g in self.grads]
            blocks = [(rows * s[0] // sum(t[0] for t in shapes), columns) for s in shapes]
        lead = {write_stacked: lambda i, c: (c[i],), write_lanes: lambda i, c: (0,)}.get(
            write, lambda i, c: ()
        )

        def out_map(i, c, w):
            return lead(i, c) + ((w[i], 0) if self.axis == 0 else (0, w[i]))

        return place_blocks(
            write,
            jnp.array(colors, jnp.int32),
            jnp.stack(where).astype(jnp.int32),
            pieces,
            shapes,
            [pl.BlockSpec(block, out_map) for block in blocks],
            into,
        )


def fence(values, *sums):
    values, moving = lax.optimization_barrier((values, [item.moving() for item in sums]))
    for item, arrived in zip(sums, moving):
        if item.held is None:
            item.out = arrived
        else:
            item.held = arrived
    return values


def sum_small(values, name, bits=None):
    count = bits_of(name)
    if count is None:
        return lax.psum(values, name) if bits is None or 0 in bits else values
    for bit in range(count) if bits is None else bits:
        values = values + swap(values, name, bit)
    return values


def sum_pairs(values, name):
    count = bits_of(name)
    if count is None:
        return lax.psum(values, name)
    for bit in range(0, count - 1, 2):
        one, two, both = (swap_mask(values, name, mask << bit) for mask in (1, 2, 3))
        values = (values + one) + (two + both)
    return values + swap(values, name, count - 1) if count % 2 else values


def norm_kernel(x_ref, gain_ref, shift_ref, out_ref):
    residual = x_ref[...].astype(F32)
    centered = residual - jnp.mean(residual, -1, keepdims=True)
    inv_std = lax.rsqrt(jnp.mean(centered * centered, -1, keepdims=True) + EPSILON)
    out_ref[...] = (centered * inv_std * gain_ref[...] + shift_ref[...]).astype(BF16)


def norm(layer_in, norm_gain, norm_shift):
    length, width = layer_in.shape
    rows = min(64, length)
    row_spec = pl.BlockSpec((rows, width), lambda i: (i, 0))
    one_spec = pl.BlockSpec((1, width), lambda i: (0, 0))
    return pl.pallas_call(
        norm_kernel,
        grid=(length // rows,),
        in_specs=[row_spec, one_spec, one_spec],
        out_specs=row_spec,
        out_shape=jax.ShapeDtypeStruct((length, width), BF16),
        name="norm",
    )(layer_in, norm_gain.reshape(1, width), norm_shift.reshape(1, width))


def tail_kernel(x_ref, g_ref, c_ref, gain_ref, stat_ref, grad_ref, sums_ref):
    @pl.when(pl.program_id(0) == 0)
    def _():
        sums_ref[...] = jnp.zeros_like(sums_ref)
        sums_ref[2:3, :] = stat_ref[...]

    residual = x_ref[...].astype(F32)
    centered = residual - jnp.mean(residual, -1, keepdims=True)
    inv_std = lax.rsqrt(jnp.mean(centered * centered, -1, keepdims=True) + EPSILON)
    normalized = centered * inv_std
    grads = g_ref[...].astype(F32)
    sums_ref[0:1, :] += jnp.sum(grads * normalized, axis=0, keepdims=True)
    sums_ref[1:2, :] += jnp.sum(grads, axis=0, keepdims=True)
    scaled = grads * gain_ref[...]
    grad_ref[:, 0, :] = (
        inv_std
        * (
            scaled
            - jnp.mean(scaled, -1, keepdims=True)
            - normalized * jnp.mean(scaled * normalized, -1, keepdims=True)
        )
        + c_ref[...].astype(F32)
    )


def tail(layer_in, grad_normed, cot_here, norm_gain, stat_row):
    length, width = layer_in.shape
    rows = min(64, length)
    row_spec = pl.BlockSpec((rows, width), lambda i: (i, 0))
    one_spec = pl.BlockSpec((1, width), lambda i: (0, 0))
    return pl.pallas_call(
        tail_kernel,
        grid=(length // rows,),
        in_specs=[row_spec, row_spec, row_spec, one_spec, one_spec],
        out_specs=[
            pl.BlockSpec((rows, 1, width), lambda i: (i, 0, 0)),
            pl.BlockSpec((4, width), lambda i: (0, 0)),
        ],
        out_shape=[
            jax.ShapeDtypeStruct((length, 1, width), F32),
            jax.ShapeDtypeStruct((4, width), F32),
        ],
        name="tail",
    )(layer_in, grad_normed, cot_here, norm_gain.reshape(1, width), stat_row)


def back_products_kernel(p_ref, q_ref, g_ref, u_ref, w_ref, out_ref):
    turned = (((1,), (1,)), ((), ()))
    columns = q_ref.shape[2]
    total = jnp.dot(g_ref[...], w_ref[0], preferred_element_type=F32)
    total += jnp.dot(u_ref[...], w_ref[1], preferred_element_type=F32)
    for number in range(3):
        total += lax.dot_general(
            p_ref[:, number * columns : (number + 1) * columns],
            q_ref[number],
            turned,
            preferred_element_type=F32,
        )
    out_ref[...] = total.astype(BF16)


def back_products(grad_proj, w_qkv, grad_gate, grad_up, w_gate_up):
    length = grad_proj.shape[0]
    _, width, columns = w_qkv.shape
    hidden = grad_gate.shape[1]
    rows = min(256, length)
    return pl.pallas_call(
        back_products_kernel,
        grid=(length // rows,),
        in_specs=[
            pl.BlockSpec((rows, 3 * columns), lambda i: (i, 0)),
            pl.BlockSpec(w_qkv.shape, lambda i: (0, 0, 0)),
            pl.BlockSpec((rows, hidden), lambda i: (i, 0)),
            pl.BlockSpec((rows, hidden), lambda i: (i, 0)),
            pl.BlockSpec(w_gate_up.shape, lambda i: (0, 0, 0)),
        ],
        out_specs=pl.BlockSpec((rows, width), lambda i: (i, 0)),
        out_shape=jax.ShapeDtypeStruct((length, width), BF16),
        name="back_products",
    )(grad_proj, w_qkv, grad_gate, grad_up, w_gate_up)


def local(
    layer_in,
    segment_ids,
    valid_counts,
    norm_gain,
    norm_shift,
    w_qkv,
    b_qkv,
    w_out,
    w_gate_up,
    w_down,
    out_grad,
):
    local_len, row_count, model_width = layer_in.shape
    assert row_count == 1
    seq_len = local_len * lax.axis_size("mp")
    col_qkv = w_qkv.shape[2]
    ff_local = w_gate_up.shape[2]
    layer_in = layer_in[:, 0]
    position_here = lax.axis_index("mp") * local_len + jnp.arange(local_len, dtype=jnp.int32)
    valid_here = (position_here < valid_counts[0]).astype(F32)

    residual = layer_in.astype(F32)
    normed = norm(layer_in, norm_gain, norm_shift)
    cot_here = jnp.where(valid_here[:, None] > 0, out_grad[:, 0], jnp.zeros((), BF16))
    gathered = lax.all_gather(normed, "mp", axis=0, tiled=True)
    cotangent = lax.all_gather(cot_here, "mp", axis=0, tiled=True)

    w_qkv = jnp.transpose(w_qkv, (1, 0, 2))
    w_gate_up = jnp.transpose(w_gate_up, (1, 2, 0))
    starts = starts_of(segment_ids)[0]
    tables = rotary_lanes(jnp.arange(seq_len, dtype=jnp.int32) - starts)
    start_blocks = starts.reshape(seq_len // BQ, 1, BQ)
    first = start_blocks[:, 0, 0] // BK
    gathered, tables, first, start_blocks = lax.optimization_barrier(
        (gathered, tables, first, start_blocks)
    )

    def product(left, right):
        return jnp.dot(left, right, preferred_element_type=F32).astype(BF16)

    def turned_product(left, right):
        return lax.dot_general(
            left, right, (((1,), (1,)), ((), ())), preferred_element_type=F32
        )

    def token_sum(left, right):
        return lax.dot_general(
            left, right, (((0,), (0,)), ((), ())), preferred_element_type=F32
        ).astype(BF16)

    def scattered(partial):
        return lax.psum_scatter(partial, "mp", scatter_dimension=0, tiled=True)

    gate = turned_product(gathered, w_gate_up[0])
    up = turned_product(gathered, w_gate_up[1])
    sigmoid_gate = jax.nn.sigmoid(gate)
    hidden = (gate * sigmoid_gate * up).astype(BF16)
    mlp_partial = product(hidden, w_down)
    mlp_sum = scattered(mlp_partial)
    gathered_next, mlp_partial = lax.optimization_barrier((gathered, mlp_partial))
    queries, key_rows, value_rows = project(gathered_next, w_qkv, b_qkv, tables)
    attended, lse = attend(first, queries, key_rows, value_rows, start_blocks)
    attn_partial = product(attended, w_out)
    attn_sum = scattered(attn_partial)

    cotangent, attn_partial = lax.optimization_barrier((cotangent, attn_partial))
    sum_down = DpSum(token_sum(hidden, cotangent), token_sum(attended, cotangent))
    cotangent = fence(cotangent, sum_down)
    sum_down.send()
    grad_hid = turned_product(cotangent, w_down).astype(BF16).astype(F32)
    grad_gate = (
        grad_hid * up * sigmoid_gate * (1.0 + gate * (1.0 - sigmoid_gate))
    ).astype(BF16)
    grad_up = (grad_hid * gate * sigmoid_gate).astype(BF16)
    grad_att = turned_product(cotangent, w_out).astype(BF16)
    sum_down.arrive()
    grad_gate, grad_up, grad_att = fence((grad_gate, grad_up, grad_att), sum_down)
    sum_down.send()
    sum_gate = token_sum(grad_gate, gathered)
    sum_down.arrive()
    sum_gate, grad_up = fence((sum_gate, grad_up), sum_down)
    sum_down.send()
    sum_gate_up = DpSum(sum_gate, token_sum(grad_up, gathered), paired=True)
    sum_down.arrive()
    grad_att = fence(grad_att, sum_gate_up, sum_down)
    sum_gate_up.send()
    sum_down.send_half(0)
    grad_proj = attend_back(
        first, queries, key_rows, value_rows, grad_att, attended, lse, start_blocks, tables
    )
    sum_gate_up.arrive()
    grad_proj, mlp_sum = fence((grad_proj, mlp_sum), sum_gate_up, sum_down)
    sum_gate_up.send()
    sum_down.send_half(1)
    sum_down.arrive()
    normed_partial = back_products(grad_proj, w_qkv, grad_gate, grad_up, w_gate_up)
    while sum_down.level < 2 * sum_down.count:
        sum_down.send()
        sum_down.arrive()
    sum_gate_up.arrive()
    grad_proj, normed_partial = fence((grad_proj, normed_partial), sum_gate_up, sum_down)
    grad_normed = scattered(normed_partial)
    sum_gate_up.send()
    sum_qkv = token_sum(gathered, grad_proj)
    sum_gate_up.arrive()
    sum_qkv = DpSum(fence(sum_qkv, sum_gate_up))
    bias_sums = jnp.sum(grad_proj, axis=0, dtype=F32).reshape(-1, 128)
    sum_qkv.send()
    sum_qkv.arrive()
    attn_sum = fence(attn_sum, sum_gate_up, sum_qkv)
    sum_gate_up.send()
    sum_qkv.send()
    mlp_part = mlp_sum.astype(F32)
    attn_part = attn_sum.astype(F32)
    layer_out = (residual + attn_part + mlp_part).astype(BF16)
    statistics = jnp.stack(
        [
            jnp.sum(valid_here * jnp.sum(residual * residual, -1)),
            jnp.sum(valid_here * jnp.sum(attn_part * attn_part, -1)),
            jnp.sum(valid_here * jnp.sum(mlp_part * mlp_part, -1)),
            jnp.sum(valid_here),
        ]
    )
    stat_row = jnp.pad(statistics, (0, model_width - 4)).reshape(1, model_width)
    fresh = sum_gate_up.fresh()
    sum_gate_up.arrive()
    sum_qkv.arrive()
    bias_sums, layer_out, stat_row, _ = fence((bias_sums, layer_out, stat_row, fresh), sum_qkv)
    bias_sums = sum_small(bias_sums, "dp", [0])
    sum_qkv.send()
    down_sums = sum_down.result(write_rows)
    sum_qkv.arrive()
    while sum_gate_up.level < 2 * sum_gate_up.count:
        sum_gate_up.send()
        sum_gate_up.arrive()
    down_sums, bias_sums = fence((down_sums, bias_sums), sum_gate_up, sum_qkv)
    placed = len(sum_qkv.held[0])
    early = sum_qkv.result(write_lanes)
    while sum_qkv.level < 2 * sum_qkv.count:
        sum_qkv.send()
        sum_qkv.arrive()
    (grad_w_gate_up,) = sum_gate_up.result(write_stacked)
    bias_sums = sum_small(bias_sums, "dp", range(1, sum_qkv.count))
    grad_w_gate_up, bias_sums, early = fence((grad_w_gate_up, bias_sums, early), sum_qkv)
    (grad_w_qkv,) = sum_qkv.result(write_lanes, placed, early)
    grad_w_down, grad_w_out = down_sums
    grad_normed, grad_w_gate_up, grad_w_qkv = fence(
        (grad_normed, grad_w_gate_up, grad_w_qkv)
    )
    input_grad, small = tail(layer_in, grad_normed, cot_here, norm_gain, stat_row)
    small = sum_pairs(sum_pairs(small, "mp"), "dp")
    totals = small[2]
    return (
        layer_out[:, None],
        input_grad,
        small[0],
        small[1],
        jnp.transpose(grad_w_qkv, (1, 0, 2)),
        bias_sums.reshape(3, col_qkv),
        grad_w_out,
        jnp.transpose(grad_w_gate_up, (2, 0, 1)),
        grad_w_down,
        jnp.sqrt(totals[:3] / (totals[3] * model_width)),
    )


def solution(mesh):
    placed = (
        P("mp", "dp", None),
        P("dp", None),
        P("dp"),
        P(),
        P(),
        P(None, None, "mp"),
        P(None, "mp"),
        P("mp", None),
        P(None, None, "mp"),
        P("mp", None),
        P("mp", "dp", None),
    )
    return jax.shard_map(
        local,
        mesh=mesh,
        in_specs=placed,
        out_specs=(
            P("mp", "dp", None),
            P("mp", "dp", None),
            P(),
            P(),
            P(None, None, "mp"),
            P(None, "mp"),
            P("mp", None),
            P(None, None, "mp"),
            P("mp", None),
            P(),
        ),
        check_vma=False,
    )
```

```python
import functools

import jax
import jax.numpy as jnp
from jax import lax
from jax.experimental import pallas as pl
from jax.experimental.pallas import tpu as pltpu
from jax.sharding import PartitionSpec as P

HEAD_DIM = 64
ROT = 16
EPSILON = 1e-05
BQ = 128
BK = 256
NEG = -1e30
F32 = jnp.float32
BF16 = jnp.bfloat16


def starts_of(segment_ids):
    length = segment_ids.shape[1]
    steps_all = jnp.arange(length, dtype=jnp.int32)[None, :]
    change = jnp.concatenate(
        [
            jnp.ones_like(segment_ids[:, :1]),
            (segment_ids[:, 1:] != segment_ids[:, :-1]).astype(jnp.int32),
        ],
        axis=1,
    )
    return lax.cummax(jnp.where(change > 0, steps_all, jnp.zeros_like(change)), axis=1)


def rotary_lanes(positions):
    half_rot = ROT // 2
    lane = jnp.arange(2 * HEAD_DIM, dtype=jnp.int32) % HEAD_DIM
    power = (lane % half_rot).astype(F32)
    frequency = jnp.where(lane < ROT, 10000.0 ** (-(power * 2.0) / ROT), 0.0)
    angles = positions.astype(F32)[:, None] * frequency
    sine = jnp.sin(angles)
    low = jnp.where(lane < half_rot, -sine, 0.0)
    high = jnp.where((lane >= half_rot) & (lane < ROT), sine, 0.0)
    return jnp.cos(angles), low, high


def lane_tile(table, columns):
    return jnp.concatenate([table] * (columns // table.shape[1]), axis=1)


def turn(values, cosine, low, high):
    columns = values.shape[1]
    half_rot = ROT // 2
    return (
        values * lane_tile(cosine, columns)
        + pltpu.roll(values, columns - half_rot, 1) * lane_tile(low, columns)
        + pltpu.roll(values, half_rot, 1) * lane_tile(high, columns)
    )


def project_kernel(x_ref, w_ref, b_ref, cos_ref, low_ref, high_ref, q_ref, k_ref, v_ref):
    tables = (cos_ref[...], low_ref[...], high_ref[...])

    def part(number):
        flat = jnp.dot(x_ref[...], w_ref[number], preferred_element_type=F32)
        return flat + b_ref[number : number + 1, :].astype(F32)

    queries = turn(part(0), *tables).astype(BF16)
    q_ref[...] = (queries.astype(F32) * HEAD_DIM**-0.5).astype(BF16)
    k_ref[...] = turn(part(1), *tables).astype(BF16)
    v_ref[...] = part(2).astype(BF16)


def project(gathered, w_qkv, b_qkv, tables):
    length, width = gathered.shape
    columns = w_qkv.shape[2]
    rows = min(256, length)
    table_spec = pl.BlockSpec((rows, tables[0].shape[1]), lambda i: (i, 0))
    out_spec = pl.BlockSpec((rows, columns), lambda i: (i, 0))
    return pl.pallas_call(
        project_kernel,
        grid=(length // rows,),
        in_specs=[
            pl.BlockSpec((rows, width), lambda i: (i, 0)),
            pl.BlockSpec(w_qkv.shape, lambda i: (0, 0, 0)),
            pl.BlockSpec(b_qkv.shape, lambda i: (0, 0)),
            table_spec,
            table_spec,
            table_spec,
        ],
        out_specs=[out_spec] * 3,
        out_shape=[jax.ShapeDtypeStruct((length, columns), BF16)] * 3,
        cost_estimate=pl.CostEstimate(
            flops=6 * length * width * columns,
            bytes_accessed=2 * (length * width + 3 * width * columns + 3 * length * columns),
            transcendentals=0,
        ),
        name="project",
    )(gathered, w_qkv, b_qkv, *tables)


def stack_heads(block):
    columns = block.shape[1]
    head_of = lax.broadcasted_iota(jnp.int32, block.shape, 1) // HEAD_DIM
    return jnp.concatenate(
        [
            jnp.where(head_of == head, block, jnp.zeros_like(block))
            for head in range(columns // HEAD_DIM)
        ],
        axis=0,
    )


def unstack_heads(stacked, block):
    heads = stacked.shape[1] // block
    return jnp.concatenate(
        [
            stacked[head * HEAD_DIM : (head + 1) * HEAD_DIM, head * block : (head + 1) * block]
            for head in range(heads)
        ],
        axis=0,
    ).T


def score_block(key_block, stacked_queries, key_at, start_row, query_row):
    scores = lax.dot_general(
        key_block, stacked_queries, (((1,), (1,)), ((), ())), preferred_element_type=F32
    )
    key_pos = key_at + lax.broadcasted_iota(jnp.int32, scores.shape, 0)
    allowed = (key_pos >= start_row) & (key_pos <= query_row)
    return scores, allowed


def query_rows(start_ref, block, heads):
    start_row = jnp.concatenate([start_ref[0]] * heads, axis=1)
    query_row = pl.program_id(0) * block + lax.broadcasted_iota(jnp.int32, (1, block), 1)
    return start_row, jnp.concatenate([query_row] * heads, axis=1)


def attend_kernel(first_ref, q_ref, k_ref, v_ref, start_ref, o_ref, lse_ref, acc_ref):
    block, columns = q_ref.shape
    heads = columns // HEAD_DIM
    index = pl.program_id(0)
    stacked = stack_heads(q_ref[...])
    start_row, query_row = query_rows(start_ref, block, heads)
    acc_ref[...] = jnp.zeros_like(acc_ref)

    def body(step, carry):
        highest, total = carry
        at = pl.multiple_of(step * BK, BK)
        scores, allowed = score_block(
            k_ref[pl.ds(at, BK), :], stacked, at, start_row, query_row
        )
        scores = jnp.where(allowed, scores, NEG)
        newest = jnp.maximum(highest, jnp.max(scores, axis=0, keepdims=True))
        weights = jnp.exp(scores - newest)
        scale = jnp.exp(highest - newest)
        total = total * scale + jnp.sum(weights, axis=0, keepdims=True)
        acc_ref[...] = acc_ref[...] * scale + lax.dot_general(
            v_ref[pl.ds(at, BK), :],
            weights.astype(BF16),
            (((0,), (0,)), ((), ())),
            preferred_element_type=F32,
        )
        return newest, total

    highest, total = lax.fori_loop(
        first_ref[index],
        (index * block + block - 1) // BK + 1,
        body,
        (jnp.full((1, heads * block), NEG, F32), jnp.zeros((1, heads * block), F32)),
    )
    o_ref[...] = unstack_heads(acc_ref[...] / total, block).astype(BF16)
    lse_ref[0] = highest + jnp.log(total)


def attend(first, queries, key_rows, value_rows, start_blocks):
    length, columns = queries.shape
    blocks = length // BQ
    heads = columns // HEAD_DIM
    row_spec = pl.BlockSpec((BQ, columns), lambda i, f: (i, 0))
    whole = pl.BlockSpec((length, columns), lambda i, f: (0, 0))
    return pl.pallas_call(
        attend_kernel,
        grid_spec=pltpu.PrefetchScalarGridSpec(
            num_scalar_prefetch=1,
            grid=(blocks,),
            in_specs=[
                row_spec,
                whole,
                whole,
                pl.BlockSpec((1, 1, BQ), lambda i, f: (i, 0, 0)),
            ],
            out_specs=[
                row_spec,
                pl.BlockSpec((1, 1, heads * BQ), lambda i, f: (i, 0, 0)),
            ],
            scratch_shapes=[pltpu.VMEM((columns, heads * BQ), F32)],
        ),
        out_shape=[
            jax.ShapeDtypeStruct((length, columns), BF16),
            jax.ShapeDtypeStruct((blocks, 1, heads * BQ), F32),
        ],
        cost_estimate=pl.CostEstimate(
            flops=4 * length * 1024 * columns * heads,
            bytes_accessed=8 * length * columns,
            transcendentals=length * 1024 * heads,
        ),
        name="attend",
    )(first, queries, key_rows, value_rows, start_blocks)


def attend_back_kernel(
    first_ref,
    q_ref,
    k_ref,
    v_ref,
    do_ref,
    o_ref,
    lse_ref,
    start_ref,
    cos_ref,
    low_ref,
    high_ref,
    grad_ref,
    key_acc,
    value_acc,
    query_acc,
):
    block, columns = q_ref.shape
    heads = columns // HEAD_DIM
    length = k_ref.shape[0]
    index = pl.program_id(0)

    @pl.when(index == 0)
    def _():
        key_acc[...] = jnp.zeros_like(key_acc)
        value_acc[...] = jnp.zeros_like(value_acc)

    stacked = stack_heads(q_ref[...])
    stacked_do = stack_heads(do_ref[...])
    start_row, query_row = query_rows(start_ref, block, heads)
    lse_row = lse_ref[0]
    products = do_ref[...].astype(F32) * o_ref[...].astype(F32)
    head_rows = lax.broadcasted_iota(jnp.int32, (8, columns), 0)
    head_lanes = lax.broadcasted_iota(jnp.int32, (8, columns), 1) // HEAD_DIM
    picked = lax.dot_general(
        (head_rows == head_lanes).astype(F32),
        products,
        (((1,), (1,)), ((), ())),
        precision=lax.Precision.HIGHEST,
        preferred_element_type=F32,
    )
    inner_row = jnp.concatenate([picked[head : head + 1, :] for head in range(heads)], axis=1)
    query_acc[...] = jnp.zeros_like(query_acc)

    def body(step, carry):
        at = pl.multiple_of(step * BK, BK)
        key_block = k_ref[pl.ds(at, BK), :]
        scores, allowed = score_block(key_block, stacked, at, start_row, query_row)
        weights = jnp.where(allowed, jnp.exp(scores - lse_row), 0.0)
        grad_weights = lax.dot_general(
            v_ref[pl.ds(at, BK), :],
            stacked_do,
            (((1,), (1,)), ((), ())),
            preferred_element_type=F32,
        )
        grad_scores = (weights * (grad_weights - inner_row)).astype(BF16)
        value_acc[pl.ds(at, BK), :] += jnp.dot(
            weights.astype(BF16), stacked_do, preferred_element_type=F32
        )
        key_acc[pl.ds(at, BK), :] += jnp.dot(grad_scores, stacked, preferred_element_type=F32)
        query_acc[...] += lax.dot_general(
            key_block, grad_scores, (((0,), (0,)), ((), ())), preferred_element_type=F32
        )
        return carry

    lax.fori_loop(first_ref[index], (index * block + block - 1) // BK + 1, body, 0)

    def turn_back(grads, at, rows):
        kept = grads.astype(BF16).astype(F32)
        return turn(
            kept,
            cos_ref[pl.ds(at, rows), :],
            -low_ref[pl.ds(at, rows), :],
            -high_ref[pl.ds(at, rows), :],
        ).astype(BF16)

    at_query = pl.multiple_of(index * block, block)
    grad_ref[pl.ds(at_query, block), :columns] = turn_back(
        unstack_heads(query_acc[...], block) * HEAD_DIM**-0.5, at_query, block
    )

    @pl.when(index == pl.num_programs(0) - 1)
    def _():
        def finish(step, carry):
            at = pl.multiple_of(step * BK, BK)
            grad_ref[pl.ds(at, BK), columns : 2 * columns] = turn_back(
                key_acc[pl.ds(at, BK), :], at, BK
            )
            grad_ref[pl.ds(at, BK), 2 * columns :] = value_acc[pl.ds(at, BK), :].astype(BF16)
            return carry

        lax.fori_loop(0, length // BK, finish, 0)


def attend_back(first, queries, key_rows, value_rows, grad_att, attended, lse, start_blocks, tables):
    length, columns = queries.shape
    blocks = length // BQ
    heads = columns // HEAD_DIM
    row_spec = pl.BlockSpec((BQ, columns), lambda i, f: (i, 0))
    whole = pl.BlockSpec((length, columns), lambda i, f: (0, 0))
    table_spec = pl.BlockSpec(tables[0].shape, lambda i, f: (0, 0))
    return pl.pallas_call(
        attend_back_kernel,
        grid_spec=pltpu.PrefetchScalarGridSpec(
            num_scalar_prefetch=1,
            grid=(blocks,),
            in_specs=[
                row_spec,
                whole,
                whole,
                row_spec,
                row_spec,
                pl.BlockSpec((1, 1, heads * BQ), lambda i, f: (i, 0, 0)),
                pl.BlockSpec((1, 1, BQ), lambda i, f: (i, 0, 0)),
                table_spec,
                table_spec,
                table_spec,
            ],
            out_specs=pl.BlockSpec((length, 3 * columns), lambda i, f: (0, 0)),
            scratch_shapes=[
                pltpu.VMEM((length, columns), F32),
                pltpu.VMEM((length, columns), F32),
                pltpu.VMEM((columns, heads * BQ), F32),
            ],
        ),
        out_shape=jax.ShapeDtypeStruct((length, 3 * columns), BF16),
        cost_estimate=pl.CostEstimate(
            flops=10 * length * 1024 * columns * heads,
            bytes_accessed=16 * length * columns,
            transcendentals=length * 1024 * heads,
        ),
        name="attend_back",
    )(first, queries, key_rows, value_rows, grad_att, attended, lse, start_blocks, *tables)


def bits_of(name):
    size = lax.axis_size(name)
    count = size.bit_length() - 1
    return count if size == 1 << count else None


def swap(values, name, bit):
    return swap_mask(values, name, 1 << bit)


def swap_mask(values, name, mask):
    size = lax.axis_size(name)
    return lax.ppermute(values, name, [(i, i ^ mask) for i in range(size)])


def write_stacked(piece, outs):
    outs[0][0] = piece.astype(F32)


def write_rows(piece, outs):
    at = 0
    for out_ref in outs:
        size = out_ref.shape[0]
        out_ref[...] = piece[at : at + size, :].astype(F32)
        at += size


def write_lanes(piece, outs):
    parts, _, size = outs[0].shape
    for part in range(parts):
        outs[0][part] = piece[:, part * size : (part + 1) * size].astype(F32)


def place_kernel(write, count, color_ref, where_ref, *refs):
    step = pl.program_id(0)
    for number in range(count):

        @pl.when(step == number)
        def _(number=number):
            write(refs[number][...], refs[count:])


def place_blocks(write, color, where, pieces, out_shapes, out_specs):
    rows, columns = pieces[0].shape
    count = len(pieces)
    return pl.pallas_call(
        functools.partial(place_kernel, write, count),
        grid_spec=pltpu.PrefetchScalarGridSpec(
            num_scalar_prefetch=2,
            grid=(count,),
            in_specs=[pl.BlockSpec((rows, columns), lambda i, c, w: (0, 0))] * count,
            out_specs=out_specs,
        ),
        out_shape=[jax.ShapeDtypeStruct(shape, F32) for shape in out_shapes],
        cost_estimate=pl.CostEstimate(
            flops=0, bytes_accessed=6 * count * rows * columns, transcendentals=0
        ),
        name="place_blocks",
    )(color, where, *pieces)


class DpSum:
    def __init__(self, *grads, paired=False):
        self.grads = grads
        self.paired = paired
        self.count = bits_of("dp")
        pieces = (1 if paired else 2) << self.count
        self.axis = 0 if all(g.shape[0] % (8 * pieces) == 0 for g in grads) else 1
        self.sizes = [g.shape[self.axis] // pieces for g in grads]
        self.mine = lax.axis_index("dp")
        self.orders = [list(range(self.count)), list(range(self.count))[::-1]]
        self.level = 0
        if paired:
            self.state = [((grad,), self.sizes[:1], 0) for grad in grads]
        else:
            self.state = [(grads, self.sizes, color << self.count) for color in range(2)]
        self.held = None
        self.ready()

    def cut(self, color, side):
        grads, units, base = self.state[color]
        span = (1 << self.count) >> (self.level + 1)
        parts = []
        for grad, unit in zip(grads, units):
            at = (base + side * span) * unit
            parts.append(lax.dynamic_slice_in_dim(grad, at, span * unit, self.axis))
        if len(parts) == 1:
            return parts[0]
        if self.axis:
            return jnp.concatenate(parts, axis=0)
        parts = [p.reshape(span, unit, p.shape[1]) for p, unit in zip(parts, units)]
        joined = jnp.concatenate(parts, axis=1)
        return joined.reshape(-1, joined.shape[2])

    def side(self, color):
        return (self.mine >> self.orders[color][self.level]) & 1

    def ready(self):
        if self.level < self.count:
            self.out = [self.cut(color, 1 - self.side(color)) for color in range(2)]
        elif self.held is None:
            self.held = [[(self.state[color][0][0], 0)] for color in range(2)]

    def send_half(self, half):
        for color in range(2):
            bit = self.orders[color][2 * self.count - 1 - self.level]
            blocks = 1 << (self.level - self.count)
            middle = max(blocks // 2, 1)
            chosen = self.held[color][:middle] if half == 0 else self.held[color][middle:blocks]
            self.held[color] += [
                (swap(piece, "dp", bit), mask ^ (1 << bit)) for piece, mask in chosen
            ]

    def send(self):
        if self.level < self.count:
            self.got = [
                swap(self.out[color], "dp", self.orders[color][self.level])
                for color in range(2)
            ]
            return
        for color in range(2):
            bit = self.orders[color][2 * self.count - 1 - self.level]
            self.held[color] += [
                (swap(piece, "dp", bit), mask ^ (1 << bit)) for piece, mask in self.held[color]
            ]

    def arrive(self):
        if self.level < self.count:
            state = []
            for color in range(2):
                keep = self.cut(color, self.side(color))
                total = (keep.astype(F32) + self.got[color].astype(F32)).astype(BF16)
                whole = self.axis == 0 and not self.paired
                state.append(((total,), [sum(self.sizes) if whole else self.sizes[0]], 0))
            self.state = state
        self.level += 1
        self.ready()

    def moving(self):
        return self.out if self.held is None else self.held

    def fresh(self):
        return [held[len(held) // 2][0] for held in self.held]

    def result(self, write):
        pieces, colors, where = [], [], []
        for color in range(2):
            for piece, mask in self.held[color]:
                owner = self.mine ^ mask
                spot = 0 if self.paired else color
                for bit in self.orders[color]:
                    spot = spot * 2 + ((owner >> bit) & 1)
                pieces.append(piece)
                colors.append(color)
                where.append(spot)
        rows, columns = pieces[0].shape
        length, width = self.grads[0].shape
        if write is write_stacked:
            shapes = [(2, length, width)]
            blocks = [(1, rows, columns)]
        elif write is write_lanes:
            shapes = [(3, length, width // 3)]
            blocks = [(3, rows, columns // 3)]
        else:
            shapes = [g.shape for g in self.grads]
            blocks = [(rows * s[0] // sum(t[0] for t in shapes), columns) for s in shapes]
        lead = {write_stacked: lambda i, c: (c[i],), write_lanes: lambda i, c: (0,)}.get(
            write, lambda i, c: ()
        )

        def out_map(i, c, w):
            return lead(i, c) + ((w[i], 0) if self.axis == 0 else (0, w[i]))

        return place_blocks(
            write,
            jnp.array(colors, jnp.int32),
            jnp.stack(where).astype(jnp.int32),
            pieces,
            shapes,
            [pl.BlockSpec(block, out_map) for block in blocks],
        )


def fence(values, *sums):
    values, moving = lax.optimization_barrier((values, [item.moving() for item in sums]))
    for item, arrived in zip(sums, moving):
        if item.held is None:
            item.out = arrived
        else:
            item.held = arrived
    return values


def sum_small(values, name, bits=None):
    count = bits_of(name)
    if count is None:
        return lax.psum(values, name) if bits is None or 0 in bits else values
    for bit in range(count) if bits is None else bits:
        values = values + swap(values, name, bit)
    return values


def sum_pairs(values, name):
    count = bits_of(name)
    if count is None:
        return lax.psum(values, name)
    for bit in range(0, count - 1, 2):
        one, two, both = (swap_mask(values, name, mask << bit) for mask in (1, 2, 3))
        values = (values + one) + (two + both)
    return values + swap(values, name, count - 1) if count % 2 else values


def norm_kernel(x_ref, gain_ref, shift_ref, out_ref):
    residual = x_ref[...].astype(F32)
    centered = residual - jnp.mean(residual, -1, keepdims=True)
    inv_std = lax.rsqrt(jnp.mean(centered * centered, -1, keepdims=True) + EPSILON)
    out_ref[...] = (centered * inv_std * gain_ref[...] + shift_ref[...]).astype(BF16)


def norm(layer_in, norm_gain, norm_shift):
    length, width = layer_in.shape
    rows = min(64, length)
    row_spec = pl.BlockSpec((rows, width), lambda i: (i, 0))
    one_spec = pl.BlockSpec((1, width), lambda i: (0, 0))
    return pl.pallas_call(
        norm_kernel,
        grid=(length // rows,),
        in_specs=[row_spec, one_spec, one_spec],
        out_specs=row_spec,
        out_shape=jax.ShapeDtypeStruct((length, width), BF16),
        name="norm",
    )(layer_in, norm_gain.reshape(1, width), norm_shift.reshape(1, width))


def tail_kernel(x_ref, g_ref, c_ref, gain_ref, stat_ref, grad_ref, sums_ref):
    @pl.when(pl.program_id(0) == 0)
    def _():
        sums_ref[...] = jnp.zeros_like(sums_ref)
        sums_ref[2:3, :] = stat_ref[...]

    residual = x_ref[...].astype(F32)
    centered = residual - jnp.mean(residual, -1, keepdims=True)
    inv_std = lax.rsqrt(jnp.mean(centered * centered, -1, keepdims=True) + EPSILON)
    normalized = centered * inv_std
    grads = g_ref[...].astype(F32)
    sums_ref[0:1, :] += jnp.sum(grads * normalized, axis=0, keepdims=True)
    sums_ref[1:2, :] += jnp.sum(grads, axis=0, keepdims=True)
    scaled = grads * gain_ref[...]
    grad_ref[:, 0, :] = (
        inv_std
        * (
            scaled
            - jnp.mean(scaled, -1, keepdims=True)
            - normalized * jnp.mean(scaled * normalized, -1, keepdims=True)
        )
        + c_ref[...].astype(F32)
    )


def tail(layer_in, grad_normed, cot_here, norm_gain, stat_row):
    length, width = layer_in.shape
    rows = min(64, length)
    row_spec = pl.BlockSpec((rows, width), lambda i: (i, 0))
    one_spec = pl.BlockSpec((1, width), lambda i: (0, 0))
    return pl.pallas_call(
        tail_kernel,
        grid=(length // rows,),
        in_specs=[row_spec, row_spec, row_spec, one_spec, one_spec],
        out_specs=[
            pl.BlockSpec((rows, 1, width), lambda i: (i, 0, 0)),
            pl.BlockSpec((4, width), lambda i: (0, 0)),
        ],
        out_shape=[
            jax.ShapeDtypeStruct((length, 1, width), F32),
            jax.ShapeDtypeStruct((4, width), F32),
        ],
        name="tail",
    )(layer_in, grad_normed, cot_here, norm_gain.reshape(1, width), stat_row)


def back_products_kernel(p_ref, q_ref, g_ref, u_ref, w_ref, out_ref):
    turned = (((1,), (1,)), ((), ()))
    columns = q_ref.shape[2]
    total = jnp.dot(g_ref[...], w_ref[0], preferred_element_type=F32)
    total += jnp.dot(u_ref[...], w_ref[1], preferred_element_type=F32)
    for number in range(3):
        total += lax.dot_general(
            p_ref[:, number * columns : (number + 1) * columns],
            q_ref[number],
            turned,
            preferred_element_type=F32,
        )
    out_ref[...] = total.astype(BF16)


def back_products(grad_proj, w_qkv, grad_gate, grad_up, w_gate_up):
    length = grad_proj.shape[0]
    _, width, columns = w_qkv.shape
    hidden = grad_gate.shape[1]
    rows = min(256, length)
    return pl.pallas_call(
        back_products_kernel,
        grid=(length // rows,),
        in_specs=[
            pl.BlockSpec((rows, 3 * columns), lambda i: (i, 0)),
            pl.BlockSpec(w_qkv.shape, lambda i: (0, 0, 0)),
            pl.BlockSpec((rows, hidden), lambda i: (i, 0)),
            pl.BlockSpec((rows, hidden), lambda i: (i, 0)),
            pl.BlockSpec(w_gate_up.shape, lambda i: (0, 0, 0)),
        ],
        out_specs=pl.BlockSpec((rows, width), lambda i: (i, 0)),
        out_shape=jax.ShapeDtypeStruct((length, width), BF16),
        name="back_products",
    )(grad_proj, w_qkv, grad_gate, grad_up, w_gate_up)


def local(
    layer_in,
    segment_ids,
    valid_counts,
    norm_gain,
    norm_shift,
    w_qkv,
    b_qkv,
    w_out,
    w_gate_up,
    w_down,
    out_grad,
):
    local_len, row_count, model_width = layer_in.shape
    assert row_count == 1
    seq_len = local_len * lax.axis_size("mp")
    col_qkv = w_qkv.shape[2]
    ff_local = w_gate_up.shape[2]
    layer_in = layer_in[:, 0]
    position_here = lax.axis_index("mp") * local_len + jnp.arange(local_len, dtype=jnp.int32)
    valid_here = (position_here < valid_counts[0]).astype(F32)

    residual = layer_in.astype(F32)
    normed = norm(layer_in, norm_gain, norm_shift)
    cot_here = jnp.where(valid_here[:, None] > 0, out_grad[:, 0], jnp.zeros((), BF16))
    gathered = lax.all_gather(normed, "mp", axis=0, tiled=True)
    cotangent = lax.all_gather(cot_here, "mp", axis=0, tiled=True)

    w_qkv = jnp.transpose(w_qkv, (1, 0, 2))
    w_gate_up = jnp.transpose(w_gate_up, (1, 2, 0))
    starts = starts_of(segment_ids)[0]
    tables = rotary_lanes(jnp.arange(seq_len, dtype=jnp.int32) - starts)
    start_blocks = starts.reshape(seq_len // BQ, 1, BQ)
    first = start_blocks[:, 0, 0] // BK
    gathered, tables, first, start_blocks = lax.optimization_barrier(
        (gathered, tables, first, start_blocks)
    )

    def product(left, right):
        return jnp.dot(left, right, preferred_element_type=F32).astype(BF16)

    def turned_product(left, right):
        return lax.dot_general(
            left, right, (((1,), (1,)), ((), ())), preferred_element_type=F32
        )

    def token_sum(left, right):
        return lax.dot_general(
            left, right, (((0,), (0,)), ((), ())), preferred_element_type=F32
        ).astype(BF16)

    def scattered(partial):
        return lax.psum_scatter(partial, "mp", scatter_dimension=0, tiled=True)

    gate = turned_product(gathered, w_gate_up[0])
    up = turned_product(gathered, w_gate_up[1])
    sigmoid_gate = jax.nn.sigmoid(gate)
    hidden = (gate * sigmoid_gate * up).astype(BF16)
    mlp_partial = product(hidden, w_down)
    mlp_sum = scattered(mlp_partial)
    gathered_next, mlp_partial = lax.optimization_barrier((gathered, mlp_partial))
    queries, key_rows, value_rows = project(gathered_next, w_qkv, b_qkv, tables)
    attended, lse = attend(first, queries, key_rows, value_rows, start_blocks)
    attn_partial = product(attended, w_out)
    attn_sum = scattered(attn_partial)

    cotangent, attn_partial = lax.optimization_barrier((cotangent, attn_partial))
    sum_down = DpSum(token_sum(hidden, cotangent), token_sum(attended, cotangent))
    cotangent = fence(cotangent, sum_down)
    sum_down.send()
    grad_hid = turned_product(cotangent, w_down).astype(BF16).astype(F32)
    grad_gate = (
        grad_hid * up * sigmoid_gate * (1.0 + gate * (1.0 - sigmoid_gate))
    ).astype(BF16)
    grad_up = (grad_hid * gate * sigmoid_gate).astype(BF16)
    grad_att = turned_product(cotangent, w_out).astype(BF16)
    sum_down.arrive()
    grad_gate, grad_up, grad_att = fence((grad_gate, grad_up, grad_att), sum_down)
    sum_down.send()
    sum_gate = token_sum(grad_gate, gathered)
    sum_down.arrive()
    sum_gate, grad_up = fence((sum_gate, grad_up), sum_down)
    sum_down.send()
    sum_gate_up = DpSum(sum_gate, token_sum(grad_up, gathered), paired=True)
    sum_down.arrive()
    grad_att = fence(grad_att, sum_gate_up, sum_down)
    sum_gate_up.send()
    sum_down.send_half(0)
    grad_proj = attend_back(
        first, queries, key_rows, value_rows, grad_att, attended, lse, start_blocks, tables
    )
    sum_gate_up.arrive()
    grad_proj, mlp_sum = fence((grad_proj, mlp_sum), sum_gate_up, sum_down)
    sum_gate_up.send()
    sum_down.send_half(1)
    sum_down.arrive()
    normed_partial = back_products(grad_proj, w_qkv, grad_gate, grad_up, w_gate_up)
    while sum_down.level < 2 * sum_down.count:
        sum_down.send()
        sum_down.arrive()
    sum_gate_up.arrive()
    grad_proj, normed_partial = fence((grad_proj, normed_partial), sum_gate_up, sum_down)
    grad_normed = scattered(normed_partial)
    sum_gate_up.send()
    sum_qkv = token_sum(gathered, grad_proj)
    sum_gate_up.arrive()
    sum_qkv = DpSum(fence(sum_qkv, sum_gate_up))
    bias_sums = jnp.sum(grad_proj, axis=0, dtype=F32).reshape(-1, 128)
    sum_qkv.send()
    sum_qkv.arrive()
    attn_sum = fence(attn_sum, sum_gate_up, sum_qkv)
    sum_gate_up.send()
    sum_qkv.send()
    mlp_part = mlp_sum.astype(F32)
    attn_part = attn_sum.astype(F32)
    layer_out = (residual + attn_part + mlp_part).astype(BF16)
    statistics = jnp.stack(
        [
            jnp.sum(valid_here * jnp.sum(residual * residual, -1)),
            jnp.sum(valid_here * jnp.sum(attn_part * attn_part, -1)),
            jnp.sum(valid_here * jnp.sum(mlp_part * mlp_part, -1)),
            jnp.sum(valid_here),
        ]
    )
    stat_row = jnp.pad(statistics, (0, model_width - 4)).reshape(1, model_width)
    fresh = sum_gate_up.fresh()
    sum_gate_up.arrive()
    sum_qkv.arrive()
    bias_sums, layer_out, stat_row, _ = fence((bias_sums, layer_out, stat_row, fresh), sum_qkv)
    bias_sums = sum_small(bias_sums, "dp", [0])
    sum_qkv.send()
    down_sums = sum_down.result(write_rows)
    sum_qkv.arrive()
    while sum_gate_up.level < 2 * sum_gate_up.count:
        sum_gate_up.send()
        sum_gate_up.arrive()
    down_sums, bias_sums = fence((down_sums, bias_sums), sum_gate_up, sum_qkv)
    while sum_qkv.level < 2 * sum_qkv.count:
        sum_qkv.send()
        sum_qkv.arrive()
    (grad_w_gate_up,) = sum_gate_up.result(write_stacked)
    bias_sums = sum_small(bias_sums, "dp", range(1, sum_qkv.count))
    grad_w_gate_up, bias_sums = fence((grad_w_gate_up, bias_sums), sum_qkv)
    (grad_w_qkv,) = sum_qkv.result(write_lanes)
    grad_w_down, grad_w_out = down_sums
    grad_normed, grad_w_gate_up, grad_w_qkv = fence(
        (grad_normed, grad_w_gate_up, grad_w_qkv)
    )
    input_grad, small = tail(layer_in, grad_normed, cot_here, norm_gain, stat_row)
    small = sum_pairs(sum_pairs(small, "mp"), "dp")
    totals = small[2]
    return (
        layer_out[:, None],
        input_grad,
        small[0],
        small[1],
        jnp.transpose(grad_w_qkv, (1, 0, 2)),
        bias_sums.reshape(3, col_qkv),
        grad_w_out,
        jnp.transpose(grad_w_gate_up, (2, 0, 1)),
        grad_w_down,
        jnp.sqrt(totals[:3] / (totals[3] * model_width)),
    )


def solution(mesh):
    placed = (
        P("mp", "dp", None),
        P("dp", None),
        P("dp"),
        P(),
        P(),
        P(None, None, "mp"),
        P(None, "mp"),
        P("mp", None),
        P(None, None, "mp"),
        P("mp", None),
        P("mp", "dp", None),
    )
    return jax.shard_map(
        local,
        mesh=mesh,
        in_specs=placed,
        out_specs=(
            P("mp", "dp", None),
            P("mp", "dp", None),
            P(),
            P(),
            P(None, None, "mp"),
            P(None, "mp"),
            P("mp", None),
            P(None, None, "mp"),
            P("mp", None),
            P(),
        ),
        check_vma=False,
    )
```
